512 devices in a mesh: ens: 16 (over y, x_hi), grid: 32 (over x_lo, z, core).
Axes of the slice: x: 4 (x_hi: 2, x_lo: 2; x = x_hi * 2 + x_lo), y: 8, z: 8, core: 2. Of those that a mesh axis runs over, the one named last changes fastest.
Arguments:
- latent: bfloat16 [16, 1024, 8192], P('ens', None, 'grid'), may hold values from -24 to 24
- w_in: bfloat16 [1024, 1024], replicated, may hold values from -0.1875 to 0.1875
- w_out: bfloat16 [99, 1024], replicated, may hold values from -0.1875 to 0.1875
- target: float32 [99, 8192], P(None, 'grid'), may hold values from -6 to 6
- area: float32 [8192], P('grid'), may hold values from 0.05 to 3, as said below
- var_weight: float32 [99], replicated, may hold values from 0.2 to 2
Outputs:
- loss: float32 [], replicated
- grad_latent: bfloat16 [16, 1024, 8192], P('ens', None, 'grid')
- grad_in: float32 [1024, 1024], P('ens', 'grid')
- grad_out: float32 [99, 1024], P(None, 'grid')
The draws below stay inside these ranges and needn't reach their ends.
Inputs may be any that keep to these rules, and one draw needn't show every extreme that they name: Every area weight is positive.
All inputs are finite; a program needn't handle non-finite values.
Results may differ from the reference program's by a relative error of at most 0.013.
Values may be sent and summed in bfloat16 or wider, within the bound.
No kernel may reach another device: no remote copies, remote signals or barrier semaphores. Data moves between devices by JAX's collectives and lax.ppermute only.
A program may use at most 64 MiB of HBM per device.

```python
import math
import jax
import jax.numpy as jnp
from jax import lax

LAT = 1024
HID = 1024
VARS = 99
PTS_DEV = 256
MEMBERS = 16
POINTS = 8192
N_GRID = 32


def draw_area(key, part):
    position = jnp.arange(POINTS, dtype=jnp.float32)
    latitude = 1.25 * (1.0 - position / POINTS)
    base = jnp.cos(latitude)
    jitter = jax.random.uniform(key, (POINTS,), jnp.float32, 0.5, 1.5)
    return (base * jitter).astype(jnp.float32)


def draw_latent(key, part):
    value_key = jax.random.fold_in(key, 11)
    pair_key = jax.random.fold_in(key, 23)
    blocks = POINTS // PTS_DEV
    lat_block = LAT // blocks
    pairing = jax.random.permutation(pair_key, blocks)
    point_block = jnp.arange(POINTS, dtype=jnp.int32) // PTS_DEV
    channel_block = jnp.arange(LAT, dtype=jnp.int32) // lat_block
    chosen = pairing[point_block]
    boost = jnp.where(channel_block[:, None] == chosen[None, :], 3.0, 1.0).astype(jnp.float32)
    share = jnp.arange(MEMBERS, dtype=jnp.float32) / float(MEMBERS - 1)
    noise = jax.random.truncated_normal(value_key, -4.0, 4.0, (MEMBERS, LAT, POINTS), jnp.float32)
    member_scale = 0.5 * jnp.exp(share * 1.3862944)
    return (noise * member_scale[:, None, None] * boost[None]).astype(jnp.bfloat16)


def block_levels(stream_key, shape, shards, least, largest):
    loudness = 1.0
    for dim, parts in shards:
        draws = jax.random.uniform(jax.random.fold_in(jax.random.fold_in(stream_key, 6), dim), (parts,), jnp.float32, least / len(shards), largest / len(shards))
        loudness = loudness * jnp.repeat(jnp.exp(draws), shape[dim] // parts).reshape((-1,) + (1,) * (len(shape) - 1 - dim))
    return loudness


def centred(key, shape, scale, bound, shards=(), kind=jnp.bfloat16):
    level = block_levels(key, shape, shards, -0.22, 0.18) if shards else 1.0
    drawn = jax.random.normal(key, shape, jnp.float32) * scale * level
    return jnp.minimum(jnp.maximum(drawn, -bound), bound).astype(kind)


def setup_inputs(seed: int = 0) -> dict:
    splits = jax.random.split(jax.random.key(seed), 7)
    latent = draw_latent(jax.random.fold_in(splits[6], 71), 0)
    w_in = centred(splits[1], (HID, LAT), LAT ** -0.5, 0.1875)
    w_out = centred(splits[2], (VARS, HID), HID ** -0.5, 0.1875)
    target = centred(splits[3], (VARS, POINTS), 1.0, 6.0, ((1, 32),), jnp.float32)
    area = draw_area(jax.random.fold_in(splits[6], 71), 0)
    var_weight = jnp.clip(jnp.exp(jax.random.uniform(splits[5], (VARS,), jnp.float32, math.log(0.2), math.log(2.0))), 0.2, 2.0)
    return {"latent": latent, "w_in": w_in, "w_out": w_out, "target": target, "area": area, "var_weight": var_weight}


smooth_sq = 0.01
gelu_c = 0.7978845608
gelu_k = 0.044715

def gelu_value(value):
    inner = jnp.tanh(gelu_c * (value + gelu_k * value * value * value))
    return 0.5 * value * (1.0 + inner)

def gelu_slope(value):
    inner = jnp.tanh(gelu_c * (value + gelu_k * value * value * value))
    return 0.5 * (1.0 + inner) + 0.5 * value * (1.0 - inner * inner) * gelu_c * (1.0 + 3.0 * gelu_k * value * value)

def distance(value):
    return jnp.sqrt(value * value + smooth_sq)

def distance_slope(value):
    return value / jnp.sqrt(value * value + smooth_sq)

def reference(latent, w_in, w_out, target, area, var_weight):
    count = float(MEMBERS)

    def forward(features):
        preact = jnp.dot(w_in, features, preferred_element_type=jnp.float32)
        hidden = gelu_value(preact).astype(jnp.bfloat16)
        decoded = jnp.dot(w_out, hidden, preferred_element_type=jnp.float32)
        return (preact, hidden, decoded)
    decoded_all = lax.map(lambda features: forward(features)[2], latent)

    def pairs(own):
        spread = own[None] - decoded_all
        return (lax.optimization_barrier(jnp.sum(distance(spread), 0)), lax.optimization_barrier(jnp.sum(distance_slope(spread), 0)))
    pair_sum, pair_slope = lax.map(pairs, decoded_all)
    weight_total = jnp.sum(area)
    weight = area[None, :] * var_weight[:, None]
    skill = distance(decoded_all - target[None])
    local = skill / count - pair_sum / (2.0 * count * (count - 1.0))
    loss = jnp.sum(weight[None] * local) / (weight_total * VARS)
    factor = POINTS / (weight_total * VARS)

    def member_step(carry, inputs):
        features, decoded, slope_pairs = inputs
        preact, hidden, unused = forward(features)
        dout = (factor * weight * (distance_slope(decoded - target) / count - slope_pairs / (count * (count - 1.0)))).astype(jnp.bfloat16)
        dhidden = lax.dot_general(w_out, dout, (((0,), (0,)), ((), ())), preferred_element_type=jnp.float32)
        dpre = (dhidden * gelu_slope(preact)).astype(jnp.bfloat16)
        grad_lat = lax.dot_general(w_in, dpre, (((0,), (0,)), ((), ())), preferred_element_type=jnp.float32).astype(jnp.bfloat16)
        dpre_blocks = dpre.reshape(HID, N_GRID, PTS_DEV).astype(jnp.float32)
        feat_blocks = features.reshape(LAT, N_GRID, PTS_DEV).astype(jnp.float32)
        term_in = jnp.einsum('hcp,lcp->chl', dpre_blocks, feat_blocks).astype(jnp.bfloat16).astype(jnp.float32)
        dout_blocks = dout.reshape(VARS, N_GRID, PTS_DEV).astype(jnp.float32)
        hid_blocks = hidden.reshape(HID, N_GRID, PTS_DEV).astype(jnp.float32)
        term_out = jnp.einsum('vcp,hcp->cvh', dout_blocks, hid_blocks).astype(jnp.bfloat16).astype(jnp.float32)
        total_in, total_out = carry
        return ((total_in + lax.optimization_barrier(jnp.sum(term_in, 0)), total_out + lax.optimization_barrier(jnp.sum(term_out, 0))), grad_lat)
    start = (jnp.zeros((HID, LAT), jnp.float32), jnp.zeros((VARS, HID), jnp.float32))
    (total_in, total_out), grad_latent = lax.scan(member_step, start, (latent, decoded_all, pair_slope))
    ratio = 1.0 / jnp.sqrt(jnp.float32(POINTS) * jnp.float32(MEMBERS))
    return (loss, grad_latent, ratio * total_in, ratio * total_out)
```

```python
import jax
import jax.numpy as jnp
from jax import lax
from jax.sharding import Mesh, PartitionSpec as P

VARS = 99
PAD = 128
ENS = ("y", "xh")
PLANE = ("xl", "z")

smooth_sq = 0.01
gelu_c = 0.7978845608
gelu_k = 0.044715
f32 = jnp.float32
bf16 = jnp.bfloat16


def gelu_value(value):
    inner = jnp.tanh(gelu_c * (value + gelu_k * value * value * value))
    return 0.5 * value * (1.0 + inner)


def gelu_slope(value):
    inner = jnp.tanh(gelu_c * (value + gelu_k * value * value * value))
    return 0.5 * (1.0 + inner) + 0.5 * value * (1.0 - inner * inner) * gelu_c * (
        1.0 + 3.0 * gelu_k * value * value
    )


def distance(value):
    return jnp.sqrt(value * value + smooth_sq)


def distance_slope(value):
    return value / jnp.sqrt(value * value + smooth_sq)


def exchange(pieces, axes):
    return lax.all_to_all(pieces, axes, split_axis=0, concat_axis=0, tiled=True)


def halves(value):
    high = lax.reduce_precision(value, 8, 7)
    return high, value - high


def with_scalars(rows, loss, area):
    row = lax.broadcasted_iota(jnp.int32, rows.shape, rows.ndim - 2)
    col = lax.broadcasted_iota(jnp.int32, rows.shape, rows.ndim - 1)
    for k, part in enumerate(halves(loss) + halves(area)):
        rows = jnp.where((row == 0) & (col == VARS + 1 + k), part, rows)
    return rows


def scalars(rows):
    at = VARS + 1
    return rows[0, at] + rows[0, at + 1], rows[0, at + 2] + rows[0, at + 3]


def per_device(latent, w_in, w_out, target, area, var_weight):
    n_ens = lax.axis_size(ENS)
    n_plane = lax.axis_size(PLANE)
    n_core = lax.axis_size("c")
    count = float(n_ens)
    pts = area.shape[0]
    points_all = n_plane * n_core * pts
    hid, lat = w_in.shape
    vars_own = PAD // n_ens
    cols = lat // (n_plane * n_core)
    me = lax.axis_index(ENS)
    core = lax.axis_index("c")
    features = latent[0]
    w_out_pad = jnp.pad(w_out, ((0, PAD - VARS), (0, 0)))

    preact = jnp.dot(w_in, features, preferred_element_type=f32)
    hidden = gelu_value(preact).astype(bf16)
    decoded = jnp.dot(w_out_pad, hidden, preferred_element_type=f32)

    fields = exchange(decoded.reshape(n_ens, vars_own, pts), ENS)
    target_own = lax.dynamic_slice_in_dim(
        jnp.pad(target, ((0, PAD - VARS), (0, 0))), me * vars_own, vars_own
    )
    weight_own = lax.dynamic_slice_in_dim(
        jnp.pad(var_weight, (0, PAD - VARS)), me * vars_own, vars_own
    )
    spread = fields[:, None] - fields[None]
    pair_sum = jnp.sum(distance(spread), 1)
    pair_slope = jnp.sum(distance_slope(spread), 1)
    weight = area[None, :] * weight_own[:, None]
    miss = fields - target_own[None]
    local = distance(miss) / count - pair_sum / (2.0 * count * (count - 1.0))
    loss = jnp.sum(weight[None] * local)
    dout_own = (
        weight[None]
        * (distance_slope(miss) / count - pair_slope / (count * (count - 1.0)))
    ).astype(bf16)
    dout = exchange(dout_own, ENS).reshape(PAD, pts)

    dhidden = lax.dot_general(
        w_out_pad, dout, (((0,), (0,)), ((), ())), preferred_element_type=f32
    )
    dpre = (dhidden * gelu_slope(preact)).astype(bf16)
    grad_lat = lax.dot_general(
        w_in, dpre, (((0,), (0,)), ((), ())), preferred_element_type=f32
    )
    grad_lat = lax.optimization_barrier(grad_lat)

    def rows_of(value, which):
        split = value.reshape(n_plane, n_core, cols, pts)
        return lax.dynamic_index_in_dim(split, which, 1, keepdims=False).reshape(-1, pts)

    def terms(which):
        contract = (((1,), (1,)), ((), ()))
        part_in = lax.dot_general(
            rows_of(features, which), dpre, contract, preferred_element_type=f32
        )
        part_out = lax.dot_general(
            rows_of(hidden, which), dout, contract, preferred_element_type=f32
        )
        return part_in, part_out.reshape(n_plane, cols, PAD)

    def packed(part_in, part_out):
        return jnp.concatenate(
            [part_in.astype(bf16), part_out.reshape(-1, PAD).astype(bf16)], 1
        )

    area_sum = jnp.sum(area)
    part_in, part_out = terms(1 - core)
    away = packed(part_in, with_scalars(part_out, loss, area_sum))
    came = lax.ppermute(away, "c", [(0, 1), (1, 0)]).astype(f32)
    part_in, part_out = terms(core)
    came_out = came[:, hid:].reshape(n_plane, cols, PAD)
    came_loss, came_area = scalars(came_out[0])
    sums = packed(
        part_in + came[:, :hid],
        with_scalars(part_out + came_out, loss + came_loss, area_sum + came_area),
    )

    got = exchange(sums.reshape(n_plane, cols, hid + PAD), PLANE)
    got = jnp.sum(got.astype(f32), 0)
    block_in = got[:, :hid].reshape(2, cols // 2, n_ens, hid // n_ens)
    block_in = block_in.transpose(2, 1, 0, 3).reshape(n_ens, cols // 2, PAD)
    block_out = with_scalars(got[:, hid:], *scalars(got[:, hid:]))
    pieces = jnp.concatenate(
        [
            block_in.astype(bf16),
            jnp.broadcast_to(block_out.astype(bf16)[None], (n_ens, cols, PAD)),
        ],
        1,
    )
    final = jnp.sum(exchange(pieces, ENS).astype(f32), 0)
    final_in = final[: cols // 2].reshape(cols // 2, 2, hid // n_ens)
    final_in = final_in.transpose(2, 1, 0).reshape(hid // n_ens, cols)
    final_out = final[cols // 2 :]
    loss_sum, area_all = scalars(final_out)
    weight_total = area_all / count
    factor = points_all / (weight_total * VARS)
    ratio = factor / jnp.sqrt(f32(points_all) * f32(count))
    return (
        loss_sum / (weight_total * VARS),
        (factor * grad_lat).astype(bf16)[None],
        ratio * final_in,
        ratio * final_out[:, :VARS].T,
    )


def solution(mesh):
    ens, grid_all = mesh.devices.shape
    split = (ens // 2, 2, 2, grid_all // 4, 2)
    fine = Mesh(mesh.devices.reshape(split), ENS + PLANE + ("c",))
    grid = PLANE + ("c",)
    in_specs = (P(ENS, None, grid), P(), P(), P(None, grid), P(grid), P())
    out_specs = (P(), P(ENS, None, grid), P(ENS, grid), P(None, grid))
    return jax.shard_map(
        per_device, mesh=fine, in_specs=in_specs, out_specs=out_specs, check_vma=False
    )
```

```python
import functools

import jax
import jax.numpy as jnp
from jax import lax
from jax.experimental import pallas as pl
from jax.experimental.pallas import tpu as pltpu
from jax.sharding import Mesh, PartitionSpec as P

VARS = 99
PAD = 128
HALF = PAD // 2
SPARE = VARS + 1
ENS = ("y", "xh")
PLANE = ("xl", "z")
CHIP_X = ("xh", "xl")
BLOCK = 256

smooth_sq = 0.01
gelu_c = 0.7978845608
gelu_k = 0.044715
f32 = jnp.float32
bf16 = jnp.bfloat16
NT = (((1,), (1,)), ((), ()))


def gelu_value(value):
    inner = jnp.tanh(gelu_c * (value + gelu_k * value * value * value))
    return 0.5 * value * (1.0 + inner)


def gelu_slope(value):
    inner = jnp.tanh(gelu_c * (value + gelu_k * value * value * value))
    return 0.5 * (1.0 + inner) + 0.5 * value * (1.0 - inner * inner) * gelu_c * (
        1.0 + 3.0 * gelu_k * value * value
    )


def exchange(pieces, axes):
    return lax.all_to_all(pieces, axes, split_axis=0, concat_axis=0, tiled=True)


def dot(a, b):
    return jnp.dot(a, b, preferred_element_type=f32)


def dot_nt(a, b):
    return lax.dot_general(a, b, NT, preferred_element_type=f32)


def whole():
    return pl.BlockSpec(memory_space=pltpu.VMEM)


def smem():
    return pl.BlockSpec(memory_space=pltpu.SMEM)


def params(mib):
    return pltpu.CompilerParams(vmem_limit_bytes=mib << 20)


def lanes(shape):
    return lax.broadcasted_iota(jnp.int32, shape, len(shape) - 1)


def forward_kernel(w_in, latent, w_out, hidden, preact, decoded):
    step = pl.program_id(0)

    @pl.when(step == 0)
    def _():
        decoded[...] = jnp.zeros_like(decoded)

    value = dot(w_in[...], latent[...])
    preact[...] = value
    rounded = gelu_value(value).astype(bf16)
    hidden[...] = rounded
    decoded[0:VARS, :] += dot(w_out[...], rounded)


def forward(w_in, latent, w_out):
    hid, lat = w_in.shape
    pts = latent.shape[1]
    return pl.pallas_call(
        forward_kernel,
        grid=(hid // BLOCK,),
        in_specs=[
            pl.BlockSpec((BLOCK, lat), lambda i: (i, 0)),
            pl.BlockSpec((lat, pts), lambda i: (0, 0)),
            pl.BlockSpec((VARS, BLOCK), lambda i: (0, i)),
        ],
        out_specs=[
            pl.BlockSpec((BLOCK, pts), lambda i: (i, 0)),
            pl.BlockSpec((BLOCK, pts), lambda i: (i, 0)),
            pl.BlockSpec((PAD, pts), lambda i: (0, 0)),
        ],
        out_shape=[
            jax.ShapeDtypeStruct((hid, pts), bf16),
            jax.ShapeDtypeStruct((hid, pts), f32),
            jax.ShapeDtypeStruct((PAD, pts), f32),
        ],
        compiler_params=params(16),
        name="forward",
    )(w_in, latent, w_out)


def pairs_kernel(members, cores, fields, target, area, weight_own, dout, sums):
    count = float(members)
    weight = area[...] * weight_own[...]
    slopes = [None] * members
    total = None
    for m in range(1, members):
        for k in range(m):
            diff = fields[m] - fields[k]
            square = diff * diff + smooth_sq
            inverse = lax.rsqrt(square)
            slope = diff * inverse
            apart = square * inverse
            total = apart if total is None else total + apart
            slopes[m] = slope if slopes[m] is None else slopes[m] + slope
            slopes[k] = -slope if slopes[k] is None else slopes[k] - slope
    total = 2.0 * total + count * smooth_sq**0.5
    local = total * (-1.0 / (2.0 * count * (count - 1.0)))
    for m in range(members):
        miss = fields[m] - target[...]
        square = miss * miss + smooth_sq
        inverse = lax.rsqrt(square)
        local = local + square * inverse * (1.0 / count)
        value = weight * (
            miss * inverse * (1.0 / count) - slopes[m] * (1.0 / (count * (count - 1.0)))
        )
        for c in range(cores):
            dout[m * cores + c] = value.astype(bf16)
    loss = jnp.sum(weight * local, keepdims=True)
    here = jnp.sum(area[...], keepdims=True)
    lane = lanes(sums.shape)
    sums[...] = jnp.where(lane == 0, loss, jnp.where(lane == 1, here, 0.0))


def pairs(fields, target, area, weight_own, cores):
    members, own, pts = fields.shape
    return pl.pallas_call(
        functools.partial(pairs_kernel, members, cores),
        in_specs=[whole()] * 4,
        out_specs=[whole()] * 2,
        out_shape=[
            jax.ShapeDtypeStruct((members * cores, own, pts), bf16),
            jax.ShapeDtypeStruct((8, PAD), f32),
        ],
        compiler_params=params(8),
        name="pairs",
    )(fields, target, area, weight_own)


def backward_kernel(
    steps, core, dout, sums, sums_far, w_out_t, slope, slope_far,
    latent, latent_far, hidden, hidden_far, terms, dpre_out, dout_near, dout_far,
):
    step = pl.program_id(0)
    me = core[0]
    rows = terms.shape[1]

    def spread(which):
        value = dout[:, pl.ds(which, 1)].astype(f32)
        return value.reshape(PAD, dout.shape[-1]).astype(bf16)

    @pl.when(step == 0)
    def _():
        dout_near[...] = spread(me)
        dout_far[...] = spread(1 - me)

    def rows_of(ref, part, parts):
        value = ref[:, pl.ds(part, parts)]
        return value.reshape(-1, value.shape[-1])

    @pl.when(step < steps)
    def _():
        first = second = None
        for half, feats in ((slope, latent), (slope_far, latent_far)):
            near = half is slope
            dh = dot(w_out_t[...], (dout_near if near else dout_far)[...])
            dpre = (dh * half[...]).astype(bf16)
            if near:
                dpre_out[...] = dpre
            swapped = jnp.concatenate(
                [
                    dpre[at + off : at + off + HALF]
                    for at in range(0, BLOCK, PAD)
                    for off in (HALF, 0)
                ],
                0,
            )
            a = dot_nt(rows_of(feats, 2 * me, 1), dpre)
            b = dot_nt(rows_of(feats, 2 * me + 1, 1), swapped)
            first = a if first is None else first + a
            second = b if second is None else second + b
        low = lax.rem(lanes(first.shape), PAD) < HALF
        for xh, value in enumerate(
            (jnp.where(low, first, second), jnp.where(low, second, first))
        ):
            for xl in range(2):
                terms[2 * xh + xl] = value[xl * rows : (xl + 1) * rows].astype(bf16)

    @pl.when(step == steps)
    def _():
        out = dot_nt(rows_of(hidden, 2 * me, 2), dout_near[...])
        out += dot_nt(rows_of(hidden_far, 2 * me, 2), dout_far[...])
        out = out.reshape(-1, 2, 16, PAD)
        left = out[:, 0].reshape(-1, PAD)
        right = out[:, 1].reshape(-1, PAD)
        both = sums[0:1, :] + sums_far[0:1, :]
        lane = lanes(both.shape)
        high = both.astype(bf16).astype(f32)
        low = both - high
        parts = jnp.zeros_like(both)
        for k in range(2):
            for j, part in enumerate((high, low)):
                value = jnp.sum(jnp.where(lane == k, part, 0.0), axis=1, keepdims=True)
                parts = jnp.where(lane == SPARE + 2 * k + j, value, parts)
        row = lax.broadcasted_iota(jnp.int32, left.shape, 0)
        left = left + jnp.where(lax.rem(row, 16) == 0, parts, 0.0)
        for xh in range(2):
            for xl in range(2):
                at = slice(xl * rows, (xl + 1) * rows)
                terms[2 * xh + xl, :, 0:PAD] = left[at].astype(bf16)
                terms[2 * xh + xl, :, PAD : 2 * PAD] = right[at].astype(bf16)


def backward(core, dout, sums, sums_far, w_out_t, slope, slope_far, latent, latent_far, hidden, hidden_far):
    hid, pts = slope.shape
    plane = latent.shape[0]
    steps = hid // BLOCK
    rows = plane * 16 // 2
    keep = lambda *shape: pl.BlockSpec(shape, lambda i: (0,) * len(shape))
    block = lambda i: (jnp.minimum(i, steps - 1), 0)
    return pl.pallas_call(
        functools.partial(backward_kernel, steps),
        grid=(steps + 1,),
        in_specs=[
            smem(),
            keep(*dout.shape),
            keep(*sums.shape),
            keep(*sums.shape),
            pl.BlockSpec((BLOCK, PAD), block),
            pl.BlockSpec((BLOCK, pts), block),
            pl.BlockSpec((BLOCK, pts), block),
            keep(*latent.shape),
            keep(*latent.shape),
            keep(*hidden.shape),
            keep(*hidden.shape),
        ],
        out_specs=[
            pl.BlockSpec((4, rows, 2 * PAD), lambda i: (0, 0, i)),
            pl.BlockSpec((BLOCK, pts), block),
        ],
        out_shape=[
            jax.ShapeDtypeStruct((4, rows, hid + 2 * PAD), bf16),
            jax.ShapeDtypeStruct((hid, pts), bf16),
        ],
        scratch_shapes=[pltpu.VMEM((PAD, pts), bf16)] * 2,
        compiler_params=params(24),
        name="backward",
    )(core, dout, sums, sums_far, w_out_t, slope, slope_far, latent, latent_far, hidden, hidden_far)


def split_again(tile):
    lane = lanes(tile.shape)
    value = tile + pltpu.roll(tile, PAD - 1, 1)
    high = value.astype(bf16).astype(f32)
    low = pltpu.roll(value - high, 1, 1)
    odd = (lane == SPARE + 1) | (lane == SPARE + 3)
    even = (lane == SPARE) | (lane == SPARE + 2)
    return jnp.where(even, high, jnp.where(odd, low, tile))


def add_x_kernel(hid, got, out):
    value = got[0].astype(f32)
    for k in range(1, got.shape[0]):
        value = value + got[k].astype(f32)
    out[:, 0:hid] = value[:, 0:hid].astype(bf16)
    out[:, hid : hid + PAD] = split_again(value[:, hid : hid + PAD]).astype(bf16)
    out[:, hid + PAD :] = value[:, hid + PAD :].astype(bf16)


def add_x(got, hid):
    return pl.pallas_call(
        functools.partial(add_x_kernel, hid),
        in_specs=[whole()],
        out_specs=whole(),
        out_shape=jax.ShapeDtypeStruct(got.shape[1:], bf16),
        compiler_params=params(8),
        name="add_x",
    )(got)


def add_z_kernel(hid, got, out):
    value = got[0].astype(f32)
    for k in range(1, got.shape[0]):
        value = value + got[k].astype(f32)
    left = split_again(value[:, hid : hid + PAD]).astype(bf16)
    right = value[:, hid + PAD :].astype(bf16)
    for y in range(out.shape[0]):
        out[y, :, 0:PAD] = value[:, y * PAD : (y + 1) * PAD].astype(bf16)
        out[y, :, PAD : 2 * PAD] = left
        out[y, :, 2 * PAD :] = right


def add_z(got, hid):
    return pl.pallas_call(
        functools.partial(add_z_kernel, hid),
        in_specs=[whole()],
        out_specs=whole(),
        out_shape=jax.ShapeDtypeStruct((hid // PAD, got.shape[1], 3 * PAD), bf16),
        compiler_params=params(4),
        name="add_z",
    )(got)


def finish_kernel(count, points_all, turn, got, grad, loss, grad_lat, grad_in, grad_out, factor):
    @pl.when(pl.program_id(0) == 0)
    def _():
        value = got[0].astype(f32)
        for k in range(1, got.shape[0]):
            value = value + got[k].astype(f32)
        left = value[:, PAD : 2 * PAD]
        head = left[0:1, :]
        lane = lanes(head.shape)

        def pick(at):
            mine = (lane == at) | (lane == at + 1)
            return jnp.sum(jnp.where(mine, head, 0.0), axis=1, keepdims=True)

        weight_total = pick(SPARE + 2) * (1.0 / count)
        scale = 1.0 / (weight_total * VARS)
        loss[...] = pick(SPARE) * scale
        scale = points_all * scale
        factor[...] = jnp.broadcast_to(scale, factor.shape)
        ratio = scale * (1.0 / (points_all * count) ** 0.5)
        tile = value[:, 0:PAD] * ratio
        other = pltpu.roll(tile, HALF, 1)
        even = turn[0] == 0
        grad_in[0:16, :] = jnp.where(even, tile, other)[:, 0:HALF]
        grad_in[16:32, :] = jnp.where(even, other, tile)[:, 0:HALF]
        grad_out[0:16, :] = (left * ratio)[:, 0:VARS]
        grad_out[16:32, :] = (value[:, 2 * PAD :] * ratio)[:, 0:VARS]

    grad_lat[...] = (grad[...] * factor[0:1, 0:1]).astype(bf16)


def finish(turn, got, grad, count, points_all):
    lat, pts = grad.shape
    keep = lambda *shape: pl.BlockSpec(shape, lambda i: (0,) * len(shape))
    return pl.pallas_call(
        functools.partial(finish_kernel, count, points_all),
        grid=(lat // BLOCK,),
        in_specs=[
            smem(),
            keep(*got.shape),
            pl.BlockSpec((BLOCK, pts), lambda i: (i, 0)),
        ],
        out_specs=[
            keep(1, 1),
            pl.BlockSpec((BLOCK, pts), lambda i: (i, 0)),
            keep(32, HALF),
            keep(32, VARS),
        ],
        out_shape=[
            jax.ShapeDtypeStruct((1, 1), f32),
            jax.ShapeDtypeStruct((lat, pts), bf16),
            jax.ShapeDtypeStruct((32, HALF), f32),
            jax.ShapeDtypeStruct((32, VARS), f32),
        ],
        scratch_shapes=[pltpu.VMEM((8, PAD), f32)],
        compiler_params=params(8),
        name="finish",
    )(turn, got, grad)


def per_device(latent, w_in, w_out, target, area, var_weight):
    n_ens = lax.axis_size(ENS)
    n_plane = lax.axis_size(PLANE)
    n_core = lax.axis_size("c")
    n_z = lax.axis_size("z")
    pts = area.shape[0]
    hid, lat = w_in.shape
    own = PAD // n_ens
    me = lax.axis_index(ENS)
    core = lax.axis_index("c")
    swap = [(0, 1), (1, 0)]
    features = latent[0]

    hidden, preact, decoded = forward(w_in, features, w_out)

    fields = exchange(decoded.reshape(n_ens, own, pts), ENS)
    features_late, preact_late, _ = lax.optimization_barrier((features, preact, decoded))
    far = lax.ppermute(features_late, "c", swap)
    slope = gelu_slope(preact_late)
    target_own = lax.dynamic_slice_in_dim(
        jnp.pad(target, ((0, PAD - VARS), (0, 0))), me * own, own
    )
    weight_own = lax.dynamic_slice_in_dim(
        jnp.pad(var_weight, (0, PAD - VARS)), me * own, own
    )
    dout, sums = pairs(fields, target_own, area[None, :], weight_own[:, None], n_core)

    dout_got = exchange(dout, ENS + ("c",))
    sums_far = lax.ppermute(sums, "c", swap)
    far_late, _ = lax.optimization_barrier((far, dout))
    preact_far = dot(w_in, far_late)
    hidden_far = gelu_value(preact_far).astype(bf16)
    slope_far = gelu_slope(preact_far)
    w_out_t = jnp.pad(w_out, ((0, PAD - VARS), (0, 0))).T

    groups = lambda value: value.reshape(n_plane, 2 * n_core, 16, pts)
    terms, dpre = backward(
        core.astype(jnp.int32)[None],
        dout_got.reshape(n_ens, n_core, own, pts),
        sums, sums_far, w_out_t, slope, slope_far,
        groups(features), groups(far_late), groups(hidden), groups(hidden_far),
    )

    got = exchange(terms, CHIP_X)
    grad = lax.dot_general(
        w_in, dpre, (((0,), (0,)), ((), ())), preferred_element_type=f32
    )
    got = exchange(add_x(got, hid).reshape(n_z, 16, hid + 2 * PAD), "z")
    got = exchange(add_z(got, hid), "y")
    loss, grad_lat, grad_in, grad_out = finish(
        lax.axis_index("xh").astype(jnp.int32)[None],
        got, grad, float(n_ens), float(n_plane * n_core * pts),
    )
    return loss[0, 0], grad_lat[None], grad_in.T, grad_out.T


def solution(mesh):
    ens, grid_all = mesh.devices.shape
    split = (ens // 2, 2, 2, grid_all // 4, 2)
    fine = Mesh(mesh.devices.reshape(split), ENS + PLANE + ("c",))
    grid = PLANE + ("c",)
    in_specs = (P(ENS, None, grid), P(), P(), P(None, grid), P(grid), P())
    out_specs = (P(), P(ENS, None, grid), P(ENS, grid), P(None, grid))
    return jax.shard_map(
        per_device, mesh=fine, in_specs=in_specs, out_specs=out_specs, check_vma=False
    )
```

```python
import functools

import jax
import jax.numpy as jnp
from jax import lax
from jax.experimental import pallas as pl
from jax.experimental.pallas import tpu as pltpu
from jax.sharding import Mesh, PartitionSpec as P

VARS = 99
PAD = 128
HALF = PAD // 2
OWN = 8
ENS = ("y", "xh")
PLANE = ("xl", "z")
CHIP_X = ("xh", "xl")
BLOCK = 256

smooth_sq = 0.01
gelu_c = 0.7978845608
gelu_k = 0.044715
f32 = jnp.float32
bf16 = jnp.bfloat16
NT = (((1,), (1,)), ((), ()))


def gelu_value(value):
    inner = jnp.tanh(gelu_c * (value + gelu_k * value * value * value))
    return 0.5 * value * (1.0 + inner)


def gelu_slope(value):
    inner = jnp.tanh(gelu_c * (value + gelu_k * value * value * value))
    return 0.5 * (1.0 + inner) + 0.5 * value * (1.0 - inner * inner) * gelu_c * (
        1.0 + 3.0 * gelu_k * value * value
    )


def exchange(pieces, axes):
    return lax.all_to_all(pieces, axes, split_axis=0, concat_axis=0, tiled=True)


def dot(a, b):
    return jnp.dot(a, b, preferred_element_type=f32)


def dot_nt(a, b):
    return lax.dot_general(a, b, NT, preferred_element_type=f32)


def whole():
    return pl.BlockSpec(memory_space=pltpu.VMEM)


def smem():
    return pl.BlockSpec(memory_space=pltpu.SMEM)


def hbm():
    return pl.BlockSpec(memory_space=pltpu.HBM)


def in_hbm(*arrays):
    return [pltpu.with_memory_space_constraint(array, pltpu.HBM) for array in arrays]


def params(mib):
    return pltpu.CompilerParams(vmem_limit_bytes=mib << 20)


class Copies:
    def __init__(self, sems):
        self.sems = sems
        self.used = 0
        self.open = []

    def start(self, source, target):
        copy = pltpu.make_async_copy(source, target, self.sems.at[self.used])
        self.used += 1
        copy.start()
        self.open.append(copy)
        return copy

    def wait(self, copy):
        copy.wait()
        self.open = [other for other in self.open if other is not copy]

    def finish(self):
        for copy in self.open:
            self.wait(copy)


def scratch(*shapes, copies):
    return [pltpu.VMEM(shape, kind) for shape, kind in shapes] + [
        pltpu.SemaphoreType.DMA((copies,))
    ]


def blocks(size):
    return [slice(at, at + BLOCK) for at in range(0, size, BLOCK)]


def spare(k):
    return OWN * (k + 1) - 1


def row_table():
    row = lax.broadcasted_iota(jnp.int32, (PAD, VARS), 0)
    held = lax.rem(row, OWN) < OWN - 1
    variable = lax.div(row, OWN) * (OWN - 1) + lax.rem(row, OWN)
    return held & (variable == lanes((PAD, VARS)))


def lanes(shape):
    return lax.broadcasted_iota(jnp.int32, shape, len(shape) - 1)


def forward_kernel(
    w_in, latent, w_out, hidden, preact, decoded,
    w_in_v, latent_v, w_out_v, hidden_v, preact_v, decoded_v, sems,
):
    copies = Copies(sems)
    parts = blocks(w_in.shape[0])
    first = [copies.start(latent, latent_v)]
    weights = [copies.start(w_in.at[here], w_in_v.at[here]) for here in parts[:1]]
    first.append(copies.start(w_out, w_out_v))
    weights += [copies.start(w_in.at[here], w_in_v.at[here]) for here in parts[1:]]
    for copy in first:
        copies.wait(copy)
    w_out_rows = dot(row_table().astype(bf16), w_out_v[...]).astype(bf16)
    total = None
    for here, weight in zip(parts, weights):
        copies.wait(weight)
        value = dot(w_in_v[here, :], latent_v[...])
        preact_v[here, :] = value
        copies.start(preact_v.at[here], preact.at[here])
        rounded = gelu_value(value).astype(bf16)
        hidden_v[here, :] = rounded
        copies.start(hidden_v.at[here], hidden.at[here])
        part = dot(w_out_rows[:, here], rounded)
        total = part if total is None else total + part
    decoded_v[...] = total
    copies.start(decoded_v, decoded)
    copies.finish()


def forward(w_in, latent, w_out):
    hid, lat = w_in.shape
    pts = latent.shape[1]
    count = len(blocks(hid))
    return pl.pallas_call(
        forward_kernel,
        in_specs=[hbm()] * 3,
        out_specs=[hbm()] * 3,
        out_shape=[
            pltpu.HBM((hid, pts), bf16),
            pltpu.HBM((hid, pts), f32),
            pltpu.HBM((PAD, pts), f32),
        ],
        scratch_shapes=scratch(
            ((hid, lat), bf16), ((lat, pts), bf16), ((VARS, hid), bf16),
            ((hid, pts), bf16), ((hid, pts), f32), ((PAD, pts), f32),
            copies=3 * count + 3,
        ),
        compiler_params=params(16),
        name="forward",
    )(*in_hbm(w_in, latent, w_out))


def far_kernel(w_in, latent, hidden, slope, w_in_v, latent_v, hidden_v, slope_v, sems):
    copies = Copies(sems)
    parts = blocks(w_in.shape[0])
    first = copies.start(latent, latent_v)
    weights = [copies.start(w_in.at[here], w_in_v.at[here]) for here in parts]
    copies.wait(first)
    for here, weight in zip(parts, weights):
        copies.wait(weight)
        value = dot(w_in_v[here, :], latent_v[...])
        hidden_v[here, :] = gelu_value(value).astype(bf16)
        copies.start(hidden_v.at[here], hidden.at[here])
        slope_v[here, :] = gelu_slope(value)
        copies.start(slope_v.at[here], slope.at[here])
    copies.finish()


def far_forward(w_in, latent):
    hid, lat = w_in.shape
    pts = latent.shape[1]
    return pl.pallas_call(
        far_kernel,
        in_specs=[hbm()] * 2,
        out_specs=[hbm()] * 2,
        out_shape=[
            pltpu.HBM((hid, pts), bf16),
            pltpu.HBM((hid, pts), f32),
        ],
        scratch_shapes=scratch(
            ((hid, lat), bf16), ((lat, pts), bf16), ((hid, pts), bf16), ((hid, pts), f32),
            copies=3 * len(blocks(hid)) + 1,
        ),
        compiler_params=params(16),
        cost_estimate=pl.CostEstimate(
            flops=2 * hid * lat * pts, bytes_accessed=4 << 20, transcendentals=hid * pts
        ),
        name="far_forward",
    )(*in_hbm(w_in), latent)


def slope_kernel(preact, w_out, slope, w_out_t, preact_v, w_out_v, slope_v, w_out_t_v, sems):
    copies = Copies(sems)
    parts = blocks(preact.shape[0])
    first = copies.start(w_out, w_out_v)
    inputs = [copies.start(preact.at[here], preact_v.at[here]) for here in parts]
    copies.wait(first)
    w_out_t_v[...] = lax.dot_general(
        w_out_v[...], row_table().astype(bf16), (((0,), (1,)), ((), ())), preferred_element_type=f32
    ).astype(bf16)
    copies.start(w_out_t_v, w_out_t)
    for here, copy in zip(parts, inputs):
        copies.wait(copy)
        slope_v[here, :] = gelu_slope(preact_v[here, :])
        copies.start(slope_v.at[here], slope.at[here])
    copies.finish()


def slopes(preact, w_out):
    hid, pts = preact.shape
    return pl.pallas_call(
        slope_kernel,
        in_specs=[hbm()] * 2,
        out_specs=[hbm()] * 2,
        out_shape=[
            pltpu.HBM((hid, pts), f32),
            pltpu.HBM((hid, PAD), bf16),
        ],
        scratch_shapes=scratch(
            ((hid, pts), f32), ((VARS, hid), bf16), ((hid, pts), f32), ((hid, PAD), bf16),
            copies=2 * len(blocks(hid)) + 2,
        ),
        compiler_params=params(16),
        cost_estimate=pl.CostEstimate(
            flops=20 * hid * pts, bytes_accessed=4 << 20, transcendentals=hid * pts
        ),
        name="slopes",
    )(*in_hbm(preact, w_out))


def grad_kernel(w_in, dpre, grad, w_in_v, dpre_v, grad_v, sems):
    copies = Copies(sems)
    inputs = [copies.start(dpre, dpre_v), copies.start(w_in, w_in_v)]
    for copy in inputs:
        copies.wait(copy)
    for here in blocks(w_in.shape[1]):
        grad_v[here, :] = lax.dot_general(
            w_in_v[:, here], dpre_v[...], (((0,), (0,)), ((), ())), preferred_element_type=f32
        )
    copies.start(grad_v, grad)
    copies.finish()


def grad_latent(w_in, dpre):
    hid, lat = w_in.shape
    pts = dpre.shape[1]
    return pl.pallas_call(
        grad_kernel,
        in_specs=[hbm()] * 2,
        out_specs=hbm(),
        out_shape=pltpu.HBM((lat, pts), f32),
        scratch_shapes=scratch(
            ((hid, lat), bf16), ((hid, pts), bf16), ((lat, pts), f32), copies=3
        ),
        compiler_params=params(16),
        cost_estimate=pl.CostEstimate(
            flops=2 * hid * lat * pts, bytes_accessed=4 << 20, transcendentals=0
        ),
        name="grad_latent",
    )(*in_hbm(w_in, dpre))


def pairs_kernel(
    members, cores, owner, fields, target_all, area_h, var_weight_h, dout,
    target_v, area_v, var_weight_v, dout_v, sems,
):
    copies = Copies(sems)
    inputs = [
        copies.start(area_h, area_v),
        copies.start(var_weight_h, var_weight_v),
        copies.start(target_all, target_v),
    ]
    count = float(members)
    own, pts = fields.shape[1:]
    slopes = [None] * members
    total = None
    for m in range(1, members):
        for k in range(m):
            diff = fields[m] - fields[k]
            square = diff * diff + smooth_sq
            inverse = lax.rsqrt(square)
            slope = diff * inverse
            apart = square * inverse
            total = apart if total is None else total + apart
            slopes[m] = slope if slopes[m] is None else slopes[m] + slope
            slopes[k] = -slope if slopes[k] is None else slopes[k] - slope
    total = 2.0 * total + count * smooth_sq**0.5
    local = total * (-1.0 / (2.0 * count * (count - 1.0)))
    for copy in inputs:
        copies.wait(copy)
    row = lax.broadcasted_iota(jnp.int32, (own, VARS), 0)
    held = (row < own - 1) & (lanes((own, VARS)) == owner[0] * (own - 1) + row)
    weight = jnp.sum(jnp.where(held, var_weight_v[...], 0.0), axis=1, keepdims=True)
    weight = area_v[...] * weight
    target = lax.dot_general(
        held.astype(f32), target_v[...], (((1,), (0,)), ((), ())),
        precision=lax.Precision.HIGHEST, preferred_element_type=f32,
    )
    values = []
    for m in range(members):
        miss = fields[m] - target
        square = miss * miss + smooth_sq
        inverse = lax.rsqrt(square)
        local = local + square * inverse * (1.0 / count)
        values.append(
            weight
            * (miss * inverse * (1.0 / count) - slopes[m] * (1.0 / (count * (count - 1.0))))
        )
    loss = jnp.sum(weight * local, keepdims=True)
    here = jnp.sum(area_v[...], keepdims=True)
    lane = lanes((own, pts))
    last = lax.broadcasted_iota(jnp.int32, (own, pts), 0) == own - 1
    ride = jnp.zeros((own, pts), f32)
    for k, value in enumerate((loss, here)):
        high = value.astype(bf16).astype(f32)
        ride = jnp.where(lane == 2 * k, high, jnp.where(lane == 2 * k + 1, value - high, ride))
    for m in range(members):
        value = jnp.where(last, ride, values[m]).astype(bf16)
        for c in range(cores):
            dout_v[m * cores + c] = value
    copies.start(dout_v, dout)
    copies.finish()


def pairs(owner, fields, target, area, var_weight, cores):
    members, own, pts = fields.shape
    return pl.pallas_call(
        functools.partial(pairs_kernel, members, cores),
        in_specs=[smem(), whole()] + [hbm()] * 3,
        out_specs=hbm(),
        out_shape=pltpu.HBM((members * cores, own, pts), bf16),
        scratch_shapes=scratch(
            (target.shape, f32), (area.shape, f32), (var_weight.shape, f32),
            ((members * cores, own, pts), bf16),
            copies=4,
        ),
        compiler_params=params(8),
        name="pairs",
    )(owner, fields, *in_hbm(target, area, var_weight))


def backward_kernel(
    core, dout, w_out_t, slope, slope_far, latent, latent_far, hidden, hidden_far,
    terms, dpre_out,
    w_out_t_v, slope_v, slope_far_v, latent_v, latent_far_v, hidden_v, hidden_far_v,
    terms_v, dpre_v, sems,
):
    copies = Copies(sems)
    me = core[0]
    rows = terms.shape[1]
    hid, pts = slope.shape
    parts = blocks(hid)

    def fetch(source, target, here):
        return copies.start(source.at[here], target.at[here])

    mine = (slice(None), pl.ds(2 * me, 2))
    fetched = [copies.start(w_out_t, w_out_t_v)]
    halves = [[fetch(slope, slope_v, parts[0]), fetch(slope_far, slope_far_v, parts[0])]]
    fetched.append(copies.start(latent.at[mine], latent_v))
    fetched.append(copies.start(latent_far.at[mine], latent_far_v))
    for here in parts[1:]:
        halves.append([fetch(slope, slope_v, here), fetch(slope_far, slope_far_v, here)])
    late = [
        copies.start(hidden.at[mine], hidden_v),
        copies.start(hidden_far.at[mine], hidden_far_v),
    ]

    row = lax.broadcasted_iota(jnp.int32, (PAD, pts), 0)
    last = lax.rem(row, OWN) == OWN - 1
    seeds = []
    ride = jnp.zeros((1, pts), f32)
    for which in (me, 1 - me):
        value = dout[:, pl.ds(which, 1)].astype(f32).reshape(PAD, pts)
        ride = ride + jnp.sum(jnp.where(last, value, 0.0), axis=0, keepdims=True)
        seeds.append(jnp.where(last, 0.0, value).astype(bf16))

    for copy in fetched:
        copies.wait(copy)
    features = [
        [ref[:, k].reshape(-1, pts) for k in range(2)] for ref in (latent_v, latent_far_v)
    ]
    for here, half in zip(parts, halves):
        first = second = None
        for copy in half:
            copies.wait(copy)
        for k, ref in enumerate((slope_v, slope_far_v)):
            dh = dot(w_out_t_v[here, :], seeds[k])
            dpre = (dh * ref[here, :]).astype(bf16)
            if k == 0:
                dpre_v[here, :] = dpre
                copies.start(dpre_v.at[here], dpre_out.at[here])
            swapped = jnp.concatenate(
                [
                    dpre[base + off : base + off + HALF]
                    for base in range(0, BLOCK, PAD)
                    for off in (HALF, 0)
                ],
                0,
            )
            a = dot_nt(features[k][0], dpre)
            b = dot_nt(features[k][1], swapped)
            first = a if first is None else first + a
            second = b if second is None else second + b
        low = lax.rem(lanes(first.shape), PAD) < HALF
        for xh, value in enumerate(
            (jnp.where(low, first, second), jnp.where(low, second, first))
        ):
            for xl in range(2):
                terms_v[2 * xh + xl, :, here] = value[xl * rows : (xl + 1) * rows].astype(bf16)
        copies.start(terms_v.at[:, :, here], terms.at[:, :, here])

    for copy in late:
        copies.wait(copy)
    out = dot_nt(hidden_v[...].reshape(-1, pts), seeds[0])
    out += dot_nt(hidden_far_v[...].reshape(-1, pts), seeds[1])
    out = out.reshape(-1, 2, 16, PAD)
    left = out[:, 0].reshape(-1, PAD)
    right = out[:, 1].reshape(-1, PAD)
    lane = lanes((1, PAD))
    parts = jnp.zeros((1, PAD), f32)
    for k in range(2):
        mine = lax.div(lanes((1, pts)), 2) == k
        value = jnp.sum(jnp.where(mine, ride, 0.0), axis=1, keepdims=True)
        high = value.astype(bf16).astype(f32)
        parts = jnp.where(lane == spare(2 * k), high, parts)
        parts = jnp.where(lane == spare(2 * k + 1), value - high, parts)
    row = lax.rem(lax.broadcasted_iota(jnp.int32, left.shape, 0), 16)
    unused = lax.rem(lanes(left.shape), OWN) == OWN - 1
    left = jnp.where(unused, jnp.where(row == 0, parts, 0.0), left)
    for xh in range(2):
        for xl in range(2):
            piece = slice(xl * rows, (xl + 1) * rows)
            terms_v[2 * xh + xl, :, hid : hid + PAD] = left[piece].astype(bf16)
            terms_v[2 * xh + xl, :, hid + PAD :] = right[piece].astype(bf16)
    tail = (slice(None), slice(None), slice(hid, hid + 2 * PAD))
    copies.start(terms_v.at[tail], terms.at[tail])
    copies.finish()


def backward(core, dout, w_out_t, slope, slope_far, latent, latent_far, hidden, hidden_far):
    hid, pts = slope.shape
    plane = latent.shape[0]
    shape = (4, plane * 16 // 2, hid + 2 * PAD)
    half = ((plane, 2, 16, pts), bf16)
    return pl.pallas_call(
        backward_kernel,
        in_specs=[smem(), whole()] + [hbm()] * 7,
        out_specs=[hbm()] * 2,
        out_shape=[
            pltpu.HBM(shape, bf16),
            pltpu.HBM((hid, pts), bf16),
        ],
        scratch_shapes=scratch(
            ((hid, PAD), bf16), ((hid, pts), f32), ((hid, pts), f32), half, half, half, half,
            (shape, bf16), ((hid, pts), bf16),
            copies=4 * len(blocks(hid)) + 6,
        ),
        compiler_params=params(24),
        name="backward",
    )(core, dout, *in_hbm(w_out_t, slope, slope_far, latent), latent_far, *in_hbm(hidden, hidden_far))


def split_again(tile):
    lane = lanes(tile.shape)
    value = tile + pltpu.roll(tile, PAD - OWN, 1)
    high = value.astype(bf16).astype(f32)
    low = pltpu.roll(value - high, OWN, 1)
    even = (lane == spare(0)) | (lane == spare(2))
    odd = (lane == spare(1)) | (lane == spare(3))
    return jnp.where(even, high, jnp.where(odd, low, tile))


def add_x_kernel(hid, got, out):
    value = got[0].astype(f32)
    for k in range(1, got.shape[0]):
        value = value + got[k].astype(f32)
    out[:, 0:hid] = value[:, 0:hid].astype(bf16)
    out[:, hid : hid + PAD] = split_again(value[:, hid : hid + PAD]).astype(bf16)
    out[:, hid + PAD :] = value[:, hid + PAD :].astype(bf16)


def add_x(got, hid):
    return pl.pallas_call(
        functools.partial(add_x_kernel, hid),
        in_specs=[whole()],
        out_specs=whole(),
        out_shape=jax.ShapeDtypeStruct(got.shape[1:], bf16),
        compiler_params=params(8),
        name="add_x",
    )(got)


def add_z_kernel(hid, got, out):
    value = got[0].astype(f32)
    for k in range(1, got.shape[0]):
        value = value + got[k].astype(f32)
    left = split_again(value[:, hid : hid + PAD]).astype(bf16)
    right = value[:, hid + PAD :].astype(bf16)
    for y in range(out.shape[0]):
        out[y, :, 0:PAD] = value[:, y * PAD : (y + 1) * PAD].astype(bf16)
        out[y, :, PAD : 2 * PAD] = left
        out[y, :, 2 * PAD :] = right


def add_z(got, hid):
    return pl.pallas_call(
        functools.partial(add_z_kernel, hid),
        in_specs=[whole()],
        out_specs=whole(),
        out_shape=jax.ShapeDtypeStruct((hid // PAD, got.shape[1], 3 * PAD), bf16),
        compiler_params=params(4),
        name="add_z",
    )(got)


def finish_kernel(
    count, points_all, turn, got, grad, loss, grad_lat, grad_in, grad_out, grad_lat_v, sems
):
    copies = Copies(sems)
    value = got[0].astype(f32)
    for k in range(1, got.shape[0]):
        value = value + got[k].astype(f32)
    left = value[:, PAD : 2 * PAD]
    head = left[0:1, :]
    lane = lanes(head.shape)

    def pick(k):
        mine = (lane == spare(2 * k)) | (lane == spare(2 * k + 1))
        return jnp.sum(jnp.where(mine, head, 0.0), axis=1, keepdims=True)

    weight_total = pick(1) * (1.0 / (count * count))
    scale = 1.0 / (weight_total * VARS)
    loss[...] = pick(0) * (1.0 / count) * scale
    scale = points_all * scale
    for here in blocks(grad.shape[0]):
        grad_lat_v[here, :] = (grad[here, :] * scale).astype(bf16)
        copies.start(grad_lat_v.at[here], grad_lat.at[here])
    ratio = scale * (1.0 / (points_all * count) ** 0.5)
    tile = value[:, 0:PAD] * ratio
    other = pltpu.roll(tile, HALF, 1)
    even = turn[0] == 0
    grad_in[0:16, :] = jnp.where(even, tile, other)[:, 0:HALF]
    grad_in[16:32, :] = jnp.where(even, other, tile)[:, 0:HALF]
    both = jnp.concatenate([left, value[:, 2 * PAD :]], 0) * ratio
    grad_out[...] = lax.dot_general(
        both, row_table().astype(f32), (((1,), (0,)), ((), ())),
        precision=lax.Precision.HIGHEST, preferred_element_type=f32,
    )
    copies.finish()


def finish(turn, got, grad, count, points_all):
    lat, pts = grad.shape
    return pl.pallas_call(
        functools.partial(finish_kernel, count, points_all),
        in_specs=[smem(), whole(), whole()],
        out_specs=[whole(), hbm(), whole(), whole()],
        out_shape=[
            jax.ShapeDtypeStruct((1, 1), f32),
            jax.ShapeDtypeStruct((lat, pts), bf16),
            jax.ShapeDtypeStruct((32, HALF), f32),
            jax.ShapeDtypeStruct((32, VARS), f32),
        ],
        scratch_shapes=scratch(((lat, pts), bf16), copies=len(blocks(lat))),
        compiler_params=params(8),
        name="finish",
    )(turn, got, grad)


def per_device(latent, w_in, w_out, target, area, var_weight):
    n_ens = lax.axis_size(ENS)
    n_plane = lax.axis_size(PLANE)
    n_core = lax.axis_size("c")
    n_z = lax.axis_size("z")
    pts = area.shape[0]
    hid, _ = w_in.shape
    own = PAD // n_ens
    assert own == OWN
    me = lax.axis_index(ENS)
    core = lax.axis_index("c")
    swap = [(0, 1), (1, 0)]
    features = latent[0]

    hidden, preact, decoded = forward(w_in, features, w_out)

    fields = exchange(decoded.reshape(n_ens, own, pts), ENS)
    late = lax.optimization_barrier((features, preact, w_out, decoded))
    far = lax.ppermute(late[0], "c", swap)
    slope, w_out_t = slopes(late[1], late[2])
    dout = pairs(
        me.astype(jnp.int32)[None], fields, target, area[None, :], var_weight[None, :], n_core
    )

    dout_got = exchange(dout, ENS + ("c",))
    far, _ = lax.optimization_barrier((far, dout))
    hidden_far, slope_far = far_forward(w_in, far)

    groups = lambda value: value.reshape(n_plane, 2 * n_core, 16, pts)
    terms, dpre = backward(
        core.astype(jnp.int32)[None],
        dout_got.reshape(n_ens, n_core, own, pts),
        w_out_t, slope, slope_far,
        groups(features), groups(far), groups(hidden), groups(hidden_far),
    )

    got = exchange(terms, CHIP_X)
    grad = grad_latent(w_in, dpre)
    got, grad = lax.optimization_barrier((got, grad))
    got = exchange(add_x(got, hid).reshape(n_z, 16, hid + 2 * PAD), "z")
    got = exchange(add_z(got, hid), "y")
    loss, grad_lat, part_in, part_out = finish(
        lax.axis_index("xh").astype(jnp.int32)[None],
        got, grad, float(n_ens), float(n_plane * n_core * pts),
    )
    return loss[0, 0], grad_lat[None], part_in.T, part_out.T


def solution(mesh):
    ens, grid_all = mesh.devices.shape
    split = (ens // 2, 2, 2, grid_all // 4, 2)
    fine = Mesh(mesh.devices.reshape(split), ENS + PLANE + ("c",))
    grid = PLANE + ("c",)
    in_specs = (P(ENS, None, grid), P(), P(), P(None, grid), P(grid), P())
    out_specs = (P(), P(ENS, None, grid), P(ENS, grid), P(None, grid))
    return jax.shard_map(
        per_device, mesh=fine, in_specs=in_specs, out_specs=out_specs, check_vma=False
    )
```

```python
import functools

import jax
import jax.numpy as jnp
from jax import lax
from jax.experimental import pallas as pl
from jax.experimental.pallas import tpu as pltpu
from jax.sharding import Mesh, PartitionSpec as P

VARS = 99
PAD = 128
HALF = PAD // 2
OWN = 8
ENS = ("y", "xh")
PLANE = ("xl", "z")
CHIP_X = ("xh", "xl")
BLOCK = 256

smooth_sq = 0.01
gelu_c = 0.7978845608
gelu_k = 0.044715
f32 = jnp.float32
bf16 = jnp.bfloat16
NT = (((1,), (1,)), ((), ()))


def gelu(value):
    square = value * value
    inner = jnp.tanh(gelu_c * (value + gelu_k * square * value))
    both = 0.5 * (1.0 + inner)
    slope = both + 0.5 * value * (1.0 - inner * inner) * (
        gelu_c * (1.0 + 3.0 * gelu_k * square)
    )
    return value * both, slope


def exchange(pieces, axes):
    return lax.all_to_all(pieces, axes, split_axis=0, concat_axis=0, tiled=True)


def dot(a, b):
    return jnp.dot(a, b, preferred_element_type=f32)


def dot_nt(a, b):
    return lax.dot_general(a, b, NT, preferred_element_type=f32)


def whole():
    return pl.BlockSpec(memory_space=pltpu.VMEM)


def smem():
    return pl.BlockSpec(memory_space=pltpu.SMEM)


def hbm():
    return pl.BlockSpec(memory_space=pltpu.HBM)


def in_hbm(*arrays):
    return [pltpu.with_memory_space_constraint(array, pltpu.HBM) for array in arrays]


def params(mib):
    return pltpu.CompilerParams(vmem_limit_bytes=mib << 20)


class Copies:
    def __init__(self, sems):
        self.sems = sems
        self.used = 0
        self.open = []

    def start(self, source, target):
        copy = pltpu.make_async_copy(source, target, self.sems.at[self.used])
        self.used += 1
        copy.start()
        self.open.append(copy)
        return copy

    def wait(self, copy):
        copy.wait()
        self.open = [other for other in self.open if other is not copy]

    def finish(self):
        for copy in self.open:
            self.wait(copy)


def scratch(*shapes, copies):
    return [pltpu.VMEM(shape, kind) for shape, kind in shapes] + [
        pltpu.SemaphoreType.DMA((copies,))
    ]


def blocks(size):
    return [slice(at, at + BLOCK) for at in range(0, size, BLOCK)]


def spare(k):
    return OWN * (k + 1) - 1


def row_table():
    row = lax.broadcasted_iota(jnp.int32, (PAD, VARS), 0)
    held = lax.rem(row, OWN) < OWN - 1
    variable = lax.div(row, OWN) * (OWN - 1) + lax.rem(row, OWN)
    return held & (variable == lanes((PAD, VARS)))


def lanes(shape):
    return lax.broadcasted_iota(jnp.int32, shape, len(shape) - 1)


def load_weights(copies, w_in, w_in_v):
    loads = []
    for here in blocks(w_in.shape[0]):
        middle = (here.start + here.stop) // 2
        loads.append(
            [
                copies.start(w_in.at[part], w_in_v.at[part])
                for part in (slice(here.start, middle), slice(middle, here.stop))
            ]
        )
    return loads


def forward_kernel(
    w_in, latent, w_out, hidden, slope, decoded,
    w_in_v, latent_v, w_out_v, hidden_v, slope_v, decoded_v, sems,
):
    copies = Copies(sems)
    first = copies.start(latent, latent_v)
    loads = load_weights(copies, w_in, w_in_v)
    rows = copies.start(w_out, w_out_v)
    copies.wait(first)
    for here, load in zip(blocks(w_in.shape[0]), loads):
        for copy in load:
            copies.wait(copy)
        value, bend = gelu(dot(w_in_v[here, :], latent_v[...]))
        hidden_v[here, :] = value.astype(bf16)
        copies.start(hidden_v.at[here], hidden.at[here])
        slope_v[here, :] = bend.astype(bf16)
        copies.start(slope_v.at[here], slope.at[here])
    copies.wait(rows)
    w_out_rows = dot(row_table().astype(bf16), w_out_v[...]).astype(bf16)
    decoded_v[...] = dot(w_out_rows, hidden_v[...])
    copies.start(decoded_v, decoded)
    copies.finish()


def forward(w_in, latent, w_out):
    hid, lat = w_in.shape
    pts = latent.shape[1]
    return pl.pallas_call(
        forward_kernel,
        in_specs=[hbm()] * 3,
        out_specs=[hbm()] * 3,
        out_shape=[
            pltpu.HBM((hid, pts), bf16),
            pltpu.HBM((hid, pts), bf16),
            pltpu.HBM((PAD, pts), f32),
        ],
        scratch_shapes=scratch(
            ((hid, lat), bf16), ((lat, pts), bf16), ((VARS, hid), bf16),
            ((hid, pts), bf16), ((hid, pts), bf16), ((PAD, pts), f32),
            copies=4 * len(blocks(hid)) + 3,
        ),
        compiler_params=params(16),
        name="forward",
    )(*in_hbm(w_in, latent, w_out))


def far_kernel(w_in, latent, hidden, slope, w_in_v, hidden_v, slope_v, sems):
    copies = Copies(sems)
    loads = load_weights(copies, w_in, w_in_v)
    for here, load in zip(blocks(w_in.shape[0]), loads):
        for copy in load:
            copies.wait(copy)
        value, bend = gelu(dot(w_in_v[here, :], latent[...]))
        hidden_v[here, :] = value.astype(bf16)
        copies.start(hidden_v.at[here], hidden.at[here])
        slope_v[here, :] = bend.astype(bf16)
        copies.start(slope_v.at[here], slope.at[here])
    copies.finish()


def far_forward(w_in, latent):
    hid, lat = w_in.shape
    pts = latent.shape[1]
    return pl.pallas_call(
        far_kernel,
        in_specs=[hbm(), whole()],
        out_specs=[hbm()] * 2,
        out_shape=[pltpu.HBM((hid, pts), bf16), pltpu.HBM((hid, pts), bf16)],
        scratch_shapes=scratch(
            ((hid, lat), bf16), ((hid, pts), bf16), ((hid, pts), bf16),
            copies=4 * len(blocks(hid)),
        ),
        compiler_params=params(16),
        cost_estimate=pl.CostEstimate(
            flops=2 * hid * lat * pts, bytes_accessed=4 << 20, transcendentals=hid * pts
        ),
        name="far_forward",
    )(*in_hbm(w_in), latent)


def prepare_kernel(
    owner, w_out_h, target_h, area_h, var_weight_h, w_out_t_h, target, weight, area_sum,
    w_out_v, w_out_t_v, target_v, area_v, var_weight_v, sems,
):
    copies = Copies(sems)
    inputs = [
        copies.start(w_out_h, w_out_v),
        copies.start(target_h, target_v),
        copies.start(area_h, area_v),
        copies.start(var_weight_h, var_weight_v),
    ]
    copies.wait(inputs[0])
    w_out_t_v[...] = lax.dot_general(
        w_out_v[...], row_table().astype(bf16), (((0,), (1,)), ((), ())),
        preferred_element_type=f32,
    ).astype(bf16)
    copies.start(w_out_t_v, w_out_t_h)
    for copy in inputs[1:]:
        copies.wait(copy)
    row = lax.broadcasted_iota(jnp.int32, (OWN, VARS), 0)
    held = (row < OWN - 1) & (lanes((OWN, VARS)) == owner[0] * (OWN - 1) + row)
    scale = jnp.sum(jnp.where(held, var_weight_v[...], 0.0), axis=1, keepdims=True)
    weight[...] = area_v[...] * scale
    target[...] = lax.dot_general(
        held.astype(f32), target_v[...], (((1,), (0,)), ((), ())),
        precision=lax.Precision.HIGHEST, preferred_element_type=f32,
    )
    area_sum[...] = jnp.broadcast_to(jnp.sum(area_v[...], keepdims=True), area_sum.shape)
    copies.finish()


def prepare(owner, w_out, target, area, var_weight):
    hid = w_out.shape[1]
    pts = target.shape[1]
    return pl.pallas_call(
        prepare_kernel,
        in_specs=[smem()] + [hbm()] * 4,
        out_specs=[hbm()] + [whole()] * 3,
        out_shape=[
            pltpu.HBM((hid, PAD), bf16),
            jax.ShapeDtypeStruct((OWN, pts), f32),
            jax.ShapeDtypeStruct((OWN, pts), f32),
            jax.ShapeDtypeStruct((8, PAD), f32),
        ],
        scratch_shapes=scratch(
            (w_out.shape, bf16), ((hid, PAD), bf16), (target.shape, f32),
            (area.shape, f32), (var_weight.shape, f32),
            copies=5,
        ),
        compiler_params=params(16),
        cost_estimate=pl.CostEstimate(flops=1 << 28, bytes_accessed=1 << 20, transcendentals=0),
        name="prepare",
    )(owner, *in_hbm(w_out, target, area, var_weight))


def grad_kernel(w_in, dpre, scale, grad, w_in_v, grad_v, sems):
    copies = Copies(sems)
    copies.start(w_in, w_in_v)
    copies.finish()
    factor = scale[0:1, 0:1]
    for here in blocks(w_in.shape[1]):
        value = lax.dot_general(
            w_in_v[:, here], dpre[...], (((0,), (0,)), ((), ())), preferred_element_type=f32
        )
        grad_v[here, :] = (value * factor).astype(bf16)
        copies.start(grad_v.at[here], grad.at[here])
    copies.finish()


def grad_latent(w_in, dpre, scale):
    hid, lat = w_in.shape
    pts = dpre.shape[1]
    return pl.pallas_call(
        grad_kernel,
        in_specs=[hbm(), whole(), whole()],
        out_specs=hbm(),
        out_shape=pltpu.HBM((lat, pts), bf16),
        scratch_shapes=scratch(
            ((hid, lat), bf16), ((lat, pts), bf16), copies=1 + len(blocks(lat))
        ),
        compiler_params=params(16),
        cost_estimate=pl.CostEstimate(
            flops=2 * hid * lat * pts, bytes_accessed=4 << 20, transcendentals=0
        ),
        name="grad_latent",
    )(*in_hbm(w_in), dpre, scale)


def pairs_kernel(members, cores, fields, target, weight, area_sum, dout, dout_v, sems):
    copies = Copies(sems)
    count = float(members)
    own, pts = fields.shape[1:]
    slopes = [None] * members
    total = None
    for m in range(1, members):
        for k in range(m):
            diff = fields[m] - fields[k]
            square = diff * diff + smooth_sq
            inverse = lax.rsqrt(square)
            slope = diff * inverse
            apart = square * inverse
            total = apart if total is None else total + apart
            slopes[m] = slope if slopes[m] is None else slopes[m] + slope
            slopes[k] = -slope if slopes[k] is None else slopes[k] - slope
    total = 2.0 * total + count * smooth_sq**0.5
    local = total * (-1.0 / (2.0 * count * (count - 1.0)))
    values = []
    for m in range(members):
        miss = fields[m] - target[...]
        square = miss * miss + smooth_sq
        inverse = lax.rsqrt(square)
        local = local + square * inverse * (1.0 / count)
        values.append(
            weight[...]
            * (miss * inverse * (1.0 / count) - slopes[m] * (1.0 / (count * (count - 1.0))))
        )
    loss = jnp.sum(weight[...] * local, keepdims=True)
    lane = lanes((own, pts))
    last = lax.broadcasted_iota(jnp.int32, (own, pts), 0) == own - 1
    ride = jnp.zeros((own, pts), f32)
    for k, value in enumerate((loss, area_sum[0:1, 0:1])):
        high = value.astype(bf16).astype(f32)
        ride = jnp.where(lane == 2 * k, high, jnp.where(lane == 2 * k + 1, value - high, ride))
    for m in range(members):
        value = jnp.where(last, ride, values[m]).astype(bf16)
        for c in range(cores):
            dout_v[m * cores + c] = value
    copies.start(dout_v, dout)
    copies.finish()


def pairs(fields, target, weight, area_sum, cores):
    members, own, pts = fields.shape
    shape = (members * cores, own, pts)
    return pl.pallas_call(
        functools.partial(pairs_kernel, members, cores),
        in_specs=[whole()] * 4,
        out_specs=hbm(),
        out_shape=pltpu.HBM(shape, bf16),
        scratch_shapes=scratch((shape, bf16), copies=1),
        compiler_params=params(8),
        name="pairs",
    )(fields, target, weight, area_sum)


def backward_kernel(
    core, dout, w_out_t, slope, slope_far, latent, latent_far, hidden, hidden_far,
    terms_v, dpre_v,
    w_out_t_v, slope_v, slope_far_v, latent_v, latent_far_v, hidden_v, hidden_far_v, sems,
):
    copies = Copies(sems)
    me = core[0]
    rows = terms_v.shape[1]
    hid, pts = slope.shape
    parts = blocks(hid)

    def fetch(source, target, here):
        return copies.start(source.at[here], target.at[here])

    mine = (slice(None), pl.ds(2 * me, 2))
    fetched = [copies.start(w_out_t, w_out_t_v)]
    halves = [[fetch(slope, slope_v, parts[0]), fetch(slope_far, slope_far_v, parts[0])]]
    fetched.append(copies.start(latent.at[mine], latent_v))
    fetched.append(copies.start(latent_far.at[mine], latent_far_v))
    for here in parts[1:]:
        halves.append([fetch(slope, slope_v, here), fetch(slope_far, slope_far_v, here)])
    late = [
        copies.start(hidden.at[mine], hidden_v),
        copies.start(hidden_far.at[mine], hidden_far_v),
    ]

    row = lax.broadcasted_iota(jnp.int32, (PAD, pts), 0)
    last = lax.rem(row, OWN) == OWN - 1
    seeds = []
    ride = jnp.zeros((1, pts), f32)
    for which in (me, 1 - me):
        value = dout[:, pl.ds(which, 1)].astype(f32).reshape(PAD, pts)
        ride = ride + jnp.sum(jnp.where(last, value, 0.0), axis=0, keepdims=True)
        seeds.append(jnp.where(last, 0.0, value).astype(bf16))

    for copy in fetched:
        copies.wait(copy)
    features = [
        [ref[:, k].reshape(-1, pts) for k in range(2)] for ref in (latent_v, latent_far_v)
    ]
    for here, half in zip(parts, halves):
        first = second = None
        for copy in half:
            copies.wait(copy)
        for k, ref in enumerate((slope_v, slope_far_v)):
            dh = dot(w_out_t_v[here, :], seeds[k])
            dpre = (dh * ref[here, :].astype(f32)).astype(bf16)
            if k == 0:
                dpre_v[here, :] = dpre
            swapped = jnp.concatenate(
                [
                    dpre[base + off : base + off + HALF]
                    for base in range(0, BLOCK, PAD)
                    for off in (HALF, 0)
                ],
                0,
            )
            a = dot_nt(features[k][0], dpre)
            b = dot_nt(features[k][1], swapped)
            first = a if first is None else first + a
            second = b if second is None else second + b
        low = lax.rem(lanes(first.shape), PAD) < HALF
        for xh, value in enumerate(
            (jnp.where(low, first, second), jnp.where(low, second, first))
        ):
            for xl in range(2):
                terms_v[2 * xh + xl, :, here] = value[xl * rows : (xl + 1) * rows].astype(bf16)

    for copy in late:
        copies.wait(copy)
    out = dot_nt(hidden_v[...].reshape(-1, pts), seeds[0])
    out += dot_nt(hidden_far_v[...].reshape(-1, pts), seeds[1])
    out = out.reshape(-1, 2, 16, PAD)
    left = out[:, 0].reshape(-1, PAD)
    right = out[:, 1].reshape(-1, PAD)
    lane = lanes((1, PAD))
    parts = jnp.zeros((1, PAD), f32)
    for k in range(2):
        mine = lax.div(lanes((1, pts)), 2) == k
        value = jnp.sum(jnp.where(mine, ride, 0.0), axis=1, keepdims=True)
        high = value.astype(bf16).astype(f32)
        parts = jnp.where(lane == spare(2 * k), high, parts)
        parts = jnp.where(lane == spare(2 * k + 1), value - high, parts)
    row = lax.rem(lax.broadcasted_iota(jnp.int32, left.shape, 0), 16)
    unused = lax.rem(lanes(left.shape), OWN) == OWN - 1
    left = jnp.where(unused, jnp.where(row == 0, parts, 0.0), left)
    for xh in range(2):
        for xl in range(2):
            piece = slice(xl * rows, (xl + 1) * rows)
            terms_v[2 * xh + xl, :, hid : hid + PAD] = left[piece].astype(bf16)
            terms_v[2 * xh + xl, :, hid + PAD :] = right[piece].astype(bf16)


def backward(core, dout, w_out_t, slope, slope_far, latent, latent_far, hidden, hidden_far):
    hid, pts = slope.shape
    plane = latent.shape[0]
    shape = (4, plane * 16 // 2, hid + 2 * PAD)
    half = ((plane, 2, 16, pts), bf16)
    return pl.pallas_call(
        backward_kernel,
        in_specs=[smem(), whole()] + [hbm()] * 7,
        out_specs=[whole()] * 2,
        out_shape=[
            jax.ShapeDtypeStruct(shape, bf16),
            jax.ShapeDtypeStruct((hid, pts), bf16),
        ],
        scratch_shapes=scratch(
            ((hid, PAD), bf16), ((hid, pts), bf16), ((hid, pts), bf16), half, half, half, half,
            copies=2 * len(blocks(hid)) + 5,
        ),
        compiler_params=params(24),
        name="backward",
    )(core, dout, *in_hbm(w_out_t, slope, slope_far, latent), latent_far, *in_hbm(hidden, hidden_far))


def split_again(tile):
    lane = lanes(tile.shape)
    value = tile + pltpu.roll(tile, PAD - OWN, 1)
    high = value.astype(bf16).astype(f32)
    low = pltpu.roll(value - high, OWN, 1)
    even = (lane == spare(0)) | (lane == spare(2))
    odd = (lane == spare(1)) | (lane == spare(3))
    return jnp.where(even, high, jnp.where(odd, low, tile))


def add_x_kernel(hid, got, out):
    value = got[0].astype(f32)
    for k in range(1, got.shape[0]):
        value = value + got[k].astype(f32)
    out[:, 0:hid] = value[:, 0:hid].astype(bf16)
    out[:, hid : hid + PAD] = split_again(value[:, hid : hid + PAD]).astype(bf16)
    out[:, hid + PAD :] = value[:, hid + PAD :].astype(bf16)


def add_x(got, hid):
    return pl.pallas_call(
        functools.partial(add_x_kernel, hid),
        in_specs=[whole()],
        out_specs=whole(),
        out_shape=jax.ShapeDtypeStruct(got.shape[1:], bf16),
        compiler_params=params(8),
        name="add_x",
    )(got)


def pick(head, k):
    lane = lanes(head.shape)
    mine = (lane == spare(2 * k)) | (lane == spare(2 * k + 1))
    return jnp.sum(jnp.where(mine, head, 0.0), axis=1, keepdims=True)


def add_z_kernel(hid, copied, points_all, got, out, scale, out_v, sems):
    copies = Copies(sems)
    value = got[0].astype(f32)
    for k in range(1, got.shape[0]):
        value = value + got[k].astype(f32)
    left = value[:, hid : hid + PAD]
    keep = split_again(left).astype(bf16)
    right = value[:, hid + PAD :].astype(bf16)
    for y in range(out.shape[0]):
        out_v[y, :, 0:PAD] = value[:, y * PAD : (y + 1) * PAD].astype(bf16)
        out_v[y, :, PAD : 2 * PAD] = keep
        out_v[y, :, 2 * PAD :] = right
    copies.start(out_v, out)
    weight_total = pick(left[0:1, :], 1) * (1.0 / copied)
    scale[...] = jnp.broadcast_to(points_all / (weight_total * VARS), scale.shape)
    copies.finish()


def add_z(got, hid, copied, points_all):
    shape = (hid // PAD, got.shape[1], 3 * PAD)
    return pl.pallas_call(
        functools.partial(add_z_kernel, hid, copied, points_all),
        in_specs=[whole()],
        out_specs=[hbm(), whole()],
        out_shape=[pltpu.HBM(shape, bf16), jax.ShapeDtypeStruct((8, PAD), f32)],
        scratch_shapes=scratch((shape, bf16), copies=1),
        compiler_params=params(4),
        name="add_z",
    )(got)


def finish_kernel(copied, points_all, count, turn, got, loss, grad_in, grad_out):
    value = got[0].astype(f32)
    for k in range(1, got.shape[0]):
        value = value + got[k].astype(f32)
    left = value[:, PAD : 2 * PAD]
    head = left[0:1, :]
    weight_total = pick(head, 1) * (1.0 / (copied * count))
    scale = 1.0 / (weight_total * VARS)
    loss[...] = pick(head, 0) * (1.0 / copied) * scale
    ratio = scale * (points_all / (points_all * count) ** 0.5)
    tile = value[:, 0:PAD] * ratio
    other = pltpu.roll(tile, HALF, 1)
    even = turn[0] == 0
    grad_in[0:16, :] = jnp.where(even, tile, other)[:, 0:HALF]
    grad_in[16:32, :] = jnp.where(even, other, tile)[:, 0:HALF]
    both = jnp.concatenate([left, value[:, 2 * PAD :]], 0) * ratio
    grad_out[...] = lax.dot_general(
        both, row_table().astype(f32), (((1,), (0,)), ((), ())),
        precision=lax.Precision.HIGHEST, preferred_element_type=f32,
    )


def finish(turn, got, copied, points_all, count):
    return pl.pallas_call(
        functools.partial(finish_kernel, copied, points_all, count),
        in_specs=[smem(), whole()],
        out_specs=[whole()] * 3,
        out_shape=[
            jax.ShapeDtypeStruct((1, 1), f32),
            jax.ShapeDtypeStruct((32, HALF), f32),
            jax.ShapeDtypeStruct((32, VARS), f32),
        ],
        compiler_params=params(4),
        name="finish",
    )(turn, got)


def per_device(latent, w_in, w_out, target, area, var_weight):
    n_ens = lax.axis_size(ENS)
    n_plane = lax.axis_size(PLANE)
    n_core = lax.axis_size("c")
    n_z = lax.axis_size("z")
    pts = area.shape[0]
    hid, _ = w_in.shape
    own = PAD // n_ens
    assert own == OWN
    me = lax.axis_index(ENS)
    core = lax.axis_index("c")
    swap = [(0, 1), (1, 0)]
    features = latent[0]

    count = float(n_ens)
    points_all = float(n_plane * n_core * pts)
    hidden, slope, decoded = forward(w_in, features, w_out)

    fields = exchange(decoded.reshape(n_ens, own, pts), ENS)
    late = lax.optimization_barrier((features, w_out, decoded))
    far = lax.ppermute(late[0], "c", swap)
    w_out_t, target_own, weight_own, area_sum = prepare(
        me.astype(jnp.int32)[None], late[1], target, area[None, :], var_weight[None, :]
    )
    dout = pairs(fields, target_own, weight_own, area_sum, n_core)

    dout_got = exchange(dout, ENS + ("c",))
    far, _ = lax.optimization_barrier((far, dout))
    hidden_far, slope_far = far_forward(w_in, far)

    groups = lambda value: value.reshape(n_plane, 2 * n_core, 16, pts)
    terms, dpre = backward(
        core.astype(jnp.int32)[None],
        dout_got.reshape(n_ens, n_core, own, pts),
        w_out_t, slope, slope_far,
        groups(features), groups(far), groups(hidden), groups(hidden_far),
    )

    got = exchange(terms, CHIP_X)
    got = exchange(add_x(got, hid).reshape(n_z, 16, hid + 2 * PAD), "z")
    got, scale = add_z(got, hid, count * lax.axis_size("xh"), points_all)
    got = exchange(got, "y")
    grad_lat = grad_latent(w_in, dpre, scale)
    loss, part_in, part_out = finish(
        lax.axis_index("xh").astype(jnp.int32)[None], got, count, points_all, count
    )
    return loss[0, 0], grad_lat[None], part_in.T, part_out.T


def solution(mesh):
    ens, grid_all = mesh.devices.shape
    split = (ens // 2, 2, 2, grid_all // 4, 2)
    fine = Mesh(mesh.devices.reshape(split), ENS + PLANE + ("c",))
    grid = PLANE + ("c",)
    in_specs = (P(ENS, None, grid), P(), P(), P(None, grid), P(grid), P())
    out_specs = (P(), P(ENS, None, grid), P(ENS, grid), P(None, grid))
    return jax.shard_map(
        per_device, mesh=fine, in_specs=in_specs, out_specs=out_specs, check_vma=False
    )
```

```python
import functools

import jax
import jax.numpy as jnp
from jax import lax
from jax.experimental import pallas as pl
from jax.experimental.pallas import tpu as pltpu
from jax.sharding import Mesh, PartitionSpec as P

VARS = 99
PAD = 128
HALF = PAD // 2
OWN = 8
ENS = ("y", "xh")
PLANE = ("xl", "z")
CHIP_X = ("xh", "xl")
BLOCK = 256

smooth_sq = 0.01
gelu_c = 0.7978845608
gelu_k = 0.044715
f32 = jnp.float32
bf16 = jnp.bfloat16
NT = (((1,), (1,)), ((), ()))


def gelu(value):
    square = value * value
    share = 0.5 + 0.5 * jnp.tanh(value * (gelu_c + gelu_c * gelu_k * square))
    bend = value * (2.0 * gelu_c + 6.0 * gelu_c * gelu_k * square)
    return value * share, share + share * ((1.0 - share) * bend)


def exchange(pieces, axes):
    return lax.all_to_all(pieces, axes, split_axis=0, concat_axis=0, tiled=True)


def dot(a, b):
    return jnp.dot(a, b, preferred_element_type=f32)


def dot_nt(a, b):
    return lax.dot_general(a, b, NT, preferred_element_type=f32)


def whole():
    return pl.BlockSpec(memory_space=pltpu.VMEM)


def smem():
    return pl.BlockSpec(memory_space=pltpu.SMEM)


def hbm():
    return pl.BlockSpec(memory_space=pltpu.HBM)


def in_hbm(*arrays):
    return [pltpu.with_memory_space_constraint(array, pltpu.HBM) for array in arrays]


def params(mib):
    return pltpu.CompilerParams(vmem_limit_bytes=mib << 20)


class Copies:
    def __init__(self, sems):
        self.sems = sems
        self.used = 0
        self.open = []

    def start(self, source, target):
        copy = pltpu.make_async_copy(source, target, self.sems.at[self.used])
        self.used += 1
        copy.start()
        self.open.append(copy)
        return copy

    def wait(self, copy):
        copy.wait()
        self.open = [other for other in self.open if other is not copy]

    def finish(self):
        for copy in self.open:
            self.wait(copy)


def scratch(*shapes, copies):
    return [pltpu.VMEM(shape, kind) for shape, kind in shapes] + [
        pltpu.SemaphoreType.DMA((copies,))
    ]


def blocks(size):
    return [slice(at, at + BLOCK) for at in range(0, size, BLOCK)]


def spare(k):
    return OWN * (k + 1) - 1


def row_table():
    row = lax.broadcasted_iota(jnp.int32, (PAD, VARS), 0)
    held = lax.rem(row, OWN) < OWN - 1
    variable = lax.div(row, OWN) * (OWN - 1) + lax.rem(row, OWN)
    return held & (variable == lanes((PAD, VARS)))


def lanes(shape):
    return lax.broadcasted_iota(jnp.int32, shape, len(shape) - 1)


def load_weights(copies, w_in, w_in_v):
    loads = []
    for here in blocks(w_in.shape[0]):
        middle = (here.start + here.stop) // 2
        loads.append(
            [
                copies.start(w_in.at[part], w_in_v.at[part])
                for part in (slice(here.start, middle), slice(middle, here.stop))
            ]
        )
    return loads


def forward_kernel(
    w_in, latent, w_out, hidden, slope, decoded, w_in_v, latent_v, w_out_v, decoded_v, sems
):
    copies = Copies(sems)
    first = copies.start(latent, latent_v)
    loads = load_weights(copies, w_in, w_in_v)
    rows = copies.start(w_out, w_out_v)
    copies.wait(first)
    total = None
    for here, load in zip(blocks(w_in.shape[0]), loads):
        for copy in load:
            copies.wait(copy)
        value, bend = gelu(dot(w_in_v[here, :], latent_v[...]))
        value = value.astype(bf16)
        hidden[here, :] = value
        slope[here, :] = bend.astype(bf16)
        if total is None:
            copies.wait(rows)
            w_out_rows = dot(row_table().astype(bf16), w_out_v[...]).astype(bf16)
        part = dot(w_out_rows[:, here], value)
        total = part if total is None else total + part
    decoded_v[...] = total
    copies.start(decoded_v, decoded)
    copies.finish()


def forward(w_in, latent, w_out):
    hid, lat = w_in.shape
    pts = latent.shape[1]
    return pl.pallas_call(
        forward_kernel,
        in_specs=[hbm()] * 3,
        out_specs=[whole(), whole(), hbm()],
        out_shape=[
            jax.ShapeDtypeStruct((hid, pts), bf16),
            jax.ShapeDtypeStruct((hid, pts), bf16),
            pltpu.HBM((PAD, pts), f32),
        ],
        scratch_shapes=scratch(
            ((hid, lat), bf16), ((lat, pts), bf16), ((VARS, hid), bf16), ((PAD, pts), f32),
            copies=2 * len(blocks(hid)) + 3,
        ),
        compiler_params=params(16),
        name="forward",
    )(*in_hbm(w_in, latent, w_out))


def far_kernel(w_in, latent, hidden, slope, w_in_v, hidden_v, slope_v, sems):
    copies = Copies(sems)
    loads = load_weights(copies, w_in, w_in_v)
    for here, load in zip(blocks(w_in.shape[0]), loads):
        for copy in load:
            copies.wait(copy)
        value, bend = gelu(dot(w_in_v[here, :], latent[...]))
        hidden_v[here, :] = value.astype(bf16)
        copies.start(hidden_v.at[here], hidden.at[here])
        slope_v[here, :] = bend.astype(bf16)
        copies.start(slope_v.at[here], slope.at[here])
    copies.finish()


def far_forward(w_in, latent):
    hid, lat = w_in.shape
    pts = latent.shape[1]
    return pl.pallas_call(
        far_kernel,
        in_specs=[hbm(), whole()],
        out_specs=[hbm()] * 2,
        out_shape=[pltpu.HBM((hid, pts), bf16), pltpu.HBM((hid, pts), bf16)],
        scratch_shapes=scratch(
            ((hid, lat), bf16), ((hid, pts), bf16), ((hid, pts), bf16),
            copies=4 * len(blocks(hid)),
        ),
        compiler_params=params(16),
        cost_estimate=pl.CostEstimate(
            flops=2 * hid * lat * pts, bytes_accessed=4 << 20, transcendentals=hid * pts
        ),
        name="far_forward",
    )(*in_hbm(w_in), latent)


def prepare_kernel(
    owner, w_out_h, target_h, area_h, var_weight_h, w_out_t, target, weight, area_sum,
    w_out_v, target_v, area_v, var_weight_v, sems,
):
    copies = Copies(sems)
    inputs = [
        copies.start(w_out_h, w_out_v),
        copies.start(target_h, target_v),
        copies.start(area_h, area_v),
        copies.start(var_weight_h, var_weight_v),
    ]
    copies.wait(inputs[0])
    w_out_t[...] = lax.dot_general(
        w_out_v[...], row_table().astype(bf16), (((0,), (1,)), ((), ())),
        preferred_element_type=f32,
    ).astype(bf16)
    for copy in inputs[1:]:
        copies.wait(copy)
    row = lax.broadcasted_iota(jnp.int32, (OWN, VARS), 0)
    held = (row < OWN - 1) & (lanes((OWN, VARS)) == owner[0] * (OWN - 1) + row)
    scale = jnp.sum(jnp.where(held, var_weight_v[...], 0.0), axis=1, keepdims=True)
    weight[...] = area_v[...] * scale
    target[...] = lax.dot_general(
        held.astype(f32), target_v[...], (((1,), (0,)), ((), ())),
        precision=lax.Precision.HIGHEST, preferred_element_type=f32,
    )
    area_sum[...] = jnp.broadcast_to(jnp.sum(area_v[...], keepdims=True), area_sum.shape)
    copies.finish()


def prepare(owner, w_out, target, area, var_weight):
    hid = w_out.shape[1]
    pts = target.shape[1]
    return pl.pallas_call(
        prepare_kernel,
        in_specs=[smem()] + [hbm()] * 4,
        out_specs=[whole()] * 4,
        out_shape=[
            jax.ShapeDtypeStruct((hid, PAD), bf16),
            jax.ShapeDtypeStruct((OWN, pts), f32),
            jax.ShapeDtypeStruct((OWN, pts), f32),
            jax.ShapeDtypeStruct((8, PAD), f32),
        ],
        scratch_shapes=scratch(
            (w_out.shape, bf16), (target.shape, f32), (area.shape, f32), (var_weight.shape, f32),
            copies=4,
        ),
        compiler_params=params(16),
        cost_estimate=pl.CostEstimate(flops=1 << 28, bytes_accessed=1 << 20, transcendentals=0),
        name="prepare",
    )(owner, *in_hbm(w_out, target, area, var_weight))


def grad_kernel(w_in, dpre, scale, grad, w_in_v, grad_v, sems):
    copies = Copies(sems)
    copies.start(w_in, w_in_v)
    copies.finish()
    factor = scale[0:1, 0:1]
    for here in blocks(w_in.shape[1]):
        value = lax.dot_general(
            w_in_v[:, here], dpre[...], (((0,), (0,)), ((), ())), preferred_element_type=f32
        )
        grad_v[here, :] = (value * factor).astype(bf16)
        copies.start(grad_v.at[here], grad.at[here])
    copies.finish()


def grad_latent(w_in, dpre, scale):
    hid, lat = w_in.shape
    pts = dpre.shape[1]
    return pl.pallas_call(
        grad_kernel,
        in_specs=[hbm(), whole(), whole()],
        out_specs=hbm(),
        out_shape=pltpu.HBM((lat, pts), bf16),
        scratch_shapes=scratch(
            ((hid, lat), bf16), ((lat, pts), bf16), copies=1 + len(blocks(lat))
        ),
        compiler_params=params(16),
        cost_estimate=pl.CostEstimate(
            flops=2 * hid * lat * pts, bytes_accessed=4 << 20, transcendentals=0
        ),
        name="grad_latent",
    )(*in_hbm(w_in), dpre, scale)


def pairs_kernel(members, cores, fields, target, weight, area_sum, dout, dout_v, sems):
    copies = Copies(sems)
    count = float(members)
    own, pts = fields.shape[1:]
    slopes = [None] * members
    total = None
    for m in range(1, members):
        for k in range(m):
            diff = fields[m] - fields[k]
            square = diff * diff + smooth_sq
            inverse = lax.rsqrt(square)
            slope = diff * inverse
            apart = square * inverse
            total = apart if total is None else total + apart
            slopes[m] = slope if slopes[m] is None else slopes[m] + slope
            slopes[k] = -slope if slopes[k] is None else slopes[k] - slope
    total = 2.0 * total + count * smooth_sq**0.5
    local = total * (-1.0 / (2.0 * count * (count - 1.0)))
    values = []
    for m in range(members):
        miss = fields[m] - target[...]
        square = miss * miss + smooth_sq
        inverse = lax.rsqrt(square)
        local = local + square * inverse * (1.0 / count)
        values.append(
            weight[...]
            * (miss * inverse * (1.0 / count) - slopes[m] * (1.0 / (count * (count - 1.0))))
        )
    loss = jnp.sum(weight[...] * local, keepdims=True)
    lane = lanes((own, pts))
    last = lax.broadcasted_iota(jnp.int32, (own, pts), 0) == own - 1
    ride = jnp.zeros((own, pts), f32)
    for k, value in enumerate((loss, area_sum[0:1, 0:1])):
        high = value.astype(bf16).astype(f32)
        ride = jnp.where(lane == 2 * k, high, jnp.where(lane == 2 * k + 1, value - high, ride))
    for m in range(members):
        value = jnp.where(last, ride, values[m]).astype(bf16)
        for c in range(cores):
            dout_v[m * cores + c] = value
    copies.start(dout_v, dout)
    copies.finish()


def pairs(fields, target, weight, area_sum, cores):
    members, own, pts = fields.shape
    shape = (members * cores, own, pts)
    return pl.pallas_call(
        functools.partial(pairs_kernel, members, cores),
        in_specs=[whole()] * 4,
        out_specs=hbm(),
        out_shape=pltpu.HBM(shape, bf16),
        scratch_shapes=scratch((shape, bf16), copies=1),
        compiler_params=params(8),
        name="pairs",
    )(fields, target, weight, area_sum)


def backward_kernel(
    place, dout, w_out_t, slope_v, slope_far, latent, latent_far, hidden, hidden_far,
    own_out, right_out, across_out, left_out, dpre_v,
    terms_v, slope_far_v, latent_v, hidden_far_v, sems,
):
    copies = Copies(sems)
    me = place[0]
    rows = terms_v.shape[1]
    hid, pts = slope_v.shape
    parts = blocks(hid)

    def fetch(source, target, here):
        return copies.start(source.at[here], target.at[here])

    mine = (slice(None), pl.ds(2 * me, 2))
    near = copies.start(latent.at[mine], latent_v)
    halves = [fetch(slope_far, slope_far_v, parts[0])]
    for here in parts[1:]:
        halves.append(fetch(slope_far, slope_far_v, here))
    late = copies.start(hidden_far.at[mine], hidden_far_v)

    row = lax.broadcasted_iota(jnp.int32, (PAD, pts), 0)
    last = lax.rem(row, OWN) == OWN - 1
    seeds = []
    ride = jnp.zeros((1, pts), f32)
    for which in (me, 1 - me):
        value = dout[:, pl.ds(which, 1)].astype(f32).reshape(PAD, pts)
        ride = ride + jnp.sum(jnp.where(last, value, 0.0), axis=0, keepdims=True)
        seeds.append(jnp.where(last, 0.0, value).astype(bf16))

    copies.wait(near)
    features = [
        [latent_v[:, k].reshape(-1, pts) for k in range(2)],
        [latent_far[:, pl.ds(2 * me + k, 1)].reshape(-1, pts) for k in range(2)],
    ]
    for here, half in zip(parts, halves):
        first = second = None
        copies.wait(half)
        for k, ref in enumerate((slope_v, slope_far_v)):
            dh = dot(w_out_t[here, :], seeds[k])
            dpre = (dh * ref[here, :].astype(f32)).astype(bf16)
            if k == 0:
                dpre_v[here, :] = dpre
            swapped = jnp.concatenate(
                [
                    dpre[base + off : base + off + HALF]
                    for base in range(0, BLOCK, PAD)
                    for off in (HALF, 0)
                ],
                0,
            )
            a = dot_nt(features[k][0], dpre)
            b = dot_nt(features[k][1], swapped)
            first = a if first is None else first + a
            second = b if second is None else second + b
        low = lax.rem(lanes(first.shape), PAD) < HALF
        for xh, value in enumerate(
            (jnp.where(low, first, second), jnp.where(low, second, first))
        ):
            for xl in range(2):
                terms_v[2 * xh + xl, :, here] = value[xl * rows : (xl + 1) * rows].astype(bf16)

    copies.wait(late)
    out = dot_nt(hidden[:, pl.ds(2 * me, 2)].reshape(-1, pts), seeds[0])
    out += dot_nt(hidden_far_v[...].reshape(-1, pts), seeds[1])
    out = out.reshape(-1, 2, 16, PAD)
    left = out[:, 0].reshape(-1, PAD)
    right = out[:, 1].reshape(-1, PAD)
    lane = lanes((1, PAD))
    parts = jnp.zeros((1, PAD), f32)
    for k in range(2):
        mine = lax.div(lanes((1, pts)), 2) == k
        value = jnp.sum(jnp.where(mine, ride, 0.0), axis=1, keepdims=True)
        high = value.astype(bf16).astype(f32)
        parts = jnp.where(lane == spare(2 * k), high, parts)
        parts = jnp.where(lane == spare(2 * k + 1), value - high, parts)
    row = lax.rem(lax.broadcasted_iota(jnp.int32, left.shape, 0), 16)
    unused = lax.rem(lanes(left.shape), OWN) == OWN - 1
    left = jnp.where(unused, jnp.where(row == 0, parts, 0.0), left)
    for xh in range(2):
        for xl in range(2):
            piece = slice(xl * rows, (xl + 1) * rows)
            terms_v[2 * xh + xl, :, hid : hid + PAD] = left[piece].astype(bf16)
            terms_v[2 * xh + xl, :, hid + PAD :] = right[piece].astype(bf16)
    for k, out in enumerate((own_out, right_out, across_out, left_out)):
        out[...] = terms_v[lax.rem(place[1] + k, 4)]


def backward(place, dout, w_out_t, slope, slope_far, latent, latent_far, hidden, hidden_far):
    hid, pts = slope.shape
    plane = latent.shape[0]
    shape = (plane * 16 // 2, hid + 2 * PAD)
    half = ((plane, 2, 16, pts), bf16)
    return pl.pallas_call(
        backward_kernel,
        in_specs=[smem()] + [whole()] * 3 + [hbm()] * 2 + [whole()] * 2 + [hbm()],
        out_specs=[whole()] * 5,
        out_shape=[jax.ShapeDtypeStruct(shape, bf16)] * 4
        + [jax.ShapeDtypeStruct((hid, pts), bf16)],
        scratch_shapes=scratch(
            ((4, *shape), bf16), ((hid, pts), bf16), half, half,
            copies=len(blocks(hid)) + 2,
        ),
        compiler_params=params(24),
        name="backward",
    )(
        place, dout, w_out_t, slope, *in_hbm(slope_far, latent), latent_far, hidden,
        *in_hbm(hidden_far),
    )


def split_again(tile):
    lane = lanes(tile.shape)
    value = tile + pltpu.roll(tile, PAD - OWN, 1)
    high = value.astype(bf16).astype(f32)
    low = pltpu.roll(value - high, OWN, 1)
    even = (lane == spare(0)) | (lane == spare(2))
    odd = (lane == spare(1)) | (lane == spare(3))
    return jnp.where(even, high, jnp.where(odd, low, tile))


def add_x_kernel(hid, own, right, across, left, out):
    value = own[...].astype(f32)
    for ref in (right, across, left):
        value = value + ref[...].astype(f32)
    out[:, 0:hid] = value[:, 0:hid].astype(bf16)
    out[:, hid : hid + PAD] = split_again(value[:, hid : hid + PAD]).astype(bf16)
    out[:, hid + PAD :] = value[:, hid + PAD :].astype(bf16)


def add_x(hid, *parts):
    return pl.pallas_call(
        functools.partial(add_x_kernel, hid),
        in_specs=[whole()] * 4,
        out_specs=whole(),
        out_shape=jax.ShapeDtypeStruct(parts[0].shape, bf16),
        compiler_params=params(8),
        name="add_x",
    )(*parts)


def pick(head, k):
    lane = lanes(head.shape)
    mine = (lane == spare(2 * k)) | (lane == spare(2 * k + 1))
    return jnp.sum(jnp.where(mine, head, 0.0), axis=1, keepdims=True)


def add_z_kernel(hid, copied, points_all, got, out, scale, out_v, sems):
    copies = Copies(sems)
    value = got[0].astype(f32)
    for k in range(1, got.shape[0]):
        value = value + got[k].astype(f32)
    left = value[:, hid : hid + PAD]
    keep = split_again(left).astype(bf16)
    right = value[:, hid + PAD :].astype(bf16)
    for y in range(out.shape[0]):
        out_v[y, :, 0:PAD] = value[:, y * PAD : (y + 1) * PAD].astype(bf16)
        out_v[y, :, PAD : 2 * PAD] = keep
        out_v[y, :, 2 * PAD :] = right
    copies.start(out_v, out)
    weight_total = pick(left[0:1, :], 1) * (1.0 / copied)
    scale[...] = jnp.broadcast_to(points_all / (weight_total * VARS), scale.shape)
    copies.finish()


def add_z(got, hid, copied, points_all):
    shape = (hid // PAD, got.shape[1], 3 * PAD)
    return pl.pallas_call(
        functools.partial(add_z_kernel, hid, copied, points_all),
        in_specs=[whole()],
        out_specs=[hbm(), whole()],
        out_shape=[pltpu.HBM(shape, bf16), jax.ShapeDtypeStruct((8, PAD), f32)],
        scratch_shapes=scratch((shape, bf16), copies=1),
        compiler_params=params(4),
        name="add_z",
    )(got)


def finish_kernel(copied, points_all, count, turn, got, loss, grad_in, grad_out):
    value = got[0].astype(f32)
    for k in range(1, got.shape[0]):
        value = value + got[k].astype(f32)
    left = value[:, PAD : 2 * PAD]
    head = left[0:1, :]
    weight_total = pick(head, 1) * (1.0 / (copied * count))
    scale = 1.0 / (weight_total * VARS)
    loss[...] = pick(head, 0) * (1.0 / copied) * scale
    ratio = scale * (points_all / (points_all * count) ** 0.5)
    tile = value[:, 0:PAD] * ratio
    other = pltpu.roll(tile, HALF, 1)
    even = turn[0] == 0
    grad_in[0:16, :] = jnp.where(even, tile, other)[:, 0:HALF]
    grad_in[16:32, :] = jnp.where(even, other, tile)[:, 0:HALF]
    both = jnp.concatenate([left, value[:, 2 * PAD :]], 0) * ratio
    grad_out[...] = lax.dot_general(
        both, row_table().astype(f32), (((1,), (0,)), ((), ())),
        precision=lax.Precision.HIGHEST, preferred_element_type=f32,
    )


def finish(turn, got, copied, points_all, count):
    return pl.pallas_call(
        functools.partial(finish_kernel, copied, points_all, count),
        in_specs=[smem(), whole()],
        out_specs=[whole()] * 3,
        out_shape=[
            jax.ShapeDtypeStruct((1, 1), f32),
            jax.ShapeDtypeStruct((32, HALF), f32),
            jax.ShapeDtypeStruct((32, VARS), f32),
        ],
        compiler_params=params(4),
        name="finish",
    )(turn, got)


def per_device(latent, w_in, w_out, target, area, var_weight):
    n_ens = lax.axis_size(ENS)
    n_plane = lax.axis_size(PLANE)
    n_core = lax.axis_size("c")
    n_z = lax.axis_size("z")
    pts = area.shape[0]
    hid, _ = w_in.shape
    own = PAD // n_ens
    assert own == OWN
    me = lax.axis_index(ENS)
    core = lax.axis_index("c")
    swap = [(0, 1), (1, 0)]
    features = latent[0]

    count = float(n_ens)
    points_all = float(n_plane * n_core * pts)
    hidden, slope, decoded = forward(w_in, features, w_out)

    fields = exchange(decoded.reshape(n_ens, own, pts), ENS)
    late = lax.optimization_barrier((features, w_out, decoded))
    far = lax.ppermute(late[0], "c", swap)
    w_out_t, target_own, weight_own, area_sum = prepare(
        me.astype(jnp.int32)[None], late[1], target, area[None, :], var_weight[None, :]
    )
    dout = pairs(fields, target_own, weight_own, area_sum, n_core)

    dout_got = exchange(dout, ENS + ("c",))
    far, _ = lax.optimization_barrier((far, dout))
    hidden_far, slope_far = far_forward(w_in, far)

    groups = lambda value: value.reshape(n_plane, 2 * n_core, 16, pts)
    own_part, right, across, left, dpre = backward(
        jnp.stack([core, lax.axis_index(CHIP_X)]).astype(jnp.int32),
        dout_got.reshape(n_ens, n_core, own, pts),
        w_out_t, slope, slope_far,
        groups(features), groups(far), groups(hidden), groups(hidden_far),
    )

    n_x = lax.axis_size(CHIP_X)
    sent = []
    for part, far_by in ((across, 2), (right, 1), (left, n_x - 1)):
        sent.append(
            lax.ppermute(part, CHIP_X, [(k, (k + far_by) % n_x) for k in range(n_x)])
        )
    got = exchange(add_x(hid, own_part, *sent).reshape(n_z, 16, hid + 2 * PAD), "z")
    got, scale = add_z(got, hid, count * lax.axis_size("xh"), points_all)
    got = exchange(got, "y")
    grad_lat = grad_latent(w_in, dpre, scale)
    loss, part_in, part_out = finish(
        lax.axis_index("xh").astype(jnp.int32)[None], got, count, points_all, count
    )
    return loss[0, 0], grad_lat[None], part_in.T, part_out.T


def solution(mesh):
    ens, grid_all = mesh.devices.shape
    split = (ens // 2, 2, 2, grid_all // 4, 2)
    fine = Mesh(mesh.devices.reshape(split), ENS + PLANE + ("c",))
    grid = PLANE + ("c",)
    in_specs = (P(ENS, None, grid), P(), P(), P(None, grid), P(grid), P())
    out_specs = (P(), P(ENS, None, grid), P(ENS, grid), P(None, grid))
    return jax.shard_map(
        per_device, mesh=fine, in_specs=in_specs, out_specs=out_specs, check_vma=False
    )
```

```python
import functools

import jax
import jax.numpy as jnp
from jax import lax
from jax.experimental import pallas as pl
from jax.experimental.pallas import tpu as pltpu
from jax.sharding import Mesh, PartitionSpec as P

VARS = 99
PAD = 128
HALF = PAD // 2
OWN = 8
ENS = ("y", "xh")
PLANE = ("xl", "z")
CHIP_X = ("xh", "xl")
BLOCK = 1024

smooth_sq = 0.01
gelu_c = 0.7978845608
gelu_k = 0.044715
f32 = jnp.float32
bf16 = jnp.bfloat16
NT = (((1,), (1,)), ((), ()))


def gelu(value):
    square = value * value
    share = 0.5 + 0.5 * jnp.tanh(value * (gelu_c + gelu_c * gelu_k * square))
    bend = value * (2.0 * gelu_c + 6.0 * gelu_c * gelu_k * square)
    return value * share, share + share * ((1.0 - share) * bend)


def exchange(pieces, axes):
    return lax.all_to_all(pieces, axes, split_axis=0, concat_axis=0, tiled=True)


def dot(a, b):
    return jnp.dot(a, b, preferred_element_type=f32)


def dot_nt(a, b):
    return lax.dot_general(a, b, NT, preferred_element_type=f32)


def whole():
    return pl.BlockSpec(memory_space=pltpu.VMEM)


def smem():
    return pl.BlockSpec(memory_space=pltpu.SMEM)


def hbm():
    return pl.BlockSpec(memory_space=pltpu.HBM)


def in_hbm(*arrays):
    return [pltpu.with_memory_space_constraint(array, pltpu.HBM) for array in arrays]


def params(mib):
    return pltpu.CompilerParams(vmem_limit_bytes=mib << 20)


class Copies:
    def __init__(self, sems):
        self.sems = sems
        self.used = 0
        self.open = []

    def start(self, source, target):
        copy = pltpu.make_async_copy(source, target, self.sems.at[self.used])
        self.used += 1
        copy.start()
        self.open.append(copy)
        return copy

    def wait(self, copy):
        copy.wait()
        self.open = [other for other in self.open if other is not copy]

    def finish(self):
        for copy in self.open:
            self.wait(copy)


def scratch(*shapes, copies):
    return [pltpu.VMEM(shape, kind) for shape, kind in shapes] + [
        pltpu.SemaphoreType.DMA((copies,))
    ]


def blocks(size):
    step = min(size, BLOCK)
    return [slice(at, at + step) for at in range(0, size, step)]


def spare(k):
    return OWN * (k + 1) - 1


def row_table():
    row = lax.broadcasted_iota(jnp.int32, (PAD, VARS), 0)
    held = lax.rem(row, OWN) < OWN - 1
    variable = lax.div(row, OWN) * (OWN - 1) + lax.rem(row, OWN)
    return held & (variable == lanes((PAD, VARS)))


def lanes(shape):
    return lax.broadcasted_iota(jnp.int32, shape, len(shape) - 1)


class Stream:
    def __init__(self, copies, source, target):
        self.copies = copies
        self.started = []
        for here in blocks(source.shape[0]):
            middle = (here.start + here.stop) // 2
            self.started.append(
                [
                    copies.start(source.at[part], target.at[part])
                    for part in (slice(here.start, middle), slice(middle, here.stop))
                ]
            )

    def wait(self, k):
        for copy in self.started[k]:
            self.copies.wait(copy)


def products(weights, w_in_v, latent):
    parts = blocks(w_in_v.shape[0])
    ahead = None
    for k, here in enumerate(parts):
        if ahead is None:
            weights.wait(k)
            ahead = dot(w_in_v[here, :], latent[...])
        now = ahead
        if k + 1 < len(parts):
            weights.wait(k + 1)
            ahead = dot(w_in_v[parts[k + 1], :], latent[...])
        yield here, now


def forward_kernel(
    w_in, latent, w_out, hidden, slope, decoded, w_in_v, latent_v, w_out_v, decoded_v, sems
):
    copies = Copies(sems)
    first = copies.start(latent, latent_v)
    rows = copies.start(w_out, w_out_v)
    weights = Stream(copies, w_in, w_in_v)
    copies.wait(first)
    copies.wait(rows)
    w_out_rows = dot(row_table().astype(bf16), w_out_v[...]).astype(bf16)
    total = None
    for here, product in products(weights, w_in_v, latent_v):
        value, bend = gelu(product)
        value = value.astype(bf16)
        hidden[here, :] = value
        slope[here, :] = bend.astype(bf16)
        part = dot(w_out_rows[:, here], value)
        total = part if total is None else total + part
    decoded_v[...] = total
    copies.start(decoded_v, decoded)
    copies.finish()


def forward(w_in, latent, w_out):
    hid, lat = w_in.shape
    pts = latent.shape[1]
    return pl.pallas_call(
        forward_kernel,
        in_specs=[hbm()] * 3,
        out_specs=[whole(), whole(), hbm()],
        out_shape=[
            jax.ShapeDtypeStruct((hid, pts), bf16),
            jax.ShapeDtypeStruct((hid, pts), bf16),
            pltpu.HBM((PAD, pts), f32),
        ],
        scratch_shapes=scratch(
            ((hid, lat), bf16), ((lat, pts), bf16), ((VARS, hid), bf16), ((PAD, pts), f32),
            copies=4 * len(blocks(hid)) + 3,
        ),
        compiler_params=params(16),
        name="forward",
    )(*in_hbm(w_in, latent, w_out))


def far_kernel(w_in, latent, hidden, slope, w_in_v, hidden_v, slope_v, sems):
    copies = Copies(sems)
    weights = Stream(copies, w_in, w_in_v)
    for here, product in products(weights, w_in_v, latent):
        value, bend = gelu(product)
        hidden_v[here, :] = value.astype(bf16)
        copies.start(hidden_v.at[here], hidden.at[here])
        slope_v[here, :] = bend.astype(bf16)
        copies.start(slope_v.at[here], slope.at[here])
    copies.finish()


def far_forward(w_in, latent):
    hid, lat = w_in.shape
    pts = latent.shape[1]
    return pl.pallas_call(
        far_kernel,
        in_specs=[hbm(), whole()],
        out_specs=[hbm()] * 2,
        out_shape=[pltpu.HBM((hid, pts), bf16), pltpu.HBM((hid, pts), bf16)],
        scratch_shapes=scratch(
            ((hid, lat), bf16), ((hid, pts), bf16), ((hid, pts), bf16),
            copies=6 * len(blocks(hid)),
        ),
        compiler_params=params(16),
        cost_estimate=pl.CostEstimate(
            flops=2 * hid * lat * pts, bytes_accessed=4 << 20, transcendentals=hid * pts
        ),
        name="far_forward",
    )(*in_hbm(w_in), latent)


def prepare_kernel(
    owner, w_out_h, target_h, area_h, var_weight_h, w_out_t, target, weight, area_sum,
    w_out_v, target_v, area_v, var_weight_v, sems,
):
    copies = Copies(sems)
    inputs = [
        copies.start(w_out_h, w_out_v),
        copies.start(target_h, target_v),
        copies.start(area_h, area_v),
        copies.start(var_weight_h, var_weight_v),
    ]
    copies.wait(inputs[0])
    w_out_t[...] = lax.dot_general(
        w_out_v[...], row_table().astype(bf16), (((0,), (1,)), ((), ())),
        preferred_element_type=f32,
    ).astype(bf16)
    for copy in inputs[1:]:
        copies.wait(copy)
    row = lax.broadcasted_iota(jnp.int32, (OWN, VARS), 0)
    held = (row < OWN - 1) & (lanes((OWN, VARS)) == owner[0] * (OWN - 1) + row)
    scale = jnp.sum(jnp.where(held, var_weight_v[...], 0.0), axis=1, keepdims=True)
    weight[...] = area_v[...] * scale
    target[...] = lax.dot_general(
        held.astype(f32), target_v[...], (((1,), (0,)), ((), ())),
        precision=lax.Precision.HIGHEST, preferred_element_type=f32,
    )
    area_sum[...] = jnp.broadcast_to(jnp.sum(area_v[...], keepdims=True), area_sum.shape)
    copies.finish()


def prepare(owner, w_out, target, area, var_weight):
    hid = w_out.shape[1]
    pts = target.shape[1]
    return pl.pallas_call(
        prepare_kernel,
        in_specs=[smem()] + [hbm()] * 4,
        out_specs=[whole()] * 4,
        out_shape=[
            jax.ShapeDtypeStruct((hid, PAD), bf16),
            jax.ShapeDtypeStruct((OWN, pts), f32),
            jax.ShapeDtypeStruct((OWN, pts), f32),
            jax.ShapeDtypeStruct((8, PAD), f32),
        ],
        scratch_shapes=scratch(
            (w_out.shape, bf16), (target.shape, f32), (area.shape, f32), (var_weight.shape, f32),
            copies=4,
        ),
        compiler_params=params(16),
        cost_estimate=pl.CostEstimate(flops=1 << 28, bytes_accessed=1 << 20, transcendentals=0),
        name="prepare",
    )(owner, *in_hbm(w_out, target, area, var_weight))


def grad_kernel(w_in, dpre, scale, grad, w_in_v, grad_v, sems):
    copies = Copies(sems)
    copies.start(w_in, w_in_v)
    copies.finish()
    factor = scale[0:1, 0:1]
    for here in blocks(w_in.shape[1]):
        value = lax.dot_general(
            w_in_v[:, here], dpre[...], (((0,), (0,)), ((), ())), preferred_element_type=f32
        )
        grad_v[here, :] = (value * factor).astype(bf16)
        copies.start(grad_v.at[here], grad.at[here])
    copies.finish()


def grad_latent(w_in, dpre, scale):
    hid, lat = w_in.shape
    pts = dpre.shape[1]
    return pl.pallas_call(
        grad_kernel,
        in_specs=[hbm(), whole(), whole()],
        out_specs=hbm(),
        out_shape=pltpu.HBM((lat, pts), bf16),
        scratch_shapes=scratch(
            ((hid, lat), bf16), ((lat, pts), bf16), copies=1 + len(blocks(lat))
        ),
        compiler_params=params(16),
        cost_estimate=pl.CostEstimate(
            flops=2 * hid * lat * pts, bytes_accessed=4 << 20, transcendentals=0
        ),
        name="grad_latent",
    )(*in_hbm(w_in), dpre, scale)


def pairs_kernel(members, cores, fields, target, weight, area_sum, dout, dout_v, sems):
    copies = Copies(sems)
    count = float(members)
    own, pts = fields.shape[1:]
    slopes = [None] * members
    total = None
    for m in range(1, members):
        for k in range(m):
            diff = fields[m] - fields[k]
            square = diff * diff + smooth_sq
            inverse = lax.rsqrt(square)
            slope = diff * inverse
            apart = square * inverse
            total = apart if total is None else total + apart
            slopes[m] = slope if slopes[m] is None else slopes[m] + slope
            slopes[k] = -slope if slopes[k] is None else slopes[k] - slope
    total = 2.0 * total + count * smooth_sq**0.5
    local = total * (-1.0 / (2.0 * count * (count - 1.0)))
    values = []
    for m in range(members):
        miss = fields[m] - target[...]
        square = miss * miss + smooth_sq
        inverse = lax.rsqrt(square)
        local = local + square * inverse * (1.0 / count)
        values.append(
            weight[...]
            * (miss * inverse * (1.0 / count) - slopes[m] * (1.0 / (count * (count - 1.0))))
        )
    loss = jnp.sum(weight[...] * local, keepdims=True)
    lane = lanes((own, pts))
    last = lax.broadcasted_iota(jnp.int32, (own, pts), 0) == own - 1
    ride = jnp.zeros((own, pts), f32)
    for k, value in enumerate((loss, area_sum[0:1, 0:1])):
        high = value.astype(bf16).astype(f32)
        ride = jnp.where(lane == 2 * k, high, jnp.where(lane == 2 * k + 1, value - high, ride))
    for m in range(members):
        value = jnp.where(last, ride, values[m]).astype(bf16)
        for c in range(cores):
            dout_v[m * cores + c] = value
    copies.start(dout_v, dout)
    copies.finish()


def pairs(fields, target, weight, area_sum, cores):
    members, own, pts = fields.shape
    shape = (members * cores, own, pts)
    return pl.pallas_call(
        functools.partial(pairs_kernel, members, cores),
        in_specs=[whole()] * 4,
        out_specs=hbm(),
        out_shape=pltpu.HBM(shape, bf16),
        scratch_shapes=scratch((shape, bf16), copies=1),
        compiler_params=params(8),
        name="pairs",
    )(fields, target, weight, area_sum)


def backward_kernel(
    place, dout, w_out_t, slope_v, slope_far, latent, latent_far, hidden, hidden_far,
    terms_v, dpre_v, slope_far_v, latent_v, hidden_far_v, sems,
):
    copies = Copies(sems)
    me = place[0]
    rows = terms_v.shape[1]
    hid, pts = slope_v.shape
    parts = blocks(hid)

    def fetch(source, target, here):
        return copies.start(source.at[here], target.at[here])

    mine = (slice(None), pl.ds(2 * me, 2))
    near = copies.start(latent.at[mine], latent_v)
    halves = [fetch(slope_far, slope_far_v, parts[0])]
    for here in parts[1:]:
        halves.append(fetch(slope_far, slope_far_v, here))
    late = copies.start(hidden_far.at[mine], hidden_far_v)

    row = lax.broadcasted_iota(jnp.int32, (PAD, pts), 0)
    last = lax.rem(row, OWN) == OWN - 1
    seeds = []
    ride = jnp.zeros((1, pts), f32)
    for which in (me, 1 - me):
        value = dout[:, pl.ds(which, 1)].astype(f32).reshape(PAD, pts)
        ride = ride + jnp.sum(jnp.where(last, value, 0.0), axis=0, keepdims=True)
        seeds.append(jnp.where(last, 0.0, value).astype(bf16))

    copies.wait(near)
    for half in halves:
        copies.wait(half)
    copies.wait(late)
    features = [
        [latent_v[:, k].reshape(-1, pts) for k in range(2)],
        [latent_far[:, pl.ds(2 * me + k, 1)].reshape(-1, pts) for k in range(2)],
    ]
    for here, half in zip(parts, halves):
        first = second = None
        for k, ref in enumerate((slope_v, slope_far_v)):
            dh = dot(w_out_t[here, :], seeds[k])
            dpre = (dh * ref[here, :].astype(f32)).astype(bf16)
            if k == 0:
                dpre_v[here, :] = dpre
            swapped = jnp.concatenate(
                [
                    dpre[base + off : base + off + HALF]
                    for base in range(0, BLOCK, PAD)
                    for off in (HALF, 0)
                ],
                0,
            )
            a = dot_nt(features[k][0], dpre)
            b = dot_nt(features[k][1], swapped)
            first = a if first is None else first + a
            second = b if second is None else second + b
        low = lax.rem(lanes(first.shape), PAD) < HALF
        for xh, value in enumerate(
            (jnp.where(low, first, second), jnp.where(low, second, first))
        ):
            for xl in range(2):
                terms_v[2 * xh + xl, :, here] = value[xl * rows : (xl + 1) * rows].astype(bf16)

    out = dot_nt(hidden[:, pl.ds(2 * me, 2)].reshape(-1, pts), seeds[0])
    out += dot_nt(hidden_far_v[...].reshape(-1, pts), seeds[1])
    out = out.reshape(-1, 2, 16, PAD)
    left = out[:, 0].reshape(-1, PAD)
    right = out[:, 1].reshape(-1, PAD)
    lane = lanes((1, PAD))
    parts = jnp.zeros((1, PAD), f32)
    for k in range(2):
        mine = lax.div(lanes((1, pts)), 2) == k
        value = jnp.sum(jnp.where(mine, ride, 0.0), axis=1, keepdims=True)
        high = value.astype(bf16).astype(f32)
        parts = jnp.where(lane == spare(2 * k), high, parts)
        parts = jnp.where(lane == spare(2 * k + 1), value - high, parts)
    row = lax.rem(lax.broadcasted_iota(jnp.int32, left.shape, 0), 16)
    unused = lax.rem(lanes(left.shape), OWN) == OWN - 1
    left = jnp.where(unused, jnp.where(row == 0, parts, 0.0), left)
    for xh in range(2):
        for xl in range(2):
            piece = slice(xl * rows, (xl + 1) * rows)
            terms_v[2 * xh + xl, :, hid : hid + PAD] = left[piece].astype(bf16)
            terms_v[2 * xh + xl, :, hid + PAD :] = right[piece].astype(bf16)


def backward(place, dout, w_out_t, slope, slope_far, latent, latent_far, hidden, hidden_far):
    hid, pts = slope.shape
    plane = latent.shape[0]
    shape = (4, plane * 16 // 2, hid + 2 * PAD)
    half = ((plane, 2, 16, pts), bf16)
    return pl.pallas_call(
        backward_kernel,
        in_specs=[smem()] + [whole()] * 3 + [hbm()] * 2 + [whole()] * 2 + [hbm()],
        out_specs=[whole()] * 2,
        out_shape=[
            jax.ShapeDtypeStruct(shape, bf16),
            jax.ShapeDtypeStruct((hid, pts), bf16),
        ],
        scratch_shapes=scratch(
            ((hid, pts), bf16), half, half,
            copies=len(blocks(hid)) + 2,
        ),
        compiler_params=params(24),
        name="backward",
    )(
        place, dout, w_out_t, slope, *in_hbm(slope_far, latent), latent_far, hidden,
        *in_hbm(hidden_far),
    )


def split_again(tile):
    lane = lanes(tile.shape)
    value = tile + pltpu.roll(tile, PAD - OWN, 1)
    high = value.astype(bf16).astype(f32)
    low = pltpu.roll(value - high, OWN, 1)
    even = (lane == spare(0)) | (lane == spare(2))
    odd = (lane == spare(1)) | (lane == spare(3))
    return jnp.where(even, high, jnp.where(odd, low, tile))


def add_x_kernel(hid, got, out):
    value = got[0].astype(f32)
    for k in range(1, got.shape[0]):
        value = value + got[k].astype(f32)
    out[:, 0:hid] = value[:, 0:hid].astype(bf16)
    out[:, hid : hid + PAD] = split_again(value[:, hid : hid + PAD]).astype(bf16)
    out[:, hid + PAD :] = value[:, hid + PAD :].astype(bf16)


def add_x(got, hid):
    return pl.pallas_call(
        functools.partial(add_x_kernel, hid),
        in_specs=[whole()],
        out_specs=whole(),
        out_shape=jax.ShapeDtypeStruct(got.shape[1:], bf16),
        compiler_params=params(8),
        name="add_x",
    )(got)


def pick(head, k):
    lane = lanes(head.shape)
    mine = (lane == spare(2 * k)) | (lane == spare(2 * k + 1))
    return jnp.sum(jnp.where(mine, head, 0.0), axis=1, keepdims=True)


def add_z_kernel(hid, copied, points_all, got, out, scale, out_v, sems):
    copies = Copies(sems)
    value = got[0].astype(f32)
    for k in range(1, got.shape[0]):
        value = value + got[k].astype(f32)
    left = value[:, hid : hid + PAD]
    keep = split_again(left).astype(bf16)
    right = value[:, hid + PAD :].astype(bf16)
    for y in range(out.shape[0]):
        out_v[y, :, 0:PAD] = value[:, y * PAD : (y + 1) * PAD].astype(bf16)
        out_v[y, :, PAD : 2 * PAD] = keep
        out_v[y, :, 2 * PAD :] = right
    copies.start(out_v, out)
    weight_total = pick(left[0:1, :], 1) * (1.0 / copied)
    scale[...] = jnp.broadcast_to(points_all / (weight_total * VARS), scale.shape)
    copies.finish()


def add_z(got, hid, copied, points_all):
    shape = (hid // PAD, got.shape[1], 3 * PAD)
    return pl.pallas_call(
        functools.partial(add_z_kernel, hid, copied, points_all),
        in_specs=[whole()],
        out_specs=[hbm(), whole()],
        out_shape=[pltpu.HBM(shape, bf16), jax.ShapeDtypeStruct((8, PAD), f32)],
        scratch_shapes=scratch((shape, bf16), copies=1),
        compiler_params=params(4),
        name="add_z",
    )(got)


def finish_kernel(copied, points_all, count, turn, got, loss, grad_in, grad_out):
    value = got[0].astype(f32)
    for k in range(1, got.shape[0]):
        value = value + got[k].astype(f32)
    left = value[:, PAD : 2 * PAD]
    head = left[0:1, :]
    weight_total = pick(head, 1) * (1.0 / (copied * count))
    scale = 1.0 / (weight_total * VARS)
    loss[...] = pick(head, 0) * (1.0 / copied) * scale
    ratio = scale * (points_all / (points_all * count) ** 0.5)
    tile = value[:, 0:PAD] * ratio
    other = pltpu.roll(tile, HALF, 1)
    even = turn[0] == 0
    grad_in[0:16, :] = jnp.where(even, tile, other)[:, 0:HALF]
    grad_in[16:32, :] = jnp.where(even, other, tile)[:, 0:HALF]
    both = jnp.concatenate([left, value[:, 2 * PAD :]], 0) * ratio
    grad_out[...] = lax.dot_general(
        both, row_table().astype(f32), (((1,), (0,)), ((), ())),
        precision=lax.Precision.HIGHEST, preferred_element_type=f32,
    )


def finish(turn, got, copied, points_all, count):
    return pl.pallas_call(
        functools.partial(finish_kernel, copied, points_all, count),
        in_specs=[smem(), whole()],
        out_specs=[whole()] * 3,
        out_shape=[
            jax.ShapeDtypeStruct((1, 1), f32),
            jax.ShapeDtypeStruct((32, HALF), f32),
            jax.ShapeDtypeStruct((32, VARS), f32),
        ],
        compiler_params=params(4),
        name="finish",
    )(turn, got)


def per_device(latent, w_in, w_out, target, area, var_weight):
    n_ens = lax.axis_size(ENS)
    n_plane = lax.axis_size(PLANE)
    n_core = lax.axis_size("c")
    n_z = lax.axis_size("z")
    pts = area.shape[0]
    hid, _ = w_in.shape
    own = PAD // n_ens
    assert own == OWN
    me = lax.axis_index(ENS)
    core = lax.axis_index("c")
    swap = [(0, 1), (1, 0)]
    features = latent[0]

    count = float(n_ens)
    points_all = float(n_plane * n_core * pts)
    hidden, slope, decoded = forward(w_in, features, w_out)

    fields = exchange(decoded.reshape(n_ens, own, pts), ENS)
    late = lax.optimization_barrier((features, w_out, decoded))
    far = lax.ppermute(late[0], "c", swap)
    w_out_t, target_own, weight_own, area_sum = prepare(
        me.astype(jnp.int32)[None], late[1], target, area[None, :], var_weight[None, :]
    )
    dout = pairs(fields, target_own, weight_own, area_sum, n_core)

    dout_got = exchange(dout, ENS + ("c",))
    far, _ = lax.optimization_barrier((far, dout))
    hidden_far, slope_far = far_forward(w_in, far)

    groups = lambda value: value.reshape(n_plane, 2 * n_core, 16, pts)
    terms, dpre = backward(
        core.astype(jnp.int32)[None],
        dout_got.reshape(n_ens, n_core, own, pts),
        w_out_t, slope, slope_far,
        groups(features), groups(far), groups(hidden), groups(hidden_far),
    )

    got = exchange(terms, CHIP_X)
    got = exchange(add_x(got, hid).reshape(n_z, 16, hid + 2 * PAD), "z")
    got, scale = add_z(got, hid, count * lax.axis_size("xh"), points_all)
    got = exchange(got, "y")
    grad_lat = grad_latent(w_in, dpre, scale)
    loss, part_in, part_out = finish(
        lax.axis_index("xh").astype(jnp.int32)[None], got, count, points_all, count
    )
    return loss[0, 0], grad_lat[None], part_in.T, part_out.T


def solution(mesh):
    ens, grid_all = mesh.devices.shape
    split = (ens // 2, 2, 2, grid_all // 4, 2)
    fine = Mesh(mesh.devices.reshape(split), ENS + PLANE + ("c",))
    grid = PLANE + ("c",)
    in_specs = (P(ENS, None, grid), P(), P(), P(None, grid), P(grid), P())
    out_specs = (P(), P(ENS, None, grid), P(ENS, grid), P(None, grid))
    return jax.shard_map(
        per_device, mesh=fine, in_specs=in_specs, out_specs=out_specs, check_vma=False
    )
```

```python
import functools

import jax
import jax.numpy as jnp
from jax import lax
from jax.experimental import pallas as pl
from jax.experimental.pallas import tpu as pltpu
from jax.sharding import Mesh, PartitionSpec as P

VARS = 99
PAD = 128
HALF = PAD // 2
OWN = 8
ENS = ("y", "xh")
PLANE = ("xl", "z")
BLOCK = 1024

smooth_sq = 0.01
gelu_c = 0.7978845608
gelu_k = 0.044715
f32 = jnp.float32
bf16 = jnp.bfloat16
NT = (((1,), (1,)), ((), ()))


def gelu(value):
    square = value * value
    share = 0.5 + 0.5 * jnp.tanh(value * (gelu_c + gelu_c * gelu_k * square))
    bend = value * (2.0 * gelu_c + 6.0 * gelu_c * gelu_k * square)
    return value * share, share + share * ((1.0 - share) * bend)


def exchange(pieces, axes):
    return lax.all_to_all(pieces, axes, split_axis=0, concat_axis=0, tiled=True)


def dot(a, b):
    return jnp.dot(a, b, preferred_element_type=f32)


def dot_nt(a, b):
    return lax.dot_general(a, b, NT, preferred_element_type=f32)


def whole():
    return pl.BlockSpec(memory_space=pltpu.VMEM)


def smem():
    return pl.BlockSpec(memory_space=pltpu.SMEM)


def hbm():
    return pl.BlockSpec(memory_space=pltpu.HBM)


def in_hbm(*arrays):
    return [pltpu.with_memory_space_constraint(array, pltpu.HBM) for array in arrays]


def params(mib):
    return pltpu.CompilerParams(vmem_limit_bytes=mib << 20)


class Copies:
    def __init__(self, sems):
        self.sems = sems
        self.used = 0
        self.open = []

    def start(self, source, target):
        copy = pltpu.make_async_copy(source, target, self.sems.at[self.used])
        self.used += 1
        copy.start()
        self.open.append(copy)
        return copy

    def wait(self, copy):
        copy.wait()
        self.open = [other for other in self.open if other is not copy]

    def finish(self):
        for copy in self.open:
            self.wait(copy)


def scratch(*shapes, copies):
    return [pltpu.VMEM(shape, kind) for shape, kind in shapes] + [
        pltpu.SemaphoreType.DMA((copies,))
    ]


def blocks(size):
    step = min(size, BLOCK)
    return [slice(at, at + step) for at in range(0, size, step)]


def spare(k):
    return OWN * (k + 1) - 1


def row_table():
    row = lax.broadcasted_iota(jnp.int32, (PAD, VARS), 0)
    held = lax.rem(row, OWN) < OWN - 1
    variable = lax.div(row, OWN) * (OWN - 1) + lax.rem(row, OWN)
    return held & (variable == lanes((PAD, VARS)))


def lanes(shape):
    return lax.broadcasted_iota(jnp.int32, shape, len(shape) - 1)


class Stream:
    def __init__(self, copies, source, target):
        self.copies = copies
        self.started = []
        for here in blocks(source.shape[0]):
            middle = (here.start + here.stop) // 2
            self.started.append(
                [
                    copies.start(source.at[part], target.at[part])
                    for part in (slice(here.start, middle), slice(middle, here.stop))
                ]
            )

    def wait(self, k):
        for copy in self.started[k]:
            self.copies.wait(copy)


def products(weights, w_in_v, latent):
    parts = blocks(w_in_v.shape[0])
    ahead = None
    for k, here in enumerate(parts):
        if ahead is None:
            weights.wait(k)
            ahead = dot(w_in_v[here, :], latent[...])
        now = ahead
        if k + 1 < len(parts):
            weights.wait(k + 1)
            ahead = dot(w_in_v[parts[k + 1], :], latent[...])
        yield here, now


def forward_kernel(
    w_in, latent, w_out, hidden, slope, decoded, w_in_v, latent_v, w_out_v, decoded_v, sems
):
    copies = Copies(sems)
    first = copies.start(latent, latent_v)
    rows = copies.start(w_out, w_out_v)
    weights = Stream(copies, w_in, w_in_v)
    copies.wait(first)
    copies.wait(rows)
    w_out_rows = dot(row_table().astype(bf16), w_out_v[...]).astype(bf16)
    total = None
    for here, product in products(weights, w_in_v, latent_v):
        value, bend = gelu(product)
        value = value.astype(bf16)
        hidden[here, :] = value
        slope[here, :] = bend.astype(bf16)
        part = dot(w_out_rows[:, here], value)
        total = part if total is None else total + part
    decoded_v[...] = total
    copies.start(decoded_v, decoded)
    copies.finish()


def forward(w_in, latent, w_out):
    hid, lat = w_in.shape
    pts = latent.shape[1]
    return pl.pallas_call(
        forward_kernel,
        in_specs=[hbm()] * 3,
        out_specs=[whole(), whole(), hbm()],
        out_shape=[
            jax.ShapeDtypeStruct((hid, pts), bf16),
            jax.ShapeDtypeStruct((hid, pts), bf16),
            pltpu.HBM((PAD, pts), f32),
        ],
        scratch_shapes=scratch(
            ((hid, lat), bf16), ((lat, pts), bf16), ((VARS, hid), bf16), ((PAD, pts), f32),
            copies=4 * len(blocks(hid)) + 3,
        ),
        compiler_params=params(16),
        name="forward",
    )(*in_hbm(w_in, latent, w_out))


def far_kernel(w_in, latent, hidden, slope, w_in_v, latent_v, hidden_v, slope_v, sems):
    copies = Copies(sems)
    first = copies.start(latent, latent_v)
    weights = Stream(copies, w_in, w_in_v)
    copies.wait(first)
    for here, product in products(weights, w_in_v, latent_v):
        value, bend = gelu(product)
        hidden_v[here, :] = value.astype(bf16)
        copies.start(hidden_v.at[here], hidden.at[here])
        slope_v[here, :] = bend.astype(bf16)
        copies.start(slope_v.at[here], slope.at[here])
    copies.finish()


def far_forward(w_in, latent):
    hid, lat = w_in.shape
    pts = latent.shape[1]
    return pl.pallas_call(
        far_kernel,
        in_specs=[hbm()] * 2,
        out_specs=[hbm()] * 2,
        out_shape=[pltpu.HBM((hid, pts), bf16), pltpu.HBM((hid, pts), bf16)],
        scratch_shapes=scratch(
            ((hid, lat), bf16), ((lat, pts), bf16), ((hid, pts), bf16), ((hid, pts), bf16),
            copies=4 * len(blocks(hid)) + 1,
        ),
        compiler_params=params(16),
        cost_estimate=pl.CostEstimate(
            flops=2 * hid * lat * pts, bytes_accessed=4 << 20, transcendentals=hid * pts
        ),
        name="far_forward",
    )(*in_hbm(w_in), latent)


def prepare_kernel(
    owner, w_out_h, target_h, area_h, var_weight_h, w_out_t_h, target, weight, area_sum,
    w_out_v, w_out_t, target_v, area_v, var_weight_v, sems,
):
    copies = Copies(sems)
    inputs = [
        copies.start(w_out_h, w_out_v),
        copies.start(target_h, target_v),
        copies.start(area_h, area_v),
        copies.start(var_weight_h, var_weight_v),
    ]
    copies.wait(inputs[0])
    w_out_t[...] = lax.dot_general(
        w_out_v[...], row_table().astype(bf16), (((0,), (1,)), ((), ())),
        preferred_element_type=f32,
    ).astype(bf16)
    copies.start(w_out_t, w_out_t_h)
    for copy in inputs[1:]:
        copies.wait(copy)
    row = lax.broadcasted_iota(jnp.int32, (OWN, VARS), 0)
    held = (row < OWN - 1) & (lanes((OWN, VARS)) == owner[0] * (OWN - 1) + row)
    scale = jnp.sum(jnp.where(held, var_weight_v[...], 0.0), axis=1, keepdims=True)
    weight[...] = area_v[...] * scale
    target[...] = lax.dot_general(
        held.astype(f32), target_v[...], (((1,), (0,)), ((), ())),
        precision=lax.Precision.HIGHEST, preferred_element_type=f32,
    )
    area_sum[...] = jnp.broadcast_to(jnp.sum(area_v[...], keepdims=True), area_sum.shape)
    copies.finish()


def prepare(owner, w_out, target, area, var_weight):
    hid = w_out.shape[1]
    pts = target.shape[1]
    return pl.pallas_call(
        prepare_kernel,
        in_specs=[smem()] + [hbm()] * 4,
        out_specs=[hbm()] + [whole()] * 3,
        out_shape=[
            pltpu.HBM((hid, PAD), bf16),
            jax.ShapeDtypeStruct((OWN, pts), f32),
            jax.ShapeDtypeStruct((OWN, pts), f32),
            jax.ShapeDtypeStruct((8, PAD), f32),
        ],
        scratch_shapes=scratch(
            (w_out.shape, bf16), ((hid, PAD), bf16), (target.shape, f32),
            (area.shape, f32), (var_weight.shape, f32),
            copies=5,
        ),
        compiler_params=params(16),
        cost_estimate=pl.CostEstimate(flops=1 << 28, bytes_accessed=1 << 20, transcendentals=0),
        name="prepare",
    )(owner, *in_hbm(w_out, target, area, var_weight))


def grad_kernel(w_in, dpre, scale, grad, w_in_v, grad_v, sems):
    copies = Copies(sems)
    copies.start(w_in, w_in_v)
    copies.finish()
    factor = scale[0:1, 0:1]
    for here in blocks(w_in.shape[1]):
        value = lax.dot_general(
            w_in_v[:, here], dpre[...], (((0,), (0,)), ((), ())), preferred_element_type=f32
        )
        grad_v[here, :] = (value * factor).astype(bf16)
        copies.start(grad_v.at[here], grad.at[here])
    copies.finish()


def grad_latent(w_in, dpre, scale):
    hid, lat = w_in.shape
    pts = dpre.shape[1]
    return pl.pallas_call(
        grad_kernel,
        in_specs=[hbm(), whole(), whole()],
        out_specs=hbm(),
        out_shape=pltpu.HBM((lat, pts), bf16),
        scratch_shapes=scratch(
            ((hid, lat), bf16), ((lat, pts), bf16), copies=1 + len(blocks(lat))
        ),
        compiler_params=params(16),
        cost_estimate=pl.CostEstimate(
            flops=2 * hid * lat * pts, bytes_accessed=4 << 20, transcendentals=0
        ),
        name="grad_latent",
    )(*in_hbm(w_in), dpre, scale)


def pairs_kernel(members, cores, fields, target, weight, area_sum, dout, dout_v, sems):
    copies = Copies(sems)
    count = float(members)
    own, pts = fields.shape[1:]
    slopes = [None] * members
    total = None
    for m in range(1, members):
        for k in range(m):
            diff = fields[m] - fields[k]
            square = diff * diff + smooth_sq
            inverse = lax.rsqrt(square)
            slope = diff * inverse
            apart = square * inverse
            total = apart if total is None else total + apart
            slopes[m] = slope if slopes[m] is None else slopes[m] + slope
            slopes[k] = -slope if slopes[k] is None else slopes[k] - slope
    total = 2.0 * total + count * smooth_sq**0.5
    local = total * (-1.0 / (2.0 * count * (count - 1.0)))
    values = []
    for m in range(members):
        miss = fields[m] - target[...]
        square = miss * miss + smooth_sq
        inverse = lax.rsqrt(square)
        local = local + square * inverse * (1.0 / count)
        values.append(
            weight[...]
            * (miss * inverse * (1.0 / count) - slopes[m] * (1.0 / (count * (count - 1.0))))
        )
    loss = jnp.sum(weight[...] * local, keepdims=True)
    lane = lanes((own, pts))
    last = lax.broadcasted_iota(jnp.int32, (own, pts), 0) == own - 1
    ride = jnp.zeros((own, pts), f32)
    for k, value in enumerate((loss, area_sum[0:1, 0:1])):
        high = value.astype(bf16).astype(f32)
        ride = jnp.where(lane == 2 * k, high, jnp.where(lane == 2 * k + 1, value - high, ride))
    for m in range(members):
        value = jnp.where(last, ride, values[m]).astype(bf16)
        for c in range(cores):
            dout_v[m * cores + c] = value
    copies.start(dout_v, dout)
    copies.finish()


def pairs(fields, target, weight, area_sum, cores):
    members, own, pts = fields.shape
    shape = (members * cores, own, pts)
    return pl.pallas_call(
        functools.partial(pairs_kernel, members, cores),
        in_specs=[whole()] * 4,
        out_specs=hbm(),
        out_shape=pltpu.HBM(shape, bf16),
        scratch_shapes=scratch((shape, bf16), copies=1),
        compiler_params=params(8),
        name="pairs",
    )(fields, target, weight, area_sum)


def backward_kernel(
    place, dout, w_out_t_h, slope, hidden, latent, *refs
):
    sides = 4
    far_latents, far_hiddens, far_slopes = refs[0:3], refs[3:6], refs[6:9]
    terms, dpre_out = refs[9:11]
    w_out_t, latents_v, hiddens_v, slopes_v, sems = refs[11:16]
    copies = Copies(sems)
    xl, core = place[0], place[1]
    hid, pts = slope.shape

    mine = (pl.ds(xl, 1), slice(None), pl.ds(core, 1))
    copies.start(w_out_t_h, w_out_t)
    copies.start(latent.at[mine], latents_v.at[0])
    for k in range(sides - 1):
        copies.start(far_latents[k].at[mine], latents_v.at[k + 1])
        copies.start(far_slopes[k], slopes_v.at[k])
        copies.start(far_hiddens[k].at[mine], hiddens_v.at[k])

    row = lax.broadcasted_iota(jnp.int32, (PAD, pts), 0)
    last = lax.rem(row, OWN) == OWN - 1
    seeds = []
    ride = jnp.zeros((1, pts), f32)
    for at_x, at_c in ((xl, core), (xl, 1 - core), (1 - xl, core), (1 - xl, 1 - core)):
        value = dout[:, pl.ds(2 * at_x + at_c, 1)].astype(f32).reshape(PAD, pts)
        ride = ride + jnp.sum(jnp.where(last, value, 0.0), axis=0, keepdims=True)
        seeds.append(jnp.where(last, 0.0, value).astype(bf16))
    copies.finish()

    first = second = out = None
    for k in range(sides):
        dh = dot(w_out_t[...], seeds[k])
        bend = slope[...] if k == 0 else slopes_v[k - 1]
        dpre = (dh * bend.astype(f32)).astype(bf16)
        if k == 0:
            dpre_out[...] = dpre
        swapped = jnp.concatenate(
            [
                dpre[base + off : base + off + HALF]
                for base in range(0, hid, PAD)
                for off in (HALF, 0)
            ],
            0,
        )
        a = dot_nt(latents_v[k, 0, :, 0, 0].reshape(-1, pts), dpre)
        b = dot_nt(latents_v[k, 0, :, 0, 1].reshape(-1, pts), swapped)
        first = a if first is None else first + a
        second = b if second is None else second + b
        if k == 0:
            rows = hidden[pl.ds(xl, 1), :, pl.ds(core, 1)]
        else:
            rows = hiddens_v[k - 1]
        part = dot_nt(rows.reshape(-1, pts), seeds[k])
        out = part if out is None else out + part
    low = lax.rem(lanes(first.shape), PAD) < HALF
    terms[:, 0:hid] = jnp.where(low, first, second).astype(bf16)
    terms[:, hid : 2 * hid] = jnp.where(low, second, first).astype(bf16)

    out = out.reshape(-1, 2, 16, PAD)
    left = out[:, 0].reshape(-1, PAD)
    right = out[:, 1].reshape(-1, PAD)
    lane = lanes((1, PAD))
    parts = jnp.zeros((1, PAD), f32)
    for k in range(2):
        both = lax.div(lanes((1, pts)), 2) == k
        value = jnp.sum(jnp.where(both, ride, 0.0), axis=1, keepdims=True)
        high = value.astype(bf16).astype(f32)
        parts = jnp.where(lane == spare(2 * k), high, parts)
        parts = jnp.where(lane == spare(2 * k + 1), value - high, parts)
    row = lax.rem(lax.broadcasted_iota(jnp.int32, left.shape, 0), 16)
    unused = lax.rem(lanes(left.shape), OWN) == OWN - 1
    left = jnp.where(unused, jnp.where(row == 0, parts, 0.0), left)
    terms[:, 2 * hid : 2 * hid + PAD] = left.astype(bf16)
    terms[:, 2 * hid + PAD :] = right.astype(bf16)


def backward(place, dout, w_out_t, slope, hidden, latent, far_latents, far_hiddens, far_slopes):
    hid, pts = slope.shape
    n_z = latent.shape[1]
    quarter = (1, n_z, 1, 2, 16, pts)
    return pl.pallas_call(
        backward_kernel,
        in_specs=[smem(), whole(), hbm(), whole(), whole()] + [hbm()] * 10,
        out_specs=[whole()] * 2,
        out_shape=[
            jax.ShapeDtypeStruct((n_z * 16, 2 * hid + 2 * PAD), bf16),
            jax.ShapeDtypeStruct((hid, pts), bf16),
        ],
        scratch_shapes=scratch(
            ((hid, PAD), bf16), ((4, *quarter), bf16), ((3, *quarter), bf16),
            ((3, hid, pts), bf16), copies=11
        ),
        compiler_params=params(28),
        name="backward",
    )(
        place, dout, *in_hbm(w_out_t), slope, hidden,
        *in_hbm(latent), *far_latents, *in_hbm(*far_hiddens, *far_slopes),
    )


def split_again(tile):
    lane = lanes(tile.shape)
    value = tile + pltpu.roll(tile, PAD - OWN, 1)
    high = value.astype(bf16).astype(f32)
    low = pltpu.roll(value - high, OWN, 1)
    even = (lane == spare(0)) | (lane == spare(2))
    odd = (lane == spare(1)) | (lane == spare(3))
    return jnp.where(even, high, jnp.where(odd, low, tile))


def pick(head, k):
    lane = lanes(head.shape)
    mine = (lane == spare(2 * k)) | (lane == spare(2 * k + 1))
    return jnp.sum(jnp.where(mine, head, 0.0), axis=1, keepdims=True)


def add_z_kernel(hid, copied, points_all, got, out, scale, out_v, sems):
    copies = Copies(sems)
    value = got[0].astype(f32)
    for k in range(1, got.shape[0]):
        value = value + got[k].astype(f32)
    left = value[:, 2 * hid : 2 * hid + PAD]
    keep = split_again(left).astype(bf16)
    right = value[:, 2 * hid + PAD :].astype(bf16)
    for k in range(out.shape[0]):
        y, xh = k // 2, k % 2
        at = xh * hid + y * PAD
        out_v[k, :, 0:PAD] = value[:, at : at + PAD].astype(bf16)
        out_v[k, :, PAD : 2 * PAD] = keep
        out_v[k, :, 2 * PAD :] = right
    copies.start(out_v, out)
    weight_total = pick(left[0:1, :], 1) * (1.0 / copied)
    scale[...] = jnp.broadcast_to(points_all / (weight_total * VARS), scale.shape)
    copies.finish()


def add_z(got, hid, copied, points_all):
    shape = (2 * hid // PAD, got.shape[1], 3 * PAD)
    return pl.pallas_call(
        functools.partial(add_z_kernel, hid, copied, points_all),
        in_specs=[whole()],
        out_specs=[hbm(), whole()],
        out_shape=[pltpu.HBM(shape, bf16), jax.ShapeDtypeStruct((8, PAD), f32)],
        scratch_shapes=scratch((shape, bf16), copies=1),
        compiler_params=params(4),
        name="add_z",
    )(got)


def finish_kernel(copied, points_all, count, turn, got, loss, grad_in, grad_out):
    value = got[0].astype(f32)
    for k in range(1, got.shape[0]):
        value = value + got[k].astype(f32)
    left = value[:, PAD : 2 * PAD]
    head = left[0:1, :]
    weight_total = pick(head, 1) * (1.0 / (copied * count))
    scale = 1.0 / (weight_total * VARS)
    loss[...] = pick(head, 0) * (1.0 / copied) * scale
    ratio = scale * (points_all / (points_all * count) ** 0.5)
    tile = value[:, 0:PAD] * ratio
    other = pltpu.roll(tile, HALF, 1)
    even = turn[0] == 0
    grad_in[0:16, :] = jnp.where(even, tile, other)[:, 0:HALF]
    grad_in[16:32, :] = jnp.where(even, other, tile)[:, 0:HALF]
    both = jnp.concatenate([left, value[:, 2 * PAD :]], 0) * ratio
    grad_out[...] = lax.dot_general(
        both, row_table().astype(f32), (((1,), (0,)), ((), ())),
        precision=lax.Precision.HIGHEST, preferred_element_type=f32,
    )


def finish(turn, got, copied, points_all, count):
    return pl.pallas_call(
        functools.partial(finish_kernel, copied, points_all, count),
        in_specs=[smem(), whole()],
        out_specs=[whole()] * 3,
        out_shape=[
            jax.ShapeDtypeStruct((1, 1), f32),
            jax.ShapeDtypeStruct((32, HALF), f32),
            jax.ShapeDtypeStruct((32, VARS), f32),
        ],
        compiler_params=params(4),
        name="finish",
    )(turn, got)


def per_device(latent, w_in, w_out, target, area, var_weight):
    n_ens = lax.axis_size(ENS)
    n_plane = lax.axis_size(PLANE)
    n_core = lax.axis_size("c")
    n_z = lax.axis_size("z")
    n_xl = lax.axis_size("xl")
    pts = area.shape[0]
    hid, _ = w_in.shape
    own = PAD // n_ens
    assert own == OWN
    me = lax.axis_index(ENS)
    core = lax.axis_index("c")
    swap = [(0, 1), (1, 0)]
    features = latent[0]

    count = float(n_ens)
    points_all = float(n_plane * n_core * pts)
    hidden, slope, decoded = forward(w_in, features, w_out)

    fields = exchange(decoded.reshape(n_ens, own, pts), ENS)
    late = lax.optimization_barrier((features, w_out, decoded))
    below = lax.ppermute(late[0], "c", swap)
    beside = lax.ppermute(late[0], "xl", swap)
    w_out_t, target_own, weight_own, area_sum = prepare(
        me.astype(jnp.int32)[None], late[1], target, area[None, :], var_weight[None, :]
    )
    hidden_below, slope_below = far_forward(w_in, below)
    dout = pairs(fields, target_own, weight_own, area_sum, n_xl * n_core)

    dout_got = exchange(dout, ENS + ("xl", "c"))
    beside, below, _ = lax.optimization_barrier((beside, below, dout))
    across = lax.ppermute(beside, "c", swap)
    hidden_beside, slope_beside = far_forward(w_in, beside)
    hidden_across, slope_across = far_forward(w_in, across)

    groups = lambda value: value.reshape(n_xl, n_z, n_core, 2, 16, pts)
    terms, dpre = backward(
        jnp.stack([lax.axis_index("xl"), core]).astype(jnp.int32),
        dout_got.reshape(n_ens, n_xl * n_core, own, pts),
        w_out_t, slope, groups(hidden), groups(features),
        [groups(value) for value in (below, beside, across)],
        [groups(value) for value in (hidden_below, hidden_beside, hidden_across)],
        [slope_below, slope_beside, slope_across],
    )

    got = exchange(terms.reshape(n_z, 16, 2 * hid + 2 * PAD), "z")
    got, scale = add_z(got, hid, count, points_all)
    got = exchange(got, ENS)
    grad_lat = grad_latent(w_in, dpre, scale)
    loss, part_in, part_out = finish(
        lax.axis_index("xh").astype(jnp.int32)[None], got, count, points_all, count
    )
    return loss[0, 0], grad_lat[None], part_in.T, part_out.T


def solution(mesh):
    ens, grid_all = mesh.devices.shape
    split = (ens // 2, 2, 2, grid_all // 4, 2)
    fine = Mesh(mesh.devices.reshape(split), ENS + PLANE + ("c",))
    grid = PLANE + ("c",)
    in_specs = (P(ENS, None, grid), P(), P(), P(None, grid), P(grid), P())
    out_specs = (P(), P(ENS, None, grid), P(ENS, grid), P(None, grid))
    return jax.shard_map(
        per_device, mesh=fine, in_specs=in_specs, out_specs=out_specs, check_vma=False
    )
```

```python
import functools

import jax
import jax.numpy as jnp
from jax import lax
from jax.experimental import pallas as pl
from jax.experimental.pallas import tpu as pltpu
from jax.sharding import Mesh, PartitionSpec as P

VARS = 99
PAD = 128
HALF = PAD // 2
OWN = 8
ENS = ("y", "xh")
PLANE = ("xl", "z")
BLOCK = 1024

smooth_sq = 0.01
gelu_c = 0.7978845608
gelu_k = 0.044715
f32 = jnp.float32
bf16 = jnp.bfloat16
NT = (((1,), (1,)), ((), ()))


def gelu(value):
    square = value * value
    share = 0.5 + 0.5 * jnp.tanh(value * (gelu_c + gelu_c * gelu_k * square))
    bend = value * (2.0 * gelu_c + 6.0 * gelu_c * gelu_k * square)
    return value * share, share + share * ((1.0 - share) * bend)


def exchange(pieces, axes):
    return lax.all_to_all(pieces, axes, split_axis=0, concat_axis=0, tiled=True)


def dot(a, b):
    return jnp.dot(a, b, preferred_element_type=f32)


def dot_nt(a, b):
    return lax.dot_general(a, b, NT, preferred_element_type=f32)


def whole():
    return pl.BlockSpec(memory_space=pltpu.VMEM)


def smem():
    return pl.BlockSpec(memory_space=pltpu.SMEM)


def hbm():
    return pl.BlockSpec(memory_space=pltpu.HBM)


def in_hbm(*arrays):
    return [pltpu.with_memory_space_constraint(array, pltpu.HBM) for array in arrays]


def params(mib):
    return pltpu.CompilerParams(vmem_limit_bytes=mib << 20)


class Copies:
    def __init__(self, sems):
        self.sems = sems
        self.used = 0
        self.open = []

    def start(self, source, target):
        copy = pltpu.make_async_copy(source, target, self.sems.at[self.used])
        self.used += 1
        copy.start()
        self.open.append(copy)
        return copy

    def wait(self, copy):
        copy.wait()
        self.open = [other for other in self.open if other is not copy]

    def finish(self):
        for copy in self.open:
            self.wait(copy)


def scratch(*shapes, copies):
    return [pltpu.VMEM(shape, kind) for shape, kind in shapes] + [
        pltpu.SemaphoreType.DMA((copies,))
    ]


def blocks(size):
    step = min(size, BLOCK)
    return [slice(at, at + step) for at in range(0, size, step)]


def spare(k):
    return OWN * (k + 1) - 1


def row_table():
    row = lax.broadcasted_iota(jnp.int32, (PAD, VARS), 0)
    held = lax.rem(row, OWN) < OWN - 1
    variable = lax.div(row, OWN) * (OWN - 1) + lax.rem(row, OWN)
    return held & (variable == lanes((PAD, VARS)))


def lanes(shape):
    return lax.broadcasted_iota(jnp.int32, shape, len(shape) - 1)


class Stream:
    def __init__(self, copies, source, target):
        self.copies = copies
        self.started = []
        for here in blocks(source.shape[0]):
            middle = (here.start + here.stop) // 2
            self.started.append(
                [
                    copies.start(source.at[part], target.at[part])
                    for part in (slice(here.start, middle), slice(middle, here.stop))
                ]
            )

    def wait(self, k):
        for copy in self.started[k]:
            self.copies.wait(copy)


def products(weights, w_in_v, latent):
    parts = blocks(w_in_v.shape[0])
    ahead = None
    for k, here in enumerate(parts):
        if ahead is None:
            weights.wait(k)
            ahead = dot(w_in_v[here, :], latent[...])
        now = ahead
        if k + 1 < len(parts):
            weights.wait(k + 1)
            ahead = dot(w_in_v[parts[k + 1], :], latent[...])
        yield here, now


def forward_kernel(
    w_in, latent, w_out, hidden, slope, decoded, w_in_v, latent_v, w_out_v, decoded_v, sems
):
    copies = Copies(sems)
    first = copies.start(latent, latent_v)
    rows = copies.start(w_out, w_out_v)
    weights = Stream(copies, w_in, w_in_v)
    copies.wait(first)
    copies.wait(rows)
    w_out_rows = dot(row_table().astype(bf16), w_out_v[...]).astype(bf16)
    total = None
    for here, product in products(weights, w_in_v, latent_v):
        value, bend = gelu(product)
        value = value.astype(bf16)
        hidden[here, :] = value
        slope[here, :] = bend.astype(bf16)
        part = dot(w_out_rows[:, here], value)
        total = part if total is None else total + part
    decoded_v[...] = total
    copies.start(decoded_v, decoded)
    copies.finish()


def forward(w_in, latent, w_out):
    hid, lat = w_in.shape
    pts = latent.shape[1]
    return pl.pallas_call(
        forward_kernel,
        in_specs=[hbm()] * 3,
        out_specs=[whole(), whole(), hbm()],
        out_shape=[
            jax.ShapeDtypeStruct((hid, pts), bf16),
            jax.ShapeDtypeStruct((hid, pts), bf16),
            pltpu.HBM((PAD, pts), f32),
        ],
        scratch_shapes=scratch(
            ((hid, lat), bf16), ((lat, pts), bf16), ((VARS, hid), bf16), ((PAD, pts), f32),
            copies=4 * len(blocks(hid)) + 3,
        ),
        compiler_params=params(16),
        name="forward",
    )(*in_hbm(w_in, latent, w_out))


def far_kernel(w_in, latent, hidden, slope, w_in_v, latent_v, hidden_v, slope_v, sems):
    copies = Copies(sems)
    first = copies.start(latent, latent_v)
    weights = Stream(copies, w_in, w_in_v)
    copies.wait(first)
    for here, product in products(weights, w_in_v, latent_v):
        value, bend = gelu(product)
        hidden_v[here, :] = value.astype(bf16)
        copies.start(hidden_v.at[here], hidden.at[here])
        slope_v[here, :] = bend.astype(bf16)
        copies.start(slope_v.at[here], slope.at[here])
    copies.finish()


def far_forward(w_in, latent):
    hid, lat = w_in.shape
    pts = latent.shape[1]
    return pl.pallas_call(
        far_kernel,
        in_specs=[hbm()] * 2,
        out_specs=[hbm()] * 2,
        out_shape=[pltpu.HBM((hid, pts), bf16), pltpu.HBM((hid, pts), bf16)],
        scratch_shapes=scratch(
            ((hid, lat), bf16), ((lat, pts), bf16), ((hid, pts), bf16), ((hid, pts), bf16),
            copies=4 * len(blocks(hid)) + 1,
        ),
        compiler_params=params(16),
        cost_estimate=pl.CostEstimate(
            flops=2 * hid * lat * pts, bytes_accessed=4 << 20, transcendentals=hid * pts
        ),
        name="far_forward",
    )(*in_hbm(w_in), latent)


def prepare_kernel(
    owner, w_out_h, target_h, area_h, var_weight_h, w_out_t_h, target, weight, area_sum,
    w_out_v, w_out_t, target_v, area_v, var_weight_v, sems,
):
    copies = Copies(sems)
    inputs = [
        copies.start(w_out_h, w_out_v),
        copies.start(target_h, target_v),
        copies.start(area_h, area_v),
        copies.start(var_weight_h, var_weight_v),
    ]
    copies.wait(inputs[0])
    w_out_t[...] = lax.dot_general(
        w_out_v[...], row_table().astype(bf16), (((0,), (1,)), ((), ())),
        preferred_element_type=f32,
    ).astype(bf16)
    copies.start(w_out_t, w_out_t_h)
    for copy in inputs[1:]:
        copies.wait(copy)
    row = lax.broadcasted_iota(jnp.int32, (OWN, VARS), 0)
    held = (row < OWN - 1) & (lanes((OWN, VARS)) == owner[0] * (OWN - 1) + row)
    scale = jnp.sum(jnp.where(held, var_weight_v[...], 0.0), axis=1, keepdims=True)
    weight[...] = area_v[...] * scale
    target[...] = lax.dot_general(
        held.astype(f32), target_v[...], (((1,), (0,)), ((), ())),
        precision=lax.Precision.HIGHEST, preferred_element_type=f32,
    )
    area_sum[...] = jnp.broadcast_to(jnp.sum(area_v[...], keepdims=True), area_sum.shape)
    copies.finish()


def prepare(owner, w_out, target, area, var_weight):
    hid = w_out.shape[1]
    pts = target.shape[1]
    return pl.pallas_call(
        prepare_kernel,
        in_specs=[smem()] + [hbm()] * 4,
        out_specs=[hbm()] + [whole()] * 3,
        out_shape=[
            pltpu.HBM((hid, PAD), bf16),
            jax.ShapeDtypeStruct((OWN, pts), f32),
            jax.ShapeDtypeStruct((OWN, pts), f32),
            jax.ShapeDtypeStruct((8, PAD), f32),
        ],
        scratch_shapes=scratch(
            (w_out.shape, bf16), ((hid, PAD), bf16), (target.shape, f32),
            (area.shape, f32), (var_weight.shape, f32),
            copies=5,
        ),
        compiler_params=params(16),
        cost_estimate=pl.CostEstimate(flops=1 << 28, bytes_accessed=1 << 20, transcendentals=0),
        name="prepare",
    )(owner, *in_hbm(w_out, target, area, var_weight))


def grad_kernel(w_in, dpre, scale, grad, w_in_v, grad_v, sems):
    copies = Copies(sems)
    copies.start(w_in, w_in_v)
    copies.finish()
    factor = scale[0:1, 0:1]
    for here in blocks(w_in.shape[1]):
        value = lax.dot_general(
            w_in_v[:, here], dpre[...], (((0,), (0,)), ((), ())), preferred_element_type=f32
        )
        grad_v[here, :] = (value * factor).astype(bf16)
        copies.start(grad_v.at[here], grad.at[here])
    copies.finish()


def grad_latent(w_in, dpre, scale):
    hid, lat = w_in.shape
    pts = dpre.shape[1]
    return pl.pallas_call(
        grad_kernel,
        in_specs=[hbm(), whole(), whole()],
        out_specs=hbm(),
        out_shape=pltpu.HBM((lat, pts), bf16),
        scratch_shapes=scratch(
            ((hid, lat), bf16), ((lat, pts), bf16), copies=1 + len(blocks(lat))
        ),
        compiler_params=params(16),
        cost_estimate=pl.CostEstimate(
            flops=2 * hid * lat * pts, bytes_accessed=4 << 20, transcendentals=0
        ),
        name="grad_latent",
    )(*in_hbm(w_in), dpre, scale)


def pairs_kernel(members, cores, fields, target, weight, area_sum, dout, dout_v, sems):
    copies = Copies(sems)
    count = float(members)
    own, pts = fields.shape[1:]
    slopes = [None] * members
    total = None
    for m in range(1, members):
        for k in range(m):
            diff = fields[m] - fields[k]
            square = diff * diff + smooth_sq
            inverse = lax.rsqrt(square)
            slope = diff * inverse
            apart = square * inverse
            total = apart if total is None else total + apart
            slopes[m] = slope if slopes[m] is None else slopes[m] + slope
            slopes[k] = -slope if slopes[k] is None else slopes[k] - slope
    total = 2.0 * total + count * smooth_sq**0.5
    local = total * (-1.0 / (2.0 * count * (count - 1.0)))
    values = []
    for m in range(members):
        miss = fields[m] - target[...]
        square = miss * miss + smooth_sq
        inverse = lax.rsqrt(square)
        local = local + square * inverse * (1.0 / count)
        values.append(
            weight[...]
            * (miss * inverse * (1.0 / count) - slopes[m] * (1.0 / (count * (count - 1.0))))
        )
    loss = jnp.sum(weight[...] * local, keepdims=True)
    lane = lanes((own, pts))
    last = lax.broadcasted_iota(jnp.int32, (own, pts), 0) == own - 1
    ride = jnp.zeros((own, pts), f32)
    for k, value in enumerate((loss, area_sum[0:1, 0:1])):
        high = value.astype(bf16).astype(f32)
        ride = jnp.where(lane == 2 * k, high, jnp.where(lane == 2 * k + 1, value - high, ride))
    for m in range(members):
        value = jnp.where(last, ride, values[m]).astype(bf16)
        for c in range(cores):
            dout_v[m * cores + c] = value
    copies.start(dout_v, dout)
    copies.finish()


def pairs(fields, target, weight, area_sum, cores):
    members, own, pts = fields.shape
    shape = (members * cores, own, pts)
    return pl.pallas_call(
        functools.partial(pairs_kernel, members, cores),
        in_specs=[whole()] * 4,
        out_specs=hbm(),
        out_shape=pltpu.HBM(shape, bf16),
        scratch_shapes=scratch((shape, bf16), copies=1),
        compiler_params=params(8),
        name="pairs",
    )(fields, target, weight, area_sum)


def seeds_of(dout, which):
    value = dout[:, pl.ds(which, 1)].astype(f32).reshape(PAD, dout.shape[-1])
    last = lax.rem(lax.broadcasted_iota(jnp.int32, value.shape, 0), OWN) == OWN - 1
    ride = jnp.sum(jnp.where(last, value, 0.0), axis=0, keepdims=True)
    return jnp.where(last, 0.0, value).astype(bf16), ride


def side_terms(seeds, w_out_t, bend, features_a, features_b, rows):
    dpre = (dot(w_out_t, seeds) * bend.astype(f32)).astype(bf16)
    swapped = jnp.concatenate(
        [
            dpre[base + off : base + off + HALF]
            for base in range(0, dpre.shape[0], PAD)
            for off in (HALF, 0)
        ],
        0,
    )
    return dpre, dot_nt(features_a, dpre), dot_nt(features_b, swapped), dot_nt(rows, seeds)


def near_kernel(
    place, dout, w_out_t_h, slope, hidden, latent, latent_far, hidden_far, slope_far,
    first, second, outer, ride, dpre_out,
    w_out_t, latents_v, hidden_v, slope_v, sems,
):
    copies = Copies(sems)
    xl, core = place[0], place[1]
    pts = slope.shape[1]
    mine = (pl.ds(xl, 1), slice(None), pl.ds(core, 1))
    copies.start(w_out_t_h, w_out_t)
    copies.start(latent.at[mine], latents_v.at[0])
    copies.start(latent_far.at[mine], latents_v.at[1])
    copies.start(slope_far, slope_v)
    copies.start(hidden_far.at[mine], hidden_v)
    seeds = [seeds_of(dout, which) for which in (core, 1 - core)]
    copies.finish()
    total = [None, None, None]
    for k, bend in enumerate((slope, slope_v)):
        rows = hidden_v[...] if k else hidden[pl.ds(xl, 1), :, pl.ds(core, 1)]
        dpre, *parts = side_terms(
            seeds[k][0], w_out_t[...], bend[...],
            latents_v[k, 0, :, 0, 0].reshape(-1, pts),
            latents_v[k, 0, :, 0, 1].reshape(-1, pts),
            rows.reshape(-1, pts),
        )
        if k == 0:
            dpre_out[...] = dpre
        total = [part if old is None else old + part for old, part in zip(total, parts)]
    first[...], second[...], outer[...] = total
    ride[...] = jnp.broadcast_to(seeds[0][1] + seeds[1][1], ride.shape)


def near(place, dout, w_out_t, slope, hidden, latent, latent_far, hidden_far, slope_far):
    hid, pts = slope.shape
    n_z = latent.shape[1]
    quarter = (1, n_z, 1, 2, 16, pts)
    return pl.pallas_call(
        near_kernel,
        in_specs=[smem(), whole(), hbm(), whole(), whole()] + [hbm()] * 4,
        out_specs=[whole()] * 5,
        out_shape=[
            jax.ShapeDtypeStruct((n_z * 16, hid), f32),
            jax.ShapeDtypeStruct((n_z * 16, hid), f32),
            jax.ShapeDtypeStruct((n_z * 32, PAD), f32),
            jax.ShapeDtypeStruct((8, pts), f32),
            jax.ShapeDtypeStruct((hid, pts), bf16),
        ],
        scratch_shapes=scratch(
            ((hid, PAD), bf16), ((2, *quarter), bf16), (quarter, bf16), ((hid, pts), bf16),
            copies=5,
        ),
        compiler_params=params(20),
        cost_estimate=pl.CostEstimate(flops=1 << 30, bytes_accessed=4 << 20, transcendentals=0),
        name="near",
    )(
        place, dout, *in_hbm(w_out_t), slope, hidden, *in_hbm(latent), latent_far,
        *in_hbm(hidden_far, slope_far),
    )


def rest_kernel(
    place, dout, first, second, outer, ride_near, w_out_t_h, *refs
):
    latents, hiddens, bends = refs[0:2], refs[2:4], refs[4:6]
    kept, sent = refs[6:8]
    w_out_t, latents_v, hiddens_v, slopes_v, sems = refs[8:13]
    copies = Copies(sems)
    xl, core, xh = place[0], place[1], place[2]
    pts = dout.shape[-1]
    hid = first.shape[1]
    mine = (pl.ds(xl, 1), slice(None), pl.ds(core, 1))
    copies.start(w_out_t_h, w_out_t)
    for k in range(2):
        copies.start(latents[k].at[mine], latents_v.at[k])
        copies.start(bends[k], slopes_v.at[k])
        copies.start(hiddens[k].at[mine], hiddens_v.at[k])
    seeds = [seeds_of(dout, which) for which in (core, 1 - core)]
    copies.finish()
    total = [first[...], second[...], outer[...]]
    for k in range(2):
        _, *parts = side_terms(
            seeds[k][0], w_out_t[...], slopes_v[k],
            latents_v[k, 0, :, 0, 0].reshape(-1, pts),
            latents_v[k, 0, :, 0, 1].reshape(-1, pts),
            hiddens_v[k].reshape(-1, pts),
        )
        total = [old + part for old, part in zip(total, parts)]
    ride = ride_near[0:1, :] + seeds[0][1] + seeds[1][1]
    low = lax.rem(lanes(total[0].shape), PAD) < HALF
    keep = low == (xh == 0)
    kept[:, 0:hid] = jnp.where(keep, total[0], total[1]).astype(bf16)
    sent[:, 0:hid] = jnp.where(keep, total[1], total[0]).astype(bf16)

    out = total[2].reshape(-1, 2, 16, PAD)
    left = out[:, 0].reshape(-1, PAD)
    right = out[:, 1].reshape(-1, PAD)
    lane = lanes((1, PAD))
    parts = jnp.zeros((1, PAD), f32)
    for k in range(2):
        both = lax.div(lanes((1, pts)), 2) == k
        value = jnp.sum(jnp.where(both, ride, 0.0), axis=1, keepdims=True)
        high = value.astype(bf16).astype(f32)
        parts = jnp.where(lane == spare(2 * k), high, parts)
        parts = jnp.where(lane == spare(2 * k + 1), value - high, parts)
    row = lax.rem(lax.broadcasted_iota(jnp.int32, left.shape, 0), 16)
    unused = lax.rem(lanes(left.shape), OWN) == OWN - 1
    left = jnp.where(unused, jnp.where(row == 0, parts, 0.0), left)
    for ref in (kept, sent):
        ref[:, hid : hid + PAD] = left.astype(bf16)
        ref[:, hid + PAD :] = right.astype(bf16)


def rest(place, dout, sums, w_out_t, latents, hiddens, bends):
    first, _, _, ride = sums
    rows, hid = first.shape
    pts = ride.shape[1]
    quarter = (1, latents[0].shape[1], 1, 2, 16, pts)
    return pl.pallas_call(
        rest_kernel,
        in_specs=[smem()] + [whole()] * 5 + [hbm()] * 7,
        out_specs=[whole()] * 2,
        out_shape=[jax.ShapeDtypeStruct((rows, hid + 2 * PAD), bf16)] * 2,
        scratch_shapes=scratch(
            ((hid, PAD), bf16), ((2, *quarter), bf16), ((2, *quarter), bf16),
            ((2, hid, pts), bf16), copies=7,
        ),
        compiler_params=params(20),
        name="rest",
    )(place, dout, *sums, *in_hbm(w_out_t), *latents, *in_hbm(*hiddens, *bends))


def split_again(tile):
    lane = lanes(tile.shape)
    value = tile + pltpu.roll(tile, PAD - OWN, 1)
    high = value.astype(bf16).astype(f32)
    low = pltpu.roll(value - high, OWN, 1)
    even = (lane == spare(0)) | (lane == spare(2))
    odd = (lane == spare(1)) | (lane == spare(3))
    return jnp.where(even, high, jnp.where(odd, low, tile))


def add_x_kernel(hid, kept, got, out):
    value = kept[...].astype(f32) + got[...].astype(f32)
    out[:, 0:hid] = value[:, 0:hid].astype(bf16)
    out[:, hid : hid + PAD] = split_again(value[:, hid : hid + PAD]).astype(bf16)
    out[:, hid + PAD :] = value[:, hid + PAD :].astype(bf16)


def add_x(kept, got, hid):
    return pl.pallas_call(
        functools.partial(add_x_kernel, hid),
        in_specs=[whole()] * 2,
        out_specs=whole(),
        out_shape=jax.ShapeDtypeStruct(kept.shape, bf16),
        compiler_params=params(8),
        name="add_x",
    )(kept, got)


def pick(head, k):
    lane = lanes(head.shape)
    mine = (lane == spare(2 * k)) | (lane == spare(2 * k + 1))
    return jnp.sum(jnp.where(mine, head, 0.0), axis=1, keepdims=True)


def add_z_kernel(hid, copied, points_all, got, out, scale, out_v, sems):
    copies = Copies(sems)
    value = got[0].astype(f32)
    for k in range(1, got.shape[0]):
        value = value + got[k].astype(f32)
    left = value[:, hid : hid + PAD]
    keep = split_again(left).astype(bf16)
    right = value[:, hid + PAD :].astype(bf16)
    for y in range(out.shape[0]):
        out_v[y, :, 0:PAD] = value[:, y * PAD : (y + 1) * PAD].astype(bf16)
        out_v[y, :, PAD : 2 * PAD] = keep
        out_v[y, :, 2 * PAD :] = right
    copies.start(out_v, out)
    weight_total = pick(left[0:1, :], 1) * (1.0 / copied)
    scale[...] = jnp.broadcast_to(points_all / (weight_total * VARS), scale.shape)
    copies.finish()


def add_z(got, hid, copied, points_all):
    shape = (hid // PAD, got.shape[1], 3 * PAD)
    return pl.pallas_call(
        functools.partial(add_z_kernel, hid, copied, points_all),
        in_specs=[whole()],
        out_specs=[hbm(), whole()],
        out_shape=[pltpu.HBM(shape, bf16), jax.ShapeDtypeStruct((8, PAD), f32)],
        scratch_shapes=scratch((shape, bf16), copies=1),
        compiler_params=params(4),
        name="add_z",
    )(got)


def finish_kernel(copied, points_all, count, turn, got, loss, grad_in, grad_out):
    value = got[0].astype(f32)
    for k in range(1, got.shape[0]):
        value = value + got[k].astype(f32)
    left = value[:, PAD : 2 * PAD]
    head = left[0:1, :]
    weight_total = pick(head, 1) * (1.0 / (copied * count))
    scale = 1.0 / (weight_total * VARS)
    loss[...] = pick(head, 0) * (1.0 / copied) * scale
    ratio = scale * (points_all / (points_all * count) ** 0.5)
    tile = value[:, 0:PAD] * ratio
    other = pltpu.roll(tile, HALF, 1)
    even = turn[0] == 0
    grad_in[0:16, :] = jnp.where(even, tile, other)[:, 0:HALF]
    grad_in[16:32, :] = jnp.where(even, other, tile)[:, 0:HALF]
    both = jnp.concatenate([left, value[:, 2 * PAD :]], 0) * ratio
    grad_out[...] = lax.dot_general(
        both, row_table().astype(f32), (((1,), (0,)), ((), ())),
        precision=lax.Precision.HIGHEST, preferred_element_type=f32,
    )


def finish(turn, got, copied, points_all, count):
    return pl.pallas_call(
        functools.partial(finish_kernel, copied, points_all, count),
        in_specs=[smem(), whole()],
        out_specs=[whole()] * 3,
        out_shape=[
            jax.ShapeDtypeStruct((1, 1), f32),
            jax.ShapeDtypeStruct((32, HALF), f32),
            jax.ShapeDtypeStruct((32, VARS), f32),
        ],
        compiler_params=params(4),
        name="finish",
    )(turn, got)


def per_device(latent, w_in, w_out, target, area, var_weight):
    n_ens = lax.axis_size(ENS)
    n_plane = lax.axis_size(PLANE)
    n_core = lax.axis_size("c")
    n_z = lax.axis_size("z")
    n_xl = lax.axis_size("xl")
    pts = area.shape[0]
    hid, _ = w_in.shape
    own = PAD // n_ens
    assert own == OWN
    me = lax.axis_index(ENS)
    core = lax.axis_index("c")
    swap = [(0, 1), (1, 0)]
    features = latent[0]

    count = float(n_ens)
    points_all = float(n_plane * n_core * pts)
    hidden, slope, decoded = forward(w_in, features, w_out)

    fields = exchange(decoded.reshape(n_ens, own, pts), ENS)
    late = lax.optimization_barrier((features, w_out, decoded))
    below = lax.ppermute(late[0], "c", swap)
    beside = lax.ppermute(late[0], "xl", swap)
    w_out_t, target_own, weight_own, area_sum = prepare(
        me.astype(jnp.int32)[None], late[1], target, area[None, :], var_weight[None, :]
    )
    hidden_below, slope_below = far_forward(w_in, below)
    dout = pairs(fields, target_own, weight_own, area_sum, n_core)

    dout_got = exchange(dout, ENS + ("c",)).reshape(n_ens, n_core, own, pts)
    beside, below, _ = lax.optimization_barrier((beside, below, dout))
    across = lax.ppermute(beside, "c", swap)
    hidden_beside, slope_beside = far_forward(w_in, beside)
    hidden_across, slope_across = far_forward(w_in, across)

    dout_beside = lax.ppermute(dout_got, "xl", swap)
    groups = lambda value: value.reshape(n_xl, n_z, n_core, 2, 16, pts)
    place = jnp.stack([lax.axis_index("xl"), core, lax.axis_index("xh")]).astype(jnp.int32)
    *sums, dpre = near(
        place, dout_got, w_out_t, slope, groups(hidden), groups(features),
        groups(below), groups(hidden_below), slope_below,
    )
    kept, sent = rest(
        place, dout_beside, sums, w_out_t,
        [groups(value) for value in (beside, across)],
        [groups(value) for value in (hidden_beside, hidden_across)],
        [slope_beside, slope_across],
    )

    got = add_x(kept, lax.ppermute(sent, "xh", swap), hid)
    got = exchange(got.reshape(n_z, 16, hid + 2 * PAD), "z")
    got, scale = add_z(got, hid, count * lax.axis_size("xh"), points_all)
    got = exchange(got, "y")
    grad_lat = grad_latent(w_in, dpre, scale)
    loss, part_in, part_out = finish(
        lax.axis_index("xh").astype(jnp.int32)[None], got, count, points_all, count
    )
    return loss[0, 0], grad_lat[None], part_in.T, part_out.T


def solution(mesh):
    ens, grid_all = mesh.devices.shape
    split = (ens // 2, 2, 2, grid_all // 4, 2)
    fine = Mesh(mesh.devices.reshape(split), ENS + PLANE + ("c",))
    grid = PLANE + ("c",)
    in_specs = (P(ENS, None, grid), P(), P(), P(None, grid), P(grid), P())
    out_specs = (P(), P(ENS, None, grid), P(ENS, grid), P(None, grid))
    return jax.shard_map(
        per_device, mesh=fine, in_specs=in_specs, out_specs=out_specs, check_vma=False
    )
```

```python
import functools

import jax
import jax.numpy as jnp
from jax import lax
from jax.experimental import pallas as pl
from jax.experimental.pallas import tpu as pltpu
from jax.sharding import Mesh, PartitionSpec as P

VARS = 99
PAD = 128
HALF = PAD // 2
OWN = 8
ENS = ("y", "xh")
PLANE = ("xl", "z")
CHIP_X = ("xh", "xl")
BLOCK = 1024

smooth_sq = 0.01
gelu_c = 0.7978845608
gelu_k = 0.044715
f32 = jnp.float32
bf16 = jnp.bfloat16
NT = (((1,), (1,)), ((), ()))


def gelu(value):
    square = value * value
    share = 0.5 + 0.5 * jnp.tanh(value * (gelu_c + gelu_c * gelu_k * square))
    bend = value * (2.0 * gelu_c + 6.0 * gelu_c * gelu_k * square)
    return value * share, share + share * ((1.0 - share) * bend)


def exchange(pieces, axes):
    return lax.all_to_all(pieces, axes, split_axis=0, concat_axis=0, tiled=True)


def dot(a, b):
    return jnp.dot(a, b, preferred_element_type=f32)


def dot_nt(a, b):
    return lax.dot_general(a, b, NT, preferred_element_type=f32)


def whole():
    return pl.BlockSpec(memory_space=pltpu.VMEM)


def smem():
    return pl.BlockSpec(memory_space=pltpu.SMEM)


def hbm():
    return pl.BlockSpec(memory_space=pltpu.HBM)


def in_hbm(*arrays):
    return [pltpu.with_memory_space_constraint(array, pltpu.HBM) for array in arrays]


def params(mib):
    return pltpu.CompilerParams(vmem_limit_bytes=mib << 20)


class Copies:
    def __init__(self, sems):
        self.sems = sems
        self.used = 0
        self.open = []

    def start(self, source, target):
        copy = pltpu.make_async_copy(source, target, self.sems.at[self.used])
        self.used += 1
        copy.start()
        self.open.append(copy)
        return copy

    def wait(self, copy):
        copy.wait()
        self.open = [other for other in self.open if other is not copy]

    def finish(self):
        for copy in self.open:
            self.wait(copy)


def scratch(*shapes, copies):
    return [pltpu.VMEM(shape, kind) for shape, kind in shapes] + [
        pltpu.SemaphoreType.DMA((copies,))
    ]


def blocks(size):
    step = min(size, BLOCK)
    return [slice(at, at + step) for at in range(0, size, step)]


def spare(k):
    return OWN * (k + 1) - 1


def row_table():
    row = lax.broadcasted_iota(jnp.int32, (PAD, VARS), 0)
    held = lax.rem(row, OWN) < OWN - 1
    variable = lax.div(row, OWN) * (OWN - 1) + lax.rem(row, OWN)
    return held & (variable == lanes((PAD, VARS)))


def lanes(shape):
    return lax.broadcasted_iota(jnp.int32, shape, len(shape) - 1)


class Stream:
    def __init__(self, copies, source, target):
        self.copies = copies
        self.started = []
        for here in blocks(source.shape[0]):
            middle = (here.start + here.stop) // 2
            self.started.append(
                [
                    copies.start(source.at[part], target.at[part])
                    for part in (slice(here.start, middle), slice(middle, here.stop))
                ]
            )

    def wait(self, k):
        for copy in self.started[k]:
            self.copies.wait(copy)


def products(weights, w_in_v, latent):
    parts = blocks(w_in_v.shape[0])
    ahead = None
    for k, here in enumerate(parts):
        if ahead is None:
            weights.wait(k)
            ahead = dot(w_in_v[here, :], latent[...])
        now = ahead
        if k + 1 < len(parts):
            weights.wait(k + 1)
            ahead = dot(w_in_v[parts[k + 1], :], latent[...])
        yield here, now


def forward_kernel(
    owner, w_in, latent, w_out, target_h, area_h, var_weight_h,
    hidden, slope, decoded, w_out_t, target, weight, area_sum,
    w_in_v, latent_v, w_out_v, target_v, area_v, var_weight_v, sems,
):
    copies = Copies(sems)
    rows = copies.start(w_out, w_out_v)
    first = copies.start(latent, latent_v)
    weights = Stream(copies, w_in, w_in_v)
    copies.start(target_h, target_v)
    copies.start(area_h, area_v)
    copies.start(var_weight_h, var_weight_v)
    copies.wait(rows)
    table = row_table().astype(bf16)
    w_out_rows = dot(table, w_out_v[...]).astype(bf16)
    w_out_t[...] = lax.dot_general(
        w_out_v[...], table, (((0,), (1,)), ((), ())), preferred_element_type=f32
    ).astype(bf16)
    copies.wait(first)
    total = None
    for here, product in products(weights, w_in_v, latent_v):
        value, bend = gelu(product)
        value = value.astype(bf16)
        hidden[here, :] = value
        slope[here, :] = bend.astype(bf16)
        part = dot(w_out_rows[:, here], value)
        total = part if total is None else total + part
    decoded[...] = total
    copies.finish()
    row = lax.broadcasted_iota(jnp.int32, (OWN, VARS), 0)
    held = (row < OWN - 1) & (lanes((OWN, VARS)) == owner[0] * (OWN - 1) + row)
    scale = jnp.sum(jnp.where(held, var_weight_v[...], 0.0), axis=1, keepdims=True)
    weight[...] = area_v[...] * scale
    target[...] = lax.dot_general(
        held.astype(f32), target_v[...], (((1,), (0,)), ((), ())),
        precision=lax.Precision.HIGHEST, preferred_element_type=f32,
    )
    area_sum[...] = jnp.broadcast_to(jnp.sum(area_v[...], keepdims=True), area_sum.shape)


def forward(owner, w_in, latent, w_out, target, area, var_weight):
    hid, lat = w_in.shape
    pts = latent.shape[1]
    return pl.pallas_call(
        forward_kernel,
        in_specs=[smem()] + [hbm()] * 6,
        out_specs=[whole()] * 7,
        out_shape=[
            jax.ShapeDtypeStruct((hid, pts), bf16),
            jax.ShapeDtypeStruct((hid, pts), bf16),
            jax.ShapeDtypeStruct((PAD, pts), f32),
            jax.ShapeDtypeStruct((hid, PAD), bf16),
            jax.ShapeDtypeStruct((OWN, pts), f32),
            jax.ShapeDtypeStruct((OWN, pts), f32),
            jax.ShapeDtypeStruct((8, PAD), f32),
        ],
        scratch_shapes=scratch(
            ((hid, lat), bf16), ((lat, pts), bf16), (w_out.shape, bf16), (target.shape, f32),
            (area.shape, f32), (var_weight.shape, f32),
            copies=2 * len(blocks(hid)) + 5,
        ),
        compiler_params=params(16),
        name="forward",
    )(owner, *in_hbm(w_in, latent, w_out, target, area, var_weight))


def far_kernel(w_in, latent, hidden, slope, w_in_v, hidden_v, slope_v, sems):
    copies = Copies(sems)
    weights = Stream(copies, w_in, w_in_v)
    for here, product in products(weights, w_in_v, latent):
        value, bend = gelu(product)
        hidden_v[here, :] = value.astype(bf16)
        copies.start(hidden_v.at[here], hidden.at[here])
        slope_v[here, :] = bend.astype(bf16)
        copies.start(slope_v.at[here], slope.at[here])
    copies.finish()


def far_forward(w_in, latent):
    hid, lat = w_in.shape
    pts = latent.shape[1]
    return pl.pallas_call(
        far_kernel,
        in_specs=[hbm(), whole()],
        out_specs=[hbm()] * 2,
        out_shape=[pltpu.HBM((hid, pts), bf16), pltpu.HBM((hid, pts), bf16)],
        scratch_shapes=scratch(
            ((hid, lat), bf16), ((hid, pts), bf16), ((hid, pts), bf16),
            copies=6 * len(blocks(hid)),
        ),
        compiler_params=params(16),
        cost_estimate=pl.CostEstimate(
            flops=2 * hid * lat * pts, bytes_accessed=4 << 20, transcendentals=hid * pts
        ),
        name="far_forward",
    )(*in_hbm(w_in), latent)


def grad_kernel(w_in, dpre, scale, grad, w_in_v, grad_v, sems):
    copies = Copies(sems)
    copies.start(w_in, w_in_v)
    copies.finish()
    factor = scale[0:1, 0:1]
    for here in blocks(w_in.shape[1]):
        value = lax.dot_general(
            w_in_v[:, here], dpre[...], (((0,), (0,)), ((), ())), preferred_element_type=f32
        )
        grad_v[here, :] = (value * factor).astype(bf16)
        copies.start(grad_v.at[here], grad.at[here])
    copies.finish()


def grad_latent(w_in, dpre, scale):
    hid, lat = w_in.shape
    pts = dpre.shape[1]
    return pl.pallas_call(
        grad_kernel,
        in_specs=[hbm(), whole(), whole()],
        out_specs=hbm(),
        out_shape=pltpu.HBM((lat, pts), bf16),
        scratch_shapes=scratch(
            ((hid, lat), bf16), ((lat, pts), bf16), copies=1 + len(blocks(lat))
        ),
        compiler_params=params(16),
        cost_estimate=pl.CostEstimate(
            flops=2 * hid * lat * pts, bytes_accessed=4 << 20, transcendentals=0
        ),
        name="grad_latent",
    )(*in_hbm(w_in), dpre, scale)


def pairs_kernel(members, cores, fields, target, weight, area_sum, dout, dout_v, sems):
    copies = Copies(sems)
    count = float(members)
    own, pts = fields.shape[1:]
    slopes = [None] * members
    total = None
    for m in range(1, members):
        for k in range(m):
            diff = fields[m] - fields[k]
            square = diff * diff + smooth_sq
            inverse = lax.rsqrt(square)
            slope = diff * inverse
            apart = square * inverse
            total = apart if total is None else total + apart
            slopes[m] = slope if slopes[m] is None else slopes[m] + slope
            slopes[k] = -slope if slopes[k] is None else slopes[k] - slope
    total = 2.0 * total + count * smooth_sq**0.5
    local = total * (-1.0 / (2.0 * count * (count - 1.0)))
    values = []
    for m in range(members):
        miss = fields[m] - target[...]
        square = miss * miss + smooth_sq
        inverse = lax.rsqrt(square)
        local = local + square * inverse * (1.0 / count)
        values.append(
            weight[...]
            * (miss * inverse * (1.0 / count) - slopes[m] * (1.0 / (count * (count - 1.0))))
        )
    loss = jnp.sum(weight[...] * local, keepdims=True)
    lane = lanes((own, pts))
    last = lax.broadcasted_iota(jnp.int32, (own, pts), 0) == own - 1
    ride = jnp.zeros((own, pts), f32)
    for k, value in enumerate((loss, area_sum[0:1, 0:1])):
        high = value.astype(bf16).astype(f32)
        ride = jnp.where(lane == 2 * k, high, jnp.where(lane == 2 * k + 1, value - high, ride))
    for m in range(members):
        value = jnp.where(last, ride, values[m]).astype(bf16)
        for c in range(cores):
            dout_v[m * cores + c] = value
    copies.start(dout_v, dout)
    copies.finish()


def pairs(fields, target, weight, area_sum, cores):
    members, own, pts = fields.shape
    shape = (members * cores, own, pts)
    return pl.pallas_call(
        functools.partial(pairs_kernel, members, cores),
        in_specs=[whole()] * 4,
        out_specs=hbm(),
        out_shape=pltpu.HBM(shape, bf16),
        scratch_shapes=scratch((shape, bf16), copies=1),
        compiler_params=params(8),
        name="pairs",
    )(fields, target, weight, area_sum)


def backward_kernel(
    place, dout, w_out_t, slope_v, slope_far, latent, latent_far, hidden, hidden_far,
    terms_v, dpre_v, slope_far_v, latent_v, hidden_far_v, sems,
):
    copies = Copies(sems)
    me = place[0]
    rows = terms_v.shape[1]
    hid, pts = slope_v.shape
    parts = blocks(hid)

    def fetch(source, target, here):
        return copies.start(source.at[here], target.at[here])

    mine = (slice(None), pl.ds(2 * me, 2))
    near = copies.start(latent.at[mine], latent_v)
    halves = [fetch(slope_far, slope_far_v, parts[0])]
    for here in parts[1:]:
        halves.append(fetch(slope_far, slope_far_v, here))
    late = copies.start(hidden_far.at[mine], hidden_far_v)

    row = lax.broadcasted_iota(jnp.int32, (PAD, pts), 0)
    last = lax.rem(row, OWN) == OWN - 1
    seeds = []
    ride = jnp.zeros((1, pts), f32)
    for which in (me, 1 - me):
        value = dout[:, pl.ds(which, 1)].astype(f32).reshape(PAD, pts)
        ride = ride + jnp.sum(jnp.where(last, value, 0.0), axis=0, keepdims=True)
        seeds.append(jnp.where(last, 0.0, value).astype(bf16))

    copies.wait(near)
    for half in halves:
        copies.wait(half)
    copies.wait(late)
    features = [
        [latent_v[:, k].reshape(-1, pts) for k in range(2)],
        [latent_far[:, pl.ds(2 * me + k, 1)].reshape(-1, pts) for k in range(2)],
    ]
    for here, half in zip(parts, halves):
        first = second = None
        for k, ref in enumerate((slope_v, slope_far_v)):
            dh = dot(w_out_t[here, :], seeds[k])
            dpre = (dh * ref[here, :].astype(f32)).astype(bf16)
            if k == 0:
                dpre_v[here, :] = dpre
            swapped = jnp.concatenate(
                [
                    dpre[base + off : base + off + HALF]
                    for base in range(0, BLOCK, PAD)
                    for off in (HALF, 0)
                ],
                0,
            )
            a = dot_nt(features[k][0], dpre)
            b = dot_nt(features[k][1], swapped)
            first = a if first is None else first + a
            second = b if second is None else second + b
        low = lax.rem(lanes(first.shape), PAD) < HALF
        for xh, value in enumerate(
            (jnp.where(low, first, second), jnp.where(low, second, first))
        ):
            for xl in range(2):
                terms_v[2 * xh + xl, :, here] = value[xl * rows : (xl + 1) * rows].astype(bf16)

    out = dot_nt(hidden[:, pl.ds(2 * me, 2)].reshape(-1, pts), seeds[0])
    out += dot_nt(hidden_far_v[...].reshape(-1, pts), seeds[1])
    out = out.reshape(-1, 2, 16, PAD)
    left = out[:, 0].reshape(-1, PAD)
    right = out[:, 1].reshape(-1, PAD)
    lane = lanes((1, PAD))
    parts = jnp.zeros((1, PAD), f32)
    for k in range(2):
        mine = lax.div(lanes((1, pts)), 2) == k
        value = jnp.sum(jnp.where(mine, ride, 0.0), axis=1, keepdims=True)
        high = value.astype(bf16).astype(f32)
        parts = jnp.where(lane == spare(2 * k), high, parts)
        parts = jnp.where(lane == spare(2 * k + 1), value - high, parts)
    row = lax.rem(lax.broadcasted_iota(jnp.int32, left.shape, 0), 16)
    unused = lax.rem(lanes(left.shape), OWN) == OWN - 1
    left = jnp.where(unused, jnp.where(row == 0, parts, 0.0), left)
    for xh in range(2):
        for xl in range(2):
            piece = slice(xl * rows, (xl + 1) * rows)
            terms_v[2 * xh + xl, :, hid : hid + PAD] = left[piece].astype(bf16)
            terms_v[2 * xh + xl, :, hid + PAD :] = right[piece].astype(bf16)


def backward(place, dout, w_out_t, slope, slope_far, latent, latent_far, hidden, hidden_far):
    hid, pts = slope.shape
    plane = latent.shape[0]
    shape = (4, plane * 16 // 2, hid + 2 * PAD)
    half = ((plane, 2, 16, pts), bf16)
    return pl.pallas_call(
        backward_kernel,
        in_specs=[smem()] + [whole()] * 3 + [hbm()] * 2 + [whole()] * 2 + [hbm()],
        out_specs=[whole()] * 2,
        out_shape=[
            jax.ShapeDtypeStruct(shape, bf16),
            jax.ShapeDtypeStruct((hid, pts), bf16),
        ],
        scratch_shapes=scratch(
            ((hid, pts), bf16), half, half,
            copies=len(blocks(hid)) + 2,
        ),
        compiler_params=params(24),
        name="backward",
    )(
        place, dout, w_out_t, slope, *in_hbm(slope_far, latent), latent_far, hidden,
        *in_hbm(hidden_far),
    )


def split_again(tile):
    lane = lanes(tile.shape)
    value = tile + pltpu.roll(tile, PAD - OWN, 1)
    high = value.astype(bf16).astype(f32)
    low = pltpu.roll(value - high, OWN, 1)
    even = (lane == spare(0)) | (lane == spare(2))
    odd = (lane == spare(1)) | (lane == spare(3))
    return jnp.where(even, high, jnp.where(odd, low, tile))


def add_x_kernel(hid, got, out):
    value = got[0].astype(f32)
    for k in range(1, got.shape[0]):
        value = value + got[k].astype(f32)
    out[:, 0:hid] = value[:, 0:hid].astype(bf16)
    out[:, hid : hid + PAD] = split_again(value[:, hid : hid + PAD]).astype(bf16)
    out[:, hid + PAD :] = value[:, hid + PAD :].astype(bf16)


def add_x(got, hid):
    return pl.pallas_call(
        functools.partial(add_x_kernel, hid),
        in_specs=[whole()],
        out_specs=whole(),
        out_shape=jax.ShapeDtypeStruct(got.shape[1:], bf16),
        compiler_params=params(8),
        name="add_x",
    )(got)


def pick(head, k):
    lane = lanes(head.shape)
    mine = (lane == spare(2 * k)) | (lane == spare(2 * k + 1))
    return jnp.sum(jnp.where(mine, head, 0.0), axis=1, keepdims=True)


def add_z_kernel(hid, copied, points_all, got, out, scale, out_v, sems):
    copies = Copies(sems)
    value = got[0].astype(f32)
    for k in range(1, got.shape[0]):
        value = value + got[k].astype(f32)
    left = value[:, hid : hid + PAD]
    keep = split_again(left).astype(bf16)
    right = value[:, hid + PAD :].astype(bf16)
    for y in range(out.shape[0]):
        out_v[y, :, 0:PAD] = value[:, y * PAD : (y + 1) * PAD].astype(bf16)
        out_v[y, :, PAD : 2 * PAD] = keep
        out_v[y, :, 2 * PAD :] = right
    copies.start(out_v, out)
    weight_total = pick(left[0:1, :], 1) * (1.0 / copied)
    scale[...] = jnp.broadcast_to(points_all / (weight_total * VARS), scale.shape)
    copies.finish()


def add_z(got, hid, copied, points_all):
    shape = (hid // PAD, got.shape[1], 3 * PAD)
    return pl.pallas_call(
        functools.partial(add_z_kernel, hid, copied, points_all),
        in_specs=[whole()],
        out_specs=[hbm(), whole()],
        out_shape=[pltpu.HBM(shape, bf16), jax.ShapeDtypeStruct((8, PAD), f32)],
        scratch_shapes=scratch((shape, bf16), copies=1),
        compiler_params=params(4),
        name="add_z",
    )(got)


def finish_kernel(copied, points_all, count, turn, got, loss, grad_in, grad_out):
    value = got[0].astype(f32)
    for k in range(1, got.shape[0]):
        value = value + got[k].astype(f32)
    left = value[:, PAD : 2 * PAD]
    head = left[0:1, :]
    weight_total = pick(head, 1) * (1.0 / (copied * count))
    scale = 1.0 / (weight_total * VARS)
    loss[...] = pick(head, 0) * (1.0 / copied) * scale
    ratio = scale * (points_all / (points_all * count) ** 0.5)
    tile = value[:, 0:PAD] * ratio
    other = pltpu.roll(tile, HALF, 1)
    even = turn[0] == 0
    grad_in[0:16, :] = jnp.where(even, tile, other)[:, 0:HALF]
    grad_in[16:32, :] = jnp.where(even, other, tile)[:, 0:HALF]
    both = jnp.concatenate([left, value[:, 2 * PAD :]], 0) * ratio
    grad_out[...] = lax.dot_general(
        both, row_table().astype(f32), (((1,), (0,)), ((), ())),
        precision=lax.Precision.HIGHEST, preferred_element_type=f32,
    )


def finish(turn, got, copied, points_all, count):
    return pl.pallas_call(
        functools.partial(finish_kernel, copied, points_all, count),
        in_specs=[smem(), whole()],
        out_specs=[whole()] * 3,
        out_shape=[
            jax.ShapeDtypeStruct((1, 1), f32),
            jax.ShapeDtypeStruct((32, HALF), f32),
            jax.ShapeDtypeStruct((32, VARS), f32),
        ],
        compiler_params=params(4),
        name="finish",
    )(turn, got)


def per_device(latent, w_in, w_out, target, area, var_weight):
    n_ens = lax.axis_size(ENS)
    n_plane = lax.axis_size(PLANE)
    n_core = lax.axis_size("c")
    n_z = lax.axis_size("z")
    pts = area.shape[0]
    hid, _ = w_in.shape
    own = PAD // n_ens
    assert own == OWN
    me = lax.axis_index(ENS)
    core = lax.axis_index("c")
    swap = [(0, 1), (1, 0)]
    features = latent[0]

    count = float(n_ens)
    points_all = float(n_plane * n_core * pts)
    hidden, slope, decoded, w_out_t, target_own, weight_own, area_sum = forward(
        me.astype(jnp.int32)[None], w_in, features, w_out, target, area[None, :],
        var_weight[None, :],
    )

    fields = exchange(decoded.reshape(n_ens, own, pts), ENS)
    dout = pairs(fields, target_own, weight_own, area_sum, n_core)

    dout_got = exchange(dout, ENS + ("c",))
    late, _ = lax.optimization_barrier((features, dout))
    far = lax.ppermute(late, "c", swap)
    hidden_far, slope_far = far_forward(w_in, far)

    groups = lambda value: value.reshape(n_plane, 2 * n_core, 16, pts)
    terms, dpre = backward(
        core.astype(jnp.int32)[None],
        dout_got.reshape(n_ens, n_core, own, pts),
        w_out_t, slope, slope_far,
        groups(features), groups(far), groups(hidden), groups(hidden_far),
    )

    got = exchange(terms, CHIP_X)
    got = exchange(add_x(got, hid).reshape(n_z, 16, hid + 2 * PAD), "z")
    got, scale = add_z(got, hid, count * lax.axis_size("xh"), points_all)
    got = exchange(got, "y")
    grad_lat = grad_latent(w_in, dpre, scale)
    loss, part_in, part_out = finish(
        lax.axis_index("xh").astype(jnp.int32)[None], got, count, points_all, count
    )
    return loss[0, 0], grad_lat[None], part_in.T, part_out.T


def solution(mesh):
    ens, grid_all = mesh.devices.shape
    split = (ens // 2, 2, 2, grid_all // 4, 2)
    fine = Mesh(mesh.devices.reshape(split), ENS + PLANE + ("c",))
    grid = PLANE + ("c",)
    in_specs = (P(ENS, None, grid), P(), P(), P(None, grid), P(grid), P())
    out_specs = (P(), P(ENS, None, grid), P(ENS, grid), P(None, grid))
    return jax.shard_map(
        per_device, mesh=fine, in_specs=in_specs, out_specs=out_specs, check_vma=False
    )
```

```python
import functools

import jax
import jax.numpy as jnp
from jax import lax
from jax.experimental import pallas as pl
from jax.experimental.pallas import tpu as pltpu
from jax.sharding import Mesh, PartitionSpec as P

VARS = 99
PAD = 128
HALF = PAD // 2
OWN = 8
ENS = ("y", "xh")
PLANE = ("xl", "z")
CHIP_X = ("xh", "xl")
BLOCK = 1024

smooth_sq = 0.01
gelu_c = 0.7978845608
gelu_k = 0.044715
f32 = jnp.float32
bf16 = jnp.bfloat16
NT = (((1,), (1,)), ((), ()))


def gelu(value):
    square = value * value
    share = 0.5 + 0.5 * jnp.tanh(value * (gelu_c + gelu_c * gelu_k * square))
    bend = value * (2.0 * gelu_c + 6.0 * gelu_c * gelu_k * square)
    return value * share, share + share * ((1.0 - share) * bend)


def exchange(pieces, axes):
    return lax.all_to_all(pieces, axes, split_axis=0, concat_axis=0, tiled=True)


def dot(a, b):
    return jnp.dot(a, b, preferred_element_type=f32)


def dot_nt(a, b):
    return lax.dot_general(a, b, NT, preferred_element_type=f32)


def whole():
    return pl.BlockSpec(memory_space=pltpu.VMEM)


def smem():
    return pl.BlockSpec(memory_space=pltpu.SMEM)


def hbm():
    return pl.BlockSpec(memory_space=pltpu.HBM)


def in_hbm(*arrays):
    return [pltpu.with_memory_space_constraint(array, pltpu.HBM) for array in arrays]


def params(mib):
    return pltpu.CompilerParams(vmem_limit_bytes=mib << 20)


class Copies:
    def __init__(self, sems):
        self.sems = sems
        self.used = 0
        self.open = []

    def start(self, source, target):
        copy = pltpu.make_async_copy(source, target, self.sems.at[self.used])
        self.used += 1
        copy.start()
        self.open.append(copy)
        return copy

    def wait(self, copy):
        copy.wait()
        self.open = [other for other in self.open if other is not copy]

    def finish(self):
        for copy in self.open:
            self.wait(copy)


def scratch(*shapes, copies):
    return [pltpu.VMEM(shape, kind) for shape, kind in shapes] + [
        pltpu.SemaphoreType.DMA((copies,))
    ]


def blocks(size):
    step = min(size, BLOCK)
    return [slice(at, at + step) for at in range(0, size, step)]


def spare(k):
    return OWN * (k + 1) - 1


def row_table():
    row = lax.broadcasted_iota(jnp.int32, (PAD, VARS), 0)
    held = lax.rem(row, OWN) < OWN - 1
    variable = lax.div(row, OWN) * (OWN - 1) + lax.rem(row, OWN)
    return held & (variable == lanes((PAD, VARS)))


def lanes(shape):
    return lax.broadcasted_iota(jnp.int32, shape, len(shape) - 1)


class Stream:
    def __init__(self, copies, source, target):
        self.copies = copies
        self.started = []
        for here in blocks(source.shape[0]):
            middle = (here.start + here.stop) // 2
            self.started.append(
                [
                    copies.start(source.at[part], target.at[part])
                    for part in (slice(here.start, middle), slice(middle, here.stop))
                ]
            )

    def wait(self, k):
        for copy in self.started[k]:
            self.copies.wait(copy)


def products(weights, w_in_v, latent):
    parts = blocks(w_in_v.shape[0])
    ahead = None
    for k, here in enumerate(parts):
        if ahead is None:
            weights.wait(k)
            ahead = dot(w_in_v[here, :], latent[...])
        now = ahead
        if k + 1 < len(parts):
            weights.wait(k + 1)
            ahead = dot(w_in_v[parts[k + 1], :], latent[...])
        yield here, now


def forward_kernel(
    w_in, latent, w_out, hidden, slope, decoded, latent_v, w_in_v, w_out_v, decoded_v, sems
):
    copies = Copies(sems)
    first = copies.start(latent, latent_v)
    rows = copies.start(w_out, w_out_v)
    weights = Stream(copies, w_in, w_in_v)
    copies.wait(first)
    copies.wait(rows)
    w_out_rows = dot(row_table().astype(bf16), w_out_v[...]).astype(bf16)
    total = None
    for here, product in products(weights, w_in_v, latent_v):
        value, bend = gelu(product)
        value = value.astype(bf16)
        hidden[here, :] = value
        slope[here, :] = bend.astype(bf16)
        part = dot(w_out_rows[:, here], value)
        total = part if total is None else total + part
    decoded_v[...] = total
    copies.start(decoded_v, decoded)
    copies.finish()


def forward(w_in, latent, w_out):
    hid, lat = w_in.shape
    pts = latent.shape[1]
    return pl.pallas_call(
        forward_kernel,
        in_specs=[hbm()] * 3,
        out_specs=[whole(), whole(), hbm(), whole()],
        out_shape=[
            jax.ShapeDtypeStruct((hid, pts), bf16),
            jax.ShapeDtypeStruct((hid, pts), bf16),
            pltpu.HBM((PAD, pts), f32),
            jax.ShapeDtypeStruct((lat, pts), bf16),
        ],
        scratch_shapes=scratch(
            ((hid, lat), bf16), ((VARS, hid), bf16), ((PAD, pts), f32),
            copies=4 * len(blocks(hid)) + 3,
        ),
        compiler_params=params(16),
        name="forward",
    )(*in_hbm(w_in, latent, w_out))


def far_kernel(w_in, latent, hidden, slope, w_in_v, hidden_v, slope_v, sems):
    copies = Copies(sems)
    weights = Stream(copies, w_in, w_in_v)
    for here, product in products(weights, w_in_v, latent):
        value, bend = gelu(product)
        hidden_v[here, :] = value.astype(bf16)
        copies.start(hidden_v.at[here], hidden.at[here])
        slope_v[here, :] = bend.astype(bf16)
        copies.start(slope_v.at[here], slope.at[here])
    copies.finish()


def far_forward(w_in, latent):
    hid, lat = w_in.shape
    pts = latent.shape[1]
    return pl.pallas_call(
        far_kernel,
        in_specs=[hbm(), whole()],
        out_specs=[hbm()] * 2,
        out_shape=[pltpu.HBM((hid, pts), bf16), pltpu.HBM((hid, pts), bf16)],
        scratch_shapes=scratch(
            ((hid, lat), bf16), ((hid, pts), bf16), ((hid, pts), bf16),
            copies=6 * len(blocks(hid)),
        ),
        compiler_params=params(16),
        cost_estimate=pl.CostEstimate(
            flops=2 * hid * lat * pts, bytes_accessed=4 << 20, transcendentals=hid * pts
        ),
        name="far_forward",
    )(*in_hbm(w_in), latent)


def prepare_kernel(
    owner, w_out_h, target_h, area_h, var_weight_h, w_out_t, target, weight, area_sum,
    w_out_v, target_v, area_v, var_weight_v, sems,
):
    copies = Copies(sems)
    inputs = [
        copies.start(w_out_h, w_out_v),
        copies.start(target_h, target_v),
        copies.start(area_h, area_v),
        copies.start(var_weight_h, var_weight_v),
    ]
    copies.wait(inputs[0])
    w_out_t[...] = lax.dot_general(
        w_out_v[...], row_table().astype(bf16), (((0,), (1,)), ((), ())),
        preferred_element_type=f32,
    ).astype(bf16)
    for copy in inputs[1:]:
        copies.wait(copy)
    row = lax.broadcasted_iota(jnp.int32, (OWN, VARS), 0)
    held = (row < OWN - 1) & (lanes((OWN, VARS)) == owner[0] * (OWN - 1) + row)
    scale = jnp.sum(jnp.where(held, var_weight_v[...], 0.0), axis=1, keepdims=True)
    weight[...] = area_v[...] * scale
    target[...] = lax.dot_general(
        held.astype(f32), target_v[...], (((1,), (0,)), ((), ())),
        precision=lax.Precision.HIGHEST, preferred_element_type=f32,
    )
    area_sum[...] = jnp.broadcast_to(jnp.sum(area_v[...], keepdims=True), area_sum.shape)
    copies.finish()


def prepare(owner, w_out, target, area, var_weight):
    hid = w_out.shape[1]
    pts = target.shape[1]
    return pl.pallas_call(
        prepare_kernel,
        in_specs=[smem()] + [hbm()] * 4,
        out_specs=[whole()] * 4,
        out_shape=[
            jax.ShapeDtypeStruct((hid, PAD), bf16),
            jax.ShapeDtypeStruct((OWN, pts), f32),
            jax.ShapeDtypeStruct((OWN, pts), f32),
            jax.ShapeDtypeStruct((8, PAD), f32),
        ],
        scratch_shapes=scratch(
            (w_out.shape, bf16), (target.shape, f32), (area.shape, f32), (var_weight.shape, f32),
            copies=4,
        ),
        compiler_params=params(16),
        cost_estimate=pl.CostEstimate(flops=1 << 28, bytes_accessed=1 << 20, transcendentals=0),
        name="prepare",
    )(owner, *in_hbm(w_out, target, area, var_weight))


def grad_kernel(w_in, dpre, scale, grad, w_in_v, grad_v, sems):
    copies = Copies(sems)
    copies.start(w_in, w_in_v)
    copies.finish()
    factor = scale[0:1, 0:1]
    for here in blocks(w_in.shape[1]):
        value = lax.dot_general(
            w_in_v[:, here], dpre[...], (((0,), (0,)), ((), ())), preferred_element_type=f32
        )
        grad_v[here, :] = (value * factor).astype(bf16)
        copies.start(grad_v.at[here], grad.at[here])
    copies.finish()


def grad_latent(w_in, dpre, scale):
    hid, lat = w_in.shape
    pts = dpre.shape[1]
    return pl.pallas_call(
        grad_kernel,
        in_specs=[hbm(), whole(), whole()],
        out_specs=hbm(),
        out_shape=pltpu.HBM((lat, pts), bf16),
        scratch_shapes=scratch(
            ((hid, lat), bf16), ((lat, pts), bf16), copies=1 + len(blocks(lat))
        ),
        compiler_params=params(16),
        cost_estimate=pl.CostEstimate(
            flops=2 * hid * lat * pts, bytes_accessed=4 << 20, transcendentals=0
        ),
        name="grad_latent",
    )(*in_hbm(w_in), dpre, scale)


def pairs_kernel(members, cores, fields, target, weight, area_sum, dout, dout_v, sems):
    copies = Copies(sems)
    count = float(members)
    own, pts = fields.shape[1:]
    slopes = [None] * members
    total = None
    for m in range(1, members):
        for k in range(m):
            diff = fields[m] - fields[k]
            square = diff * diff + smooth_sq
            inverse = lax.rsqrt(square)
            slope = diff * inverse
            apart = square * inverse
            total = apart if total is None else total + apart
            slopes[m] = slope if slopes[m] is None else slopes[m] + slope
            slopes[k] = -slope if slopes[k] is None else slopes[k] - slope
    total = 2.0 * total + count * smooth_sq**0.5
    local = total * (-1.0 / (2.0 * count * (count - 1.0)))
    values = []
    for m in range(members):
        miss = fields[m] - target[...]
        square = miss * miss + smooth_sq
        inverse = lax.rsqrt(square)
        local = local + square * inverse * (1.0 / count)
        values.append(
            weight[...]
            * (miss * inverse * (1.0 / count) - slopes[m] * (1.0 / (count * (count - 1.0))))
        )
    loss = jnp.sum(weight[...] * local, keepdims=True)
    lane = lanes((own, pts))
    last = lax.broadcasted_iota(jnp.int32, (own, pts), 0) == own - 1
    ride = jnp.zeros((own, pts), f32)
    for k, value in enumerate((loss, area_sum[0:1, 0:1])):
        high = value.astype(bf16).astype(f32)
        ride = jnp.where(lane == 2 * k, high, jnp.where(lane == 2 * k + 1, value - high, ride))
    for m in range(members):
        value = jnp.where(last, ride, values[m]).astype(bf16)
        for c in range(cores):
            dout_v[m * cores + c] = value
    copies.start(dout_v, dout)
    copies.finish()


def pairs(fields, target, weight, area_sum, cores):
    members, own, pts = fields.shape
    shape = (members * cores, own, pts)
    return pl.pallas_call(
        functools.partial(pairs_kernel, members, cores),
        in_specs=[whole()] * 4,
        out_specs=hbm(),
        out_shape=pltpu.HBM(shape, bf16),
        scratch_shapes=scratch((shape, bf16), copies=1),
        compiler_params=params(8),
        name="pairs",
    )(fields, target, weight, area_sum)


def backward_kernel(
    place, dout, w_out_t, slope_v, slope_far, latent, latent_far, hidden, hidden_far,
    terms_v, dpre_v, slope_far_v, latent_v, hidden_far_v, sems,
):
    copies = Copies(sems)
    me = place[0]
    rows = terms_v.shape[1]
    hid, pts = slope_v.shape
    parts = blocks(hid)

    def fetch(source, target, here):
        return copies.start(source.at[here], target.at[here])

    mine = (slice(None), pl.ds(2 * me, 2))
    near = copies.start(latent.at[mine], latent_v)
    halves = [fetch(slope_far, slope_far_v, parts[0])]
    for here in parts[1:]:
        halves.append(fetch(slope_far, slope_far_v, here))
    late = copies.start(hidden_far.at[mine], hidden_far_v)

    row = lax.broadcasted_iota(jnp.int32, (PAD, pts), 0)
    last = lax.rem(row, OWN) == OWN - 1
    seeds = []
    ride = jnp.zeros((1, pts), f32)
    for which in (me, 1 - me):
        value = dout[:, pl.ds(which, 1)].astype(f32).reshape(PAD, pts)
        ride = ride + jnp.sum(jnp.where(last, value, 0.0), axis=0, keepdims=True)
        seeds.append(jnp.where(last, 0.0, value).astype(bf16))

    copies.wait(near)
    for half in halves:
        copies.wait(half)
    copies.wait(late)
    features = [
        [latent_v[:, k].reshape(-1, pts) for k in range(2)],
        [latent_far[:, pl.ds(2 * me + k, 1)].reshape(-1, pts) for k in range(2)],
    ]
    for here, half in zip(parts, halves):
        first = second = None
        for k, ref in enumerate((slope_v, slope_far_v)):
            dh = dot(w_out_t[here, :], seeds[k])
            dpre = (dh * ref[here, :].astype(f32)).astype(bf16)
            if k == 0:
                dpre_v[here, :] = dpre
            swapped = jnp.concatenate(
                [
                    dpre[base + off : base + off + HALF]
                    for base in range(0, BLOCK, PAD)
                    for off in (HALF, 0)
                ],
                0,
            )
            a = dot_nt(features[k][0], dpre)
            b = dot_nt(features[k][1], swapped)
            first = a if first is None else first + a
            second = b if second is None else second + b
        low = lax.rem(lanes(first.shape), PAD) < HALF
        for xh, value in enumerate(
            (jnp.where(low, first, second), jnp.where(low, second, first))
        ):
            for xl in range(2):
                terms_v[2 * xh + xl, :, here] = value[xl * rows : (xl + 1) * rows].astype(bf16)

    out = dot_nt(hidden[:, pl.ds(2 * me, 2)].reshape(-1, pts), seeds[0])
    out += dot_nt(hidden_far_v[...].reshape(-1, pts), seeds[1])
    out = out.reshape(-1, 2, 16, PAD)
    left = out[:, 0].reshape(-1, PAD)
    right = out[:, 1].reshape(-1, PAD)
    lane = lanes((1, PAD))
    parts = jnp.zeros((1, PAD), f32)
    for k in range(2):
        mine = lax.div(lanes((1, pts)), 2) == k
        value = jnp.sum(jnp.where(mine, ride, 0.0), axis=1, keepdims=True)
        high = value.astype(bf16).astype(f32)
        parts = jnp.where(lane == spare(2 * k), high, parts)
        parts = jnp.where(lane == spare(2 * k + 1), value - high, parts)
    row = lax.rem(lax.broadcasted_iota(jnp.int32, left.shape, 0), 16)
    unused = lax.rem(lanes(left.shape), OWN) == OWN - 1
    left = jnp.where(unused, jnp.where(row == 0, parts, 0.0), left)
    for xh in range(2):
        for xl in range(2):
            piece = slice(xl * rows, (xl + 1) * rows)
            terms_v[2 * xh + xl, :, hid : hid + PAD] = left[piece].astype(bf16)
            terms_v[2 * xh + xl, :, hid + PAD :] = right[piece].astype(bf16)


def backward(place, dout, w_out_t, slope, slope_far, latent, latent_far, hidden, hidden_far):
    hid, pts = slope.shape
    plane = latent.shape[0]
    shape = (4, plane * 16 // 2, hid + 2 * PAD)
    half = ((plane, 2, 16, pts), bf16)
    return pl.pallas_call(
        backward_kernel,
        in_specs=[smem()] + [whole()] * 3 + [hbm()] * 2 + [whole()] * 2 + [hbm()],
        out_specs=[whole()] * 2,
        out_shape=[
            jax.ShapeDtypeStruct(shape, bf16),
            jax.ShapeDtypeStruct((hid, pts), bf16),
        ],
        scratch_shapes=scratch(
            ((hid, pts), bf16), half, half,
            copies=len(blocks(hid)) + 2,
        ),
        compiler_params=params(24),
        name="backward",
    )(
        place, dout, w_out_t, slope, *in_hbm(slope_far, latent), latent_far, hidden,
        *in_hbm(hidden_far),
    )


def split_again(tile):
    lane = lanes(tile.shape)
    value = tile + pltpu.roll(tile, PAD - OWN, 1)
    high = value.astype(bf16).astype(f32)
    low = pltpu.roll(value - high, OWN, 1)
    even = (lane == spare(0)) | (lane == spare(2))
    odd = (lane == spare(1)) | (lane == spare(3))
    return jnp.where(even, high, jnp.where(odd, low, tile))


def add_x_kernel(hid, got, out):
    value = got[0].astype(f32)
    for k in range(1, got.shape[0]):
        value = value + got[k].astype(f32)
    out[:, 0:hid] = value[:, 0:hid].astype(bf16)
    out[:, hid : hid + PAD] = split_again(value[:, hid : hid + PAD]).astype(bf16)
    out[:, hid + PAD :] = value[:, hid + PAD :].astype(bf16)


def add_x(got, hid):
    return pl.pallas_call(
        functools.partial(add_x_kernel, hid),
        in_specs=[whole()],
        out_specs=whole(),
        out_shape=jax.ShapeDtypeStruct(got.shape[1:], bf16),
        compiler_params=params(8),
        name="add_x",
    )(got)


def pick(head, k):
    lane = lanes(head.shape)
    mine = (lane == spare(2 * k)) | (lane == spare(2 * k + 1))
    return jnp.sum(jnp.where(mine, head, 0.0), axis=1, keepdims=True)


def add_z_kernel(hid, copied, points_all, got, out, scale, out_v, sems):
    copies = Copies(sems)
    value = got[0].astype(f32)
    for k in range(1, got.shape[0]):
        value = value + got[k].astype(f32)
    left = value[:, hid : hid + PAD]
    keep = split_again(left).astype(bf16)
    right = value[:, hid + PAD :].astype(bf16)
    for y in range(out.shape[0]):
        out_v[y, :, 0:PAD] = value[:, y * PAD : (y + 1) * PAD].astype(bf16)
        out_v[y, :, PAD : 2 * PAD] = keep
        out_v[y, :, 2 * PAD :] = right
    copies.start(out_v, out)
    weight_total = pick(left[0:1, :], 1) * (1.0 / copied)
    scale[...] = jnp.broadcast_to(points_all / (weight_total * VARS), scale.shape)
    copies.finish()


def add_z(got, hid, copied, points_all):
    shape = (hid // PAD, got.shape[1], 3 * PAD)
    return pl.pallas_call(
        functools.partial(add_z_kernel, hid, copied, points_all),
        in_specs=[whole()],
        out_specs=[hbm(), whole()],
        out_shape=[pltpu.HBM(shape, bf16), jax.ShapeDtypeStruct((8, PAD), f32)],
        scratch_shapes=scratch((shape, bf16), copies=1),
        compiler_params=params(4),
        name="add_z",
    )(got)


def finish_kernel(copied, points_all, count, turn, got, loss, grad_in, grad_out):
    value = got[0].astype(f32)
    for k in range(1, got.shape[0]):
        value = value + got[k].astype(f32)
    left = value[:, PAD : 2 * PAD]
    head = left[0:1, :]
    weight_total = pick(head, 1) * (1.0 / (copied * count))
    scale = 1.0 / (weight_total * VARS)
    loss[...] = pick(head, 0) * (1.0 / copied) * scale
    ratio = scale * (points_all / (points_all * count) ** 0.5)
    tile = value[:, 0:PAD] * ratio
    other = pltpu.roll(tile, HALF, 1)
    even = turn[0] == 0
    grad_in[0:16, :] = jnp.where(even, tile, other)[:, 0:HALF]
    grad_in[16:32, :] = jnp.where(even, other, tile)[:, 0:HALF]
    both = jnp.concatenate([left, value[:, 2 * PAD :]], 0) * ratio
    grad_out[...] = lax.dot_general(
        both, row_table().astype(f32), (((1,), (0,)), ((), ())),
        precision=lax.Precision.HIGHEST, preferred_element_type=f32,
    )


def finish(turn, got, copied, points_all, count):
    return pl.pallas_call(
        functools.partial(finish_kernel, copied, points_all, count),
        in_specs=[smem(), whole()],
        out_specs=[whole()] * 3,
        out_shape=[
            jax.ShapeDtypeStruct((1, 1), f32),
            jax.ShapeDtypeStruct((32, HALF), f32),
            jax.ShapeDtypeStruct((32, VARS), f32),
        ],
        compiler_params=params(4),
        name="finish",
    )(turn, got)


def per_device(latent, w_in, w_out, target, area, var_weight):
    n_ens = lax.axis_size(ENS)
    n_plane = lax.axis_size(PLANE)
    n_core = lax.axis_size("c")
    n_z = lax.axis_size("z")
    pts = area.shape[0]
    hid, _ = w_in.shape
    own = PAD // n_ens
    assert own == OWN
    me = lax.axis_index(ENS)
    core = lax.axis_index("c")
    swap = [(0, 1), (1, 0)]
    features = latent[0]

    count = float(n_ens)
    points_all = float(n_plane * n_core * pts)
    hidden, slope, decoded, latent_near = forward(w_in, features, w_out)

    fields = exchange(decoded.reshape(n_ens, own, pts), ENS)
    late = lax.optimization_barrier((latent_near, w_out, decoded))
    far = lax.ppermute(late[0], "c", swap)
    w_out_t, target_own, weight_own, area_sum = prepare(
        me.astype(jnp.int32)[None], late[1], target, area[None, :], var_weight[None, :]
    )
    dout = pairs(fields, target_own, weight_own, area_sum, n_core)

    dout_got = exchange(dout, ENS + ("c",))
    far, _ = lax.optimization_barrier((far, dout))
    hidden_far, slope_far = far_forward(w_in, far)

    groups = lambda value: value.reshape(n_plane, 2 * n_core, 16, pts)
    terms, dpre = backward(
        core.astype(jnp.int32)[None],
        dout_got.reshape(n_ens, n_core, own, pts),
        w_out_t, slope, slope_far,
        groups(features), groups(far), groups(hidden), groups(hidden_far),
    )

    got = exchange(terms, CHIP_X)
    got = exchange(add_x(got, hid).reshape(n_z, 16, hid + 2 * PAD), "z")
    got, scale = add_z(got, hid, count * lax.axis_size("xh"), points_all)
    got = exchange(got, "y")
    grad_lat = grad_latent(w_in, dpre, scale)
    loss, part_in, part_out = finish(
        lax.axis_index("xh").astype(jnp.int32)[None], got, count, points_all, count
    )
    return loss[0, 0], grad_lat[None], part_in.T, part_out.T


def solution(mesh):
    ens, grid_all = mesh.devices.shape
    split = (ens // 2, 2, 2, grid_all // 4, 2)
    fine = Mesh(mesh.devices.reshape(split), ENS + PLANE + ("c",))
    grid = PLANE + ("c",)
    in_specs = (P(ENS, None, grid), P(), P(), P(None, grid), P(grid), P())
    out_specs = (P(), P(ENS, None, grid), P(ENS, grid), P(None, grid))
    return jax.shard_map(
        per_device, mesh=fine, in_specs=in_specs, out_specs=out_specs, check_vma=False
    )
```
